32 devices in a mesh: row: 4 (over z), col: 8 (over y, x, core).
Axes of the slice: x: 2, y: 2, z: 4, core: 2. Of those that a mesh axis runs over, the one named last changes fastest.
Arguments:
- tokens: bfloat16 [16384, 768], P(('row', 'col')), may hold values from -6 to 6
- lengths: int32 [32, 8], P(('row', 'col')), may hold values from 1 to 128, 512 in all within a row
- pair_index: int32 [256], replicated, may hold values from 0 to 255, as said below
- tile_slot: int32 [25], replicated, may hold values from 0 to 31, as said below
- master_store: float32 [32, 768, 768], P('col', 'row')
- first_moment_store: float32 [32, 768, 768], P('col', 'row'), may hold values from -0.0014648438 to 0.0014648438
- second_moment_store: float32 [32, 768, 768], P('col', 'row'), may hold values from 8.59375e-10 to 3.515625e-09
- vectors: float32 [25, 768], replicated
- vector_first: float32 [25, 768], replicated, may hold values from -0.0048828125 to 0.0048828125
- vector_second: float32 [25, 768], replicated, may hold values from 7.8125e-09 to 3.125e-08
Outputs:
- d_tokens: float32 [16384, 768], P(('row', 'col'))
- mean_loss: float32 [], replicated
- store_grad: float32 [32, 768, 768], P('col', 'row')
- new_store: float32 [32, 768, 768], P('col', 'row')
- new_store_first: float32 [32, 768, 768], P('col', 'row')
- new_store_second: float32 [32, 768, 768], P('col', 'row')
- vector_grad: float32 [25, 768], replicated
- new_vectors: float32 [25, 768], replicated
- new_vector_first: float32 [25, 768], replicated
- new_vector_second: float32 [25, 768], replicated
- out_bias_grad: float32 [768], replicated
The draws below stay inside these ranges and needn't reach their ends.
Inputs may be any that keep to these rules, and one draw needn't show every extreme that they name: Each row's 8 lengths sum to 512 and the largest is 128. pair_index[i] != i. `tile_slot`: the 25 values are distinct; slot s lies on index s // 4 of col.
All inputs are finite; a program needn't handle non-finite values.
Results may differ from the reference program's by a relative error of at most 0.03.
Values may be sent and summed in bfloat16 or wider, within the bound.
A program may use at most 320 MiB of HBM per device.

```python
import math
import jax
import jax.numpy as jnp
import numpy as np
from jax import lax

MODEL_DIMENSION = 768
FF = 3072
HEADS = 12
HEAD_DIM = 64
LAYERS = 2
SEQ = 512
SENTS = 8
MOST = 128
STEP = 10
NROWS = 32
TOKENS = 16384
SENTENCE_COUNT = 256
SQUARE_TILES = 25
NVEC = 25
WEIGHT_SLOTS = 32


def slot_table(key):
    return jax.random.permutation(key, WEIGHT_SLOTS)[:SQUARE_TILES].astype(jnp.int32)


def draw_tile_slot(key, part):
    return slot_table(jax.random.fold_in(key, 11))


def draw_master_store(key, part):
    table = slot_table(jax.random.fold_in(key, 11))
    slot_indices = jnp.arange(WEIGHT_SLOTS, dtype=jnp.int32)
    matches = table[None, :] == slot_indices[:, None]
    tile_scale = np.full((SQUARE_TILES,), MODEL_DIMENSION ** (-0.5), np.float32)
    for number in range(SQUARE_TILES - 1):
        tile_kind = number % 12
        if tile_kind == 3:
            tile_scale[number] = 6.0 * MODEL_DIMENSION ** (-0.5)
        elif tile_kind >= 8:
            tile_scale[number] = 1.5 * FF ** (-0.5)
    scales = jnp.sum(jnp.where(matches, jnp.asarray(tile_scale)[None, :], 0.0), axis=1)
    scales = scales + jnp.where(jnp.any(matches, axis=1), 0.0, MODEL_DIMENSION ** (-0.5))
    random_base_sample = jax.random.normal(jax.random.fold_in(key, 12), (WEIGHT_SLOTS, MODEL_DIMENSION, MODEL_DIMENSION), jnp.float32)
    return random_base_sample * scales[:, None, None]


def draw_pair_index(key, part):
    offsets = jax.random.randint(jax.random.fold_in(key, 21), (SENTENCE_COUNT,), 1, SENTENCE_COUNT)
    return ((jnp.arange(SENTENCE_COUNT, dtype=jnp.int32) + offsets) % SENTENCE_COUNT).astype(jnp.int32)


def draw_vectors(key, part):
    row_kind = np.zeros((NVEC,), np.float32)
    for number in range(NVEC - 1):
        if number % 12 in (3, 10):
            row_kind[number] = 1.0
    gain_rows = jnp.asarray(row_kind)[:, None]
    noise = jax.random.normal(jax.random.fold_in(key, 31), (NVEC, MODEL_DIMENSION), jnp.float32)
    return gain_rows * (1.0 + 0.1 * noise) + (1.0 - gain_rows) * (0.3 * noise)


def block_levels(stream_key, dims, split, low, largest):
    def one(dim, shards_of):
        draws = jax.random.uniform(jax.random.fold_in(jax.random.fold_in(stream_key, 6), dim), (shards_of,), jnp.float32, low / len(split), largest / len(split))
        return jnp.repeat(jnp.exp(draws), dims[dim] // shards_of).reshape((-1,) + (1,) * (len(dims) - dim - 1))

    gain = one(*split[0])
    for cut in split[1:]:
        gain = gain * one(*cut)
    return gain


def split_up(number_of, total, bound, lean):
    weights = [(1 << 20) // math.isqrt(standing ** lean) + 1 for standing in range(2, number_of + 1)]
    spare, counts = total - bound - (number_of - 1), [1] * (number_of - 1)
    while spare > 0:
        free = [i for i in range(number_of - 1) if counts[i] < bound]
        whole, budget = sum([weights[i] for i in free]), spare
        for i in free:
            addition = min(bound - counts[i], max(1, budget * weights[i] // whole), spare)
            counts[i] = counts[i] + addition
            spare = spare - addition
    return np.array([bound] + counts)


def uneven_parts(stream_key, amount, total, limit, skew):
    if amount == 2:
        one = jax.random.randint(stream_key, (), max(1, total - limit), min(limit, total - 1) + 1)
        return jnp.stack([one, total - one])
    sizes = jnp.asarray(split_up(amount, total, limit, skew), jnp.int32)
    couples = (amount - 1) // 2
    donor, sink = sizes[1:1 + 2 * couples:2], sizes[2:2 + 2 * couples:2]
    margin = jnp.minimum(donor - 1, limit - sink)
    shifted = jax.random.randint(jax.random.fold_in(stream_key, 1), (couples,), 0, 1 << 20) % (margin + 1)
    sizes = sizes.at[1:1 + 2 * couples:2].set(donor - shifted).at[2:2 + 2 * couples:2].set(sink + shifted)
    return sizes[jax.random.permutation(jax.random.fold_in(stream_key, 2), amount)]


def scatter_about(rng, extent, scale, bound, shards=(), kind=jnp.bfloat16):
    factor_of = block_levels(rng, extent, shards, -0.22, 0.18) if shards else 1.0
    values = jax.random.normal(rng, extent, jnp.float32) * scale * factor_of
    return jnp.minimum(jnp.maximum(values, -bound), bound).astype(kind)


def setup_inputs(seed: int = 0) -> dict:
    key_list = jax.random.split(jax.random.key(seed), 11)
    tokens = scatter_about(key_list[0], (TOKENS, MODEL_DIMENSION), 1.0, 6.0, ((0, 32),))
    lengths = jax.vmap(lambda own: uneven_parts(own, SENTS, SEQ, MOST, 2))(jax.random.split(key_list[1], NROWS)).reshape((NROWS, SENTS)).astype(jnp.int32)
    pair_index = draw_pair_index(jax.random.fold_in(key_list[10], 71), 0)
    tile_slot = draw_tile_slot(jax.random.fold_in(key_list[10], 71), 0)
    master_store = draw_master_store(jax.random.fold_in(key_list[10], 71), 0)
    first_moment_store = scatter_about(key_list[5], (WEIGHT_SLOTS, MODEL_DIMENSION, MODEL_DIMENSION), (0.0017 / SENTENCE_COUNT ** 0.5), 0.0014648438, ((0, 8), (1, 4)), jnp.float32)
    second_moment_store = jnp.clip(jnp.exp(math.log(3.515624902306058e-09) - 1.4087672 * jax.random.uniform(key_list[6], (WEIGHT_SLOTS, MODEL_DIMENSION, MODEL_DIMENSION), jnp.float32) ** block_levels(key_list[6], (WEIGHT_SLOTS, MODEL_DIMENSION, MODEL_DIMENSION), ((0, 8), (1, 4)), -0.2, 0.2)), 8.593750155938551e-10, 3.515624902306058e-09)
    vectors = draw_vectors(jax.random.fold_in(key_list[10], 71), 0)
    vector_first = scatter_about(key_list[8], (NVEC, MODEL_DIMENSION), (0.005 / SENTENCE_COUNT ** 0.5), 0.0048828125, (), jnp.float32)
    vector_second = jnp.clip(jnp.exp(jax.random.uniform(key_list[9], (NVEC, MODEL_DIMENSION), jnp.float32, math.log(7.812499980275334e-09), math.log(3.1249999921101335e-08))), 7.812499980275334e-09, 3.1249999921101335e-08)
    return {"tokens": tokens, "lengths": lengths, "pair_index": pair_index, "tile_slot": tile_slot, "master_store": master_store, "first_moment_store": first_moment_store, "second_moment_store": second_moment_store, "vectors": vectors, "vector_first": vector_first, "vector_second": vector_second}


@jax.custom_vjp
def low(v):
    return lax.optimization_barrier(v.astype(jnp.bfloat16)).astype(jnp.float32)

@jax.custom_vjp
def low_back(v):
    return v

def low_keep(v):
    return (low(v), None)

def low_pass(kept, grad):
    return (grad,)

def back_keep(v):
    return (v, None)

def back_low(kept, grad):
    return (low(grad),)
low.defvjp(low_keep, low_pass)
low_back.defvjp(back_keep, back_low)
norm_eps = 1e-12
unit_eps = 1e-06
logit_sharpness_divisor = 0.05
first_decay = 0.9
second_decay = 0.999
adam_eps = 1e-08
weight_decay = 0.01
vector_rate = 0.5
store_rate_factor = 1.5
highest = lax.Precision.HIGHEST

def linear_map_apply(left_side, right_side):
    return jnp.dot(left_side, right_side, preferred_element_type=jnp.float32, precision=highest)

def layer_norm(values, gain_values, shift_values):
    center = values - lax.optimization_barrier(jnp.mean(values, axis=-1, keepdims=True))
    spread = lax.optimization_barrier(jnp.mean(center * center, axis=-1, keepdims=True))
    return center * lax.rsqrt(spread + norm_eps) * gain_values + shift_values

def gelu_exact(values):
    return 0.5 * values * (1.0 + lax.erf(values * (1.0 / math.sqrt(2.0))))

def attend_row(joint_row, seg_row):
    queries = joint_row[:, :MODEL_DIMENSION].reshape(SEQ, HEADS, HEAD_DIM)
    keys_here = joint_row[:, MODEL_DIMENSION:2 * MODEL_DIMENSION].reshape(SEQ, HEADS, HEAD_DIM)
    values_here = joint_row[:, 2 * MODEL_DIMENSION:].reshape(SEQ, HEADS, HEAD_DIM)
    raw_scores = jnp.einsum('qhd,khd->hqk', queries, keys_here, precision=highest)
    scores = low_back(raw_scores) * (1.0 / math.sqrt(HEAD_DIM))
    same_segment = seg_row[:, None] == seg_row[None, :]
    scores = jnp.where(same_segment[None], scores, -1e+30)
    row_peak = lax.optimization_barrier(jnp.max(scores, axis=-1, keepdims=True))
    weights = jnp.exp(scores - row_peak)
    row_probabilities = weights / lax.optimization_barrier(jnp.sum(weights, axis=-1, keepdims=True))
    mixed_heads = jnp.einsum('hqk,khd->qhd', low(row_probabilities), values_here, precision=highest)
    return mixed_heads.reshape(SEQ, MODEL_DIMENSION)

def layer_apply(row_block, block_segment, weight_tiles, vectors, base):
    flat = row_block.reshape(-1, MODEL_DIMENSION)
    joint_weight = jnp.concatenate([weight_tiles[base], weight_tiles[base + 1], weight_tiles[base + 2]], axis=1)
    up_weight = jnp.concatenate([weight_tiles[base + 4 + number] for number in range(4)], axis=1)
    down_weight = jnp.concatenate([weight_tiles[base + 8 + number] for number in range(4)], axis=0)
    joint_bias = jnp.concatenate([vectors[base], jnp.zeros((MODEL_DIMENSION,), jnp.float32), vectors[base + 1]])
    inputs_low = low(flat)
    joint_out = low(low_back(linear_map_apply(inputs_low, joint_weight) + joint_bias))
    mixed = jax.vmap(attend_row)(joint_out.reshape(-1, SEQ, 3 * MODEL_DIMENSION), block_segment).reshape(-1, MODEL_DIMENSION)
    mixed_low = low(low_back(mixed))
    branch = low_back(linear_map_apply(mixed_low, weight_tiles[base + 3]) + vectors[base + 2])
    hidden = layer_norm(flat + branch, vectors[base + 3], vectors[base + 4])
    pre_gelu = low_back(linear_map_apply(low(hidden), up_weight) + vectors[base + 5:base + 9].reshape(-1))
    output = low_back(linear_map_apply(low(gelu_exact(pre_gelu)), down_weight) + vectors[base + 9])
    result = layer_norm(hidden + output, vectors[base + 10], vectors[base + 11])
    return result.reshape(row_block.shape)

def adam_step(weights, first_moment, second_moment, grad_values, step_rate):
    first_new = first_decay * first_moment + (1.0 - first_decay) * grad_values
    second_new = second_decay * second_moment + (1.0 - second_decay) * grad_values * grad_values
    first_hat = first_new / (1.0 - first_decay ** STEP)
    second_hat = second_new / (1.0 - second_decay ** STEP)
    new_weights = weights - step_rate * (first_hat / (jnp.sqrt(second_hat) + adam_eps) + weight_decay * weights)
    return (new_weights, first_new, second_new)

def pick_rows(row_values, row_starts):
    return row_values[row_starts]

def reference(tokens, lengths, pair_index, tile_slot, master_store, first_moment_store, second_moment_store, vectors, vector_first, vector_second):
    starts = jnp.cumsum(lengths, axis=1) - lengths
    places = jnp.arange(SEQ, dtype=jnp.int32)
    segment = lax.optimization_barrier(jnp.sum((places[None, :, None] >= starts[:, None, :]).astype(jnp.int32), axis=2)) - 1
    sent_ids = jnp.arange(SENTENCE_COUNT, dtype=jnp.int32)
    group = math.gcd(NROWS, max(1, 4096 // SEQ))

    def loss_of(tokens_in, store_in, vectors_in):
        weight_tiles = low(jnp.take(store_in, tile_slot, axis=0))

        def group_apply(carry_value, row_items):
            row_block, block_segment = row_items
            for layer_number in range(LAYERS):
                row_block = layer_apply(row_block, block_segment, weight_tiles, vectors_in, 12 * layer_number)
            return (carry_value, row_block)
        carry_out, encoded = lax.scan(jax.checkpoint(group_apply), jnp.zeros((), jnp.float32), (tokens_in.reshape(NROWS // group, group, SEQ, MODEL_DIMENSION), segment.reshape(NROWS // group, group, SEQ)))
        encoded = encoded.reshape(NROWS, SEQ, MODEL_DIMENSION)
        cls_rows = jax.vmap(pick_rows)(encoded, starts).reshape(SENTENCE_COUNT, MODEL_DIMENSION)
        pre_pool = low_back(linear_map_apply(low(cls_rows), weight_tiles[SQUARE_TILES - 1]) + vectors_in[NVEC - 1])
        pooled = jnp.tanh(pre_pool)
        unit_rows = pooled * lax.rsqrt(lax.optimization_barrier(jnp.sum(pooled * pooled, axis=1, keepdims=True)) + unit_eps)
        unit_low = low(unit_rows)
        angular_closeness = low_back(linear_map_apply(unit_low, unit_low.T)) / logit_sharpness_divisor
        angular_closeness = jnp.where(sent_ids[:, None] == sent_ids[None, :], -1e+30, angular_closeness)
        row_peak = lax.optimization_barrier(jnp.max(angular_closeness, axis=1, keepdims=True))
        log_mass = row_peak[:, 0] + jnp.log(lax.optimization_barrier(jnp.sum(jnp.exp(angular_closeness - row_peak), axis=1)))
        positive = lax.optimization_barrier(jnp.sum(jnp.where(sent_ids[None, :] == pair_index[:, None], angular_closeness, 0.0), axis=1))
        return jnp.mean(log_mass - positive)
    mean_loss, pullback = jax.vjp(loss_of, tokens.astype(jnp.float32), master_store, vectors)
    d_tokens, store_grad, vector_grad = pullback(jnp.ones((), jnp.float32))
    new_store, new_store_first, new_store_second = adam_step(master_store, first_moment_store, second_moment_store, store_grad, store_rate_factor / math.sqrt(MODEL_DIMENSION))
    new_vectors, new_vector_first, new_vector_second = adam_step(vectors, vector_first, vector_second, vector_grad, vector_rate)
    out_bias_grad = vector_grad[12 * (LAYERS - 1) + 2]
    return (d_tokens, mean_loss, store_grad, new_store, new_store_first, new_store_second, vector_grad, new_vectors, new_vector_first, new_vector_second, out_bias_grad)
```

```python
import functools
import math

import jax
import jax.numpy as jnp
from jax import lax
from jax.experimental import pallas as pl
from jax.experimental.pallas import tpu as pltpu
from jax.sharding import PartitionSpec as P

HEADS = 12
LAYERS = 2
STEP = 10


norm_eps = 1e-12
unit_eps = 1e-06
logit_sharpness_divisor = 0.05
first_decay = 0.9
second_decay = 0.999
adam_eps = 1e-08
weight_decay = 0.01
vector_rate = 0.5
store_rate_factor = 1.5
root_half = 1.0 / math.sqrt(2.0)
slope_norm = 1.0 / math.sqrt(2.0 * math.pi)


MESH = pl.DeviceIdType.MESH
D = 768
H = 384
R = 48
BIG = 67043328 - 256 * 1024


def remote(src, dst, s, r, dev):
    return pltpu.make_async_remote_copy(
        src_ref=src, dst_ref=dst, send_sem=s, recv_sem=r, device_id=dev, device_id_type=MESH
    )


def place():
    z = lax.axis_index("row")
    c = lax.axis_index("col")
    return z, c, c // 4, (c // 2) % 2, c % 2


def col_peer(c, d):
    return lax.rem(c + d, 8)


def row_peer(z, d):
    return lax.rem(z + d, 4)


def half_of(k):
    return pl.ds(pl.multiple_of(k * H, H), H)


BF = jnp.bfloat16
F32 = jnp.float32
KT = 14
ORDER = tuple(range(12)) + (13, 14, 12, 15) + tuple(range(16, 25))


def dot_nn(left, right):
    return jnp.dot(left, right, preferred_element_type=F32)


def dot_nt(left, right):
    return lax.dot_general(left, right, (((1,), (1,)), ((), ())), preferred_element_type=F32)


def dot_tn(left, right):
    return lax.dot_general(left, right, (((0,), (0,)), ((), ())), preferred_element_type=F32)


def colsum(v):
    return jnp.sum(v.astype(F32), axis=0, keepdims=True)


def norm_rows(v):
    center = v - jnp.mean(v, axis=1, keepdims=True)
    factor = lax.rsqrt(jnp.mean(center * center, axis=1, keepdims=True) + norm_eps)
    return center * factor, factor


def norm_rows_back(grad, normed, factor, gain):
    e = grad * gain
    return factor * (e - jnp.mean(e, axis=1, keepdims=True) - normed * jnp.mean(e * normed, axis=1, keepdims=True))


def window(block):
    return max(0, block - 1) * 128, min(4, block + 2) * 128


def forward_kernel(
    T, total, slot_ref, len_ref, pair_ref, master_ref, tok_ref, vec_ref, pairr_ref,
    w_out, qkv_out, p_out, o_out, n1_out, h1_out, act_out, slope_out, n2_out, s_out, low_out,
    dkv_ref, dcls_ref, packed_ref, right_ref, vg_ref, loss_ref,
    w, stage, spread, qkv, prob, mixed, acc, normed, h1, h1b, u1b, act, slope, fac, kv, bias, uc, acts, slopes, unit, everyone,
    lsem, xs, xr, zs, zr, as_, ar, bs, br, cs, cr, osem, fsem, ss, sr,
):
    z, c, y, x, k = place()
    cx = c + 2 - 4 * x
    cy = c + 4 - 8 * y
    ck = c + 1 - 2 * k
    half = half_of(k)
    me = z * 8 + c
    bar = pltpu.get_barrier_semaphore()

    def peer(d):
        p = lax.rem(me + d, 32)
        return p, (p // 8, lax.rem(p, 8))

    def greet(d, _):
        pl.semaphore_signal(bar, inc=1, device_id=peer(d)[1], device_id_type=MESH)
        return 0

    lax.fori_loop(1, 32, greet, 0)

    def cast(s, _):
        stage[s] = master_ref[s].reshape(4, R, D).astype(BF)
        return 0

    lax.fori_loop(0, 4, cast, 0)
    pl.semaphore_wait(bar, 31)

    def spread_copy(d):
        p = col_peer(c, d)
        return remote(stage.at[:, p // 2, :, half_of(p % 2)], spread.at[pl.ds(4 * c, 4)], xs.at[d - 1], xr.at[d - 1], (z, p))

    for d in range(1, 8):
        spread_copy(d).start()
    own = pltpu.make_async_copy(stage.at[:, c // 2, :, half], spread.at[pl.ds(4 * c, 4)], lsem)
    own.start()
    starts = [0]
    for i in range(7):
        starts.append(starts[i] + len_ref[i])
    row_places = lax.broadcasted_iota(jnp.int32, (1, 512), 1)
    segr = jnp.zeros((1, 512), jnp.int32)
    for i in range(1, 8):
        segr = segr + (row_places >= starts[i]).astype(jnp.int32)
    for b in range(4):
        lo, hi = window(b)
        places = lax.broadcasted_iota(jnp.int32, (128, 1), 0) + 128 * b
        segc = jnp.zeros((128, 1), jnp.int32)
        for i in range(1, 8):
            segc = segc + (places >= starts[i]).astype(jnp.int32)
        bias[b, :, 0 : hi - lo] = jnp.where(segc == segr[:, lo:hi], 0.0, -1e30)
    own.wait()
    for d in range(1, 8):
        spread_copy(d).wait_recv()

    def zcopies(t):
        v = w.at[t, z, y, x, :, half]
        return [remote(v, v, zs.at[t, d - 1], zr.at[t, d - 1], (row_peer(z, d), c)) for d in (1, 2, 3)]

    def first(t):
        va, vb = w.at[t, 0:2, y, x, :, half], w.at[t, 2:4, y, x, :, half]
        return [remote(va, va, as_.at[t, 0], ar.at[t, 0], (z, cx)), remote(vb, vb, as_.at[t, 1], ar.at[t, 1], (z, cy))]

    def second(t):
        va, vb = w.at[t, 0:2, y, :, :, half], w.at[t, 2:4, :, x, :, half]
        return [remote(va, va, bs.at[t, 0], br.at[t, 0], (z, cy)), remote(vb, vb, bs.at[t, 1], br.at[t, 1], (z, cx))]

    def core(t):
        v = w.at[t, :, :, :, :, half]
        return remote(v, v, cs.at[t], cr.at[t], (z, ck))

    def outc(t):
        return pltpu.make_async_copy(w.at[t], w_out.at[t], osem.at[t])

    for t in range(T):
        w[t, z, y, x, :, half] = spread[slot_ref[ORDER[t]]]

    def issue(t, _):
        for cpy in zcopies(t):
            cpy.start()
        return 0

    lax.fori_loop(0, KT, issue, 0)

    def pair_first(t):
        v = w.at[t, z, y, x, :, half]
        return remote(v, v, as_.at[t, 0], ar.at[t, 0], (z, cx if t % 2 == 0 else cy))

    def pair_z(t):
        v = w.at[t, z, y, :, :, half] if t % 2 == 0 else w.at[t, z, :, x, :, half]
        return [remote(v, v, zs.at[t, d - 1], zr.at[t, d - 1], (row_peer(z, d), c)) for d in (1, 2, 3)]

    def pair_last(t):
        v = w.at[t, :, y, :, :, half] if t % 2 == 0 else w.at[t, :, :, x, :, half]
        return remote(v, v, bs.at[t, 0], br.at[t, 0], (z, cy if t % 2 == 0 else cx))

    for t in range(KT, T):
        pair_first(t).start()
    LAGS = (0, 1, 3, 4)

    def f0(t):
        if isinstance(t, int) and t >= KT:
            for cpy in pair_z(t):
                cpy.wait_recv()
            pair_last(t).start()
            return
        for cpy in zcopies(t):
            cpy.wait_recv()
        for cpy in first(t):
            cpy.start()

    def f1(t):
        if isinstance(t, int) and t >= KT:
            return
        for there, on in zip(first(t), second(t)):
            there.wait_recv()
            on.start()

    def f2(t):
        for cpy in [pair_last(t)] if isinstance(t, int) and t >= KT else second(t):
            cpy.wait_recv()
        core(t).start()

    def f3(t):
        core(t).wait_recv()
        outc(t).start()

    state = [0]

    def pump():
        i = state[0]
        if i < T + LAGS[3]:
            for f, lag in zip((f0, f1, f2, f3), LAGS):
                if 0 <= i - lag < T:
                    f(i - lag)
            state[0] = i + 1

    def pump_at(i):
        for f, lag in zip((f0, f1, f2, f3), LAGS):
            f(i - lag)

    def need(t):
        if isinstance(t, int):
            while state[0] <= t + LAGS[3]:
                pump()

    flushes = []
    counter = [0]

    def flush(src, dst):
        cpy = pltpu.make_async_copy(src, dst, fsem.at[counter[0]])
        counter[0] += 1
        cpy.start()
        flushes.append(cpy)

    def wcols(t, n):
        return w[t, :, :, :, :, pl.ds(pl.multiple_of(n * 256, 256), 256)].reshape(D, 256)

    def cols(n):
        return pl.ds(pl.multiple_of(n * 256, 256), 256)

    def norm(gain, shift, normed, out, low, number):
        def rows(m, _):
            rs = pl.ds(pl.multiple_of(m * 64, 64), 64)
            v = acc[rs, :]
            center = v - jnp.mean(v, axis=1, keepdims=True)
            factor = lax.rsqrt(jnp.mean(center * center, axis=1, keepdims=True) + norm_eps)
            nv = center * factor
            normed[rs, :] = nv
            fac[rs, number : number + 1] = factor
            o = nv * gain + shift
            out[rs, :] = o
            if low is not None:
                low[rs, :] = o.astype(BF)
            return 0

        lax.fori_loop(0, 8, rows, 0)

    for part in range(3):
        need(part)
        if part == 1:
            for t in range(KT, T):
                pair_first(t).wait_recv()
                for cpy in pair_z(t):
                    cpy.start()

        def project(n, _):
            r = dot_nn(tok_ref[...], wcols(part, n))
            if part != 1:
                r = r + vec_ref[part // 2 : part // 2 + 1, cols(n)]
            qkv[part, :, cols(n)] = r.astype(BF)
            return 0

        lax.fori_loop(0, 3, project, 0)
    flush(qkv, qkv_out)
    left = lax.broadcasted_iota(jnp.int32, (1, 128), 1) < 64

    keep_left = jnp.where(left, 0.125, 0.0).astype(BF)
    keep_right = jnp.where(left, 0.0, 0.125).astype(BF)

    def pair(p, side):
        lanes = pl.ds(pl.multiple_of(p * 128, 128), 128)
        for b in range(4):
            lo, hi = window(b)
            q = qkv[0, 128 * b : 128 * (b + 1), lanes]
            kk = qkv[1, lo:hi, lanes]
            vv = qkv[2, lo:hi, lanes]
            s = dot_nt(jnp.concatenate([q * keep_left, q * keep_right], axis=0), kk)
            mask = bias[b, :, 0 : hi - lo]
            s = s + jnp.concatenate([mask, mask], axis=0)
            ex = jnp.exp(s - jnp.max(s, axis=1, keepdims=True))
            pr = (ex * (1.0 / jnp.sum(ex, axis=1, keepdims=True))).astype(BF)
            prob[side, b, :, 0 : hi - lo] = pr
            big = dot_nn(pr, vv)
            mixed[128 * b : 128 * (b + 1), lanes] = jnp.where(left, big[0:128, :], big[128:256, :]).astype(BF)

    def pairs(m, _):
        for side in range(2):
            p = 2 * m + side
            slot = prob.at[side]
            out = pltpu.make_async_copy(slot, p_out.at[p], fsem.at[20 + side])

            @pl.when(m > 0)
            def _():
                out.wait()

            pair(p, side)
            out.start()
            pump_at(base + p)
        return 0

    base = state[0]
    lax.fori_loop(0, 3, pairs, 0)
    state[0] = base + 6
    for side in range(2):
        pltpu.make_async_copy(prob.at[side], p_out.at[4 + side], fsem.at[20 + side]).wait()
    flush(mixed, o_out)
    need(3)

    def attend_out(n, _):
        acc[:, cols(n)] = (
            dot_nn(mixed[...], wcols(3, n)) + vec_ref[2:3, cols(n)] + tok_ref[:, cols(n)].astype(F32)
        )
        return 0

    lax.fori_loop(0, 3, attend_out, 0)
    norm(vec_ref[3:4, :], vec_ref[4:5, :], normed, h1, h1b, 0)
    flush(normed, n1_out)
    first_norm = flushes.pop()
    flush(h1b, h1_out)
    slope_copies = []
    for j in range(4):
        need(4 + j)

        def up(n, _):
            acc[:, cols(n)] = dot_nn(h1b[...], wcols(4 + j, n)) + vec_ref[5 + j : 6 + j, cols(n)]
            return 0

        lax.fori_loop(0, 3, up, 0)

        def gelu(m, _):
            rs = pl.ds(pl.multiple_of(m * 32, 32), 32)
            f = acc[rs, :]
            cdf = 0.5 * (1.0 + lax.erf(f * root_half))
            act[j, rs, :] = (f * cdf).astype(BF)
            slope[j % 2, rs, :] = (cdf + f * jnp.exp(-0.5 * f * f) * slope_norm).astype(BF)
            return 0

        if j >= 2:
            slope_copies[j - 2].wait()
        lax.fori_loop(0, 16, gelu, 0)
        flush(act.at[j], act_out.at[j])
        slope_copies.append(pltpu.make_async_copy(slope.at[j % 2], slope_out.at[j], fsem.at[22 + j % 2]))
        slope_copies[j].start()
    for j in range(4):
        need(8 + j)

        def down(n, _):
            r = dot_nn(act[j], wcols(8 + j, n))
            if j == 0:
                acc[:, cols(n)] = r + vec_ref[9:10, cols(n)] + h1[:, cols(n)]
            else:
                acc[:, cols(n)] += r
            return 0

        lax.fori_loop(0, 3, down, 0)
    first_norm.wait()
    norm(vec_ref[10:11, :], vec_ref[11:12, :], normed, h1, u1b, 1)
    flush(normed, n2_out)
    flush(fac, s_out)
    flush(u1b, low_out)
    for part in range(2):
        need(12 + part)

        def project_next(n, _):
            r = dot_nn(u1b[...], wcols(12 + part, n))
            if part == 1:
                r = r + vec_ref[13:14, cols(n)]
            kv[part, :, cols(n)] = r.astype(BF)
            return 0

        lax.fori_loop(0, 3, project_next, 0)
    def tile(t):
        return w[t].reshape(D, D)

    def vrow(r):
        return vec_ref[12 + r : 13 + r, :]

    def emit(r, v):
        vg_ref[r : r + 1, :] = v

    head_of = lax.broadcasted_iota(jnp.int32, (1, D), 1) // 64

    def by_head(v):
        v = v.astype(F32)
        return jnp.concatenate([jnp.where(head_of == h, v, 0.0) for h in range(12)], axis=0).astype(BF)

    def from_heads(big):
        out = jnp.where(head_of == 0, big[0:8, :], 0.0)
        for h in range(1, 12):
            out = out + jnp.where(head_of == h, big[8 * h : 8 * h + 8, :], 0.0)
        return out

    for s in range(8):
        uc[s : s + 1, :] = h1[pl.ds(starts[s], 1), :]
    low = uc[...].astype(BF)
    need(14)
    q = (dot_nn(low, tile(14)) + vrow(0)).astype(BF)
    qbig = by_head(q)
    same = segr == lax.broadcasted_iota(jnp.int32, (8, 512), 0)
    bias = jnp.where(same, 0.0, -1e30)
    sc = dot_nt(qbig, kv[0]) * 0.125 + jnp.concatenate([bias] * 12, axis=0)
    ex = jnp.exp(sc - jnp.max(sc, axis=1, keepdims=True))
    prob = ex * (1.0 / jnp.sum(ex, axis=1, keepdims=True))
    plow = prob.astype(BF)
    o = from_heads(dot_nn(plow, kv[1])).astype(BF)
    need(15)
    n1, s1 = norm_rows(uc[...] + dot_nn(o, tile(15)) + vrow(2))
    h1 = n1 * vrow(3) + vrow(4)
    h1b_cls = h1.astype(BF)
    need(19)

    def up_cls(j, _):
        f = dot_nn(h1b_cls, tile(16 + j)) + vec_ref[pl.ds(17 + j, 1), :]
        cdf = 0.5 * (1.0 + lax.erf(f * root_half))
        acts[j] = (f * cdf).astype(BF)
        slopes[j] = cdf + f * jnp.exp(-0.5 * f * f) * slope_norm
        return 0

    lax.fori_loop(0, 4, up_cls, 0)
    need(23)
    out = lax.fori_loop(0, 4, lambda j, total_: total_ + dot_nn(acts[j], tile(20 + j)), h1 + vrow(9))
    n2, s2 = norm_rows(out)
    zb = (n2 * vrow(10) + vrow(11)).astype(BF)
    need(24)
    pooled = jnp.tanh(dot_nn(zb, tile(24)) + vrow(12))
    inv = lax.rsqrt(jnp.sum(pooled * pooled, axis=1, keepdims=True) + unit_eps)
    unit[...] = (pooled * inv).astype(BF)
    everyone[me] = unit[...]

    def send(d, _):
        p, dev = peer(d)
        remote(unit, everyone.at[me], ss.at[d], sr.at[d], dev).start()
        return 0

    lax.fori_loop(1, 32, send, 0)
    packed_ref[...] = jnp.zeros((16, 4, 8, 128), BF)
    wholes = (acts[0], acts[1], acts[2], acts[3], h1b_cls, o, low, zb)
    for n, v in enumerate(wholes):
        v = v.astype(F32)
        off = 64 * (n % 2)
        for i in range(16):
            packed_ref[i, n // 2, :, off : off + R] = v[:, R * i : R * i + R].astype(BF)

    def arrive(d, _):
        q_ = lax.rem(me + 32 - d, 32)
        remote(unit, everyone.at[q_], ss.at[d], sr.at[d], peer(d)[1]).wait()
        return 0

    lax.fori_loop(1, 32, arrive, 0)
    everybody = everyone[...].astype(F32).reshape(256, D).astype(BF)
    sim = dot_nt(everybody, everybody) / logit_sharpness_divisor
    ri = lax.broadcasted_iota(jnp.int32, (256, 256), 0)
    ci = lax.broadcasted_iota(jnp.int32, (256, 256), 1)
    sim = jnp.where(ri == ci, -1e30, sim)
    peak = jnp.max(sim, axis=0, keepdims=True)
    lse = peak + jnp.log(jnp.sum(jnp.exp(sim - peak), axis=0, keepdims=True))
    pos = jnp.sum(jnp.where(ri == pairr_ref[...], sim, 0.0), axis=0, keepdims=True)
    loss_ref[...] = jnp.sum(lse - pos, axis=1, keepdims=True) / total
    own = dot_nt(unit[...], everybody) / logit_sharpness_divisor
    oi = lax.broadcasted_iota(jnp.int32, (8, 256), 0) + me * 8
    oj = lax.broadcasted_iota(jnp.int32, (8, 256), 1)
    own = jnp.where(oi == oj, -1e30, own)
    opeak = jnp.max(own, axis=1, keepdims=True)
    olse = opeak + jnp.log(jnp.sum(jnp.exp(own - opeak), axis=1, keepdims=True))
    sub = lax.broadcasted_iota(jnp.int32, (8, 1), 0)
    opair = jnp.zeros((8, 1), jnp.int32)
    for s in range(8):
        opair = jnp.where(sub == s, pair_ref[me * 8 + s], opair)
    g_rows = ((jnp.exp(own - olse) - (oj == opair).astype(F32)) / total / logit_sharpness_divisor).astype(BF)
    g_cols = ((jnp.exp(own - lse) - (pairr_ref[...] == oi).astype(F32)) / total / logit_sharpness_divisor).astype(BF)
    dunit = dot_nn(g_rows, everybody) + dot_nn(g_cols, everybody)
    dpooled = inv * dunit - pooled * (inv * inv * inv * jnp.sum(pooled * dunit, axis=1, keepdims=True))
    dpre = (dpooled * (1.0 - pooled * pooled)).astype(BF)
    right_ref[0] = dpre
    emit(12, colsum(dpre))
    dz = dot_nt(dpre, tile(24))
    emit(10, colsum(dz * n2))
    emit(11, colsum(dz))
    dr2 = norm_rows_back(dz, n2, s2, vrow(10))
    dy = dr2.astype(BF)
    right_ref[1] = dy
    emit(9, colsum(dy))

    def down_cls(j, dh):
        df = (dot_nt(dy, tile(20 + j)) * slopes[j]).astype(BF)
        right_ref[2 + j] = df
        vg_ref[pl.ds(5 + j, 1), :] = colsum(df)
        return dh + dot_nt(df, tile(16 + j))

    dh = lax.fori_loop(0, 4, down_cls, dr2)
    emit(3, colsum(dh * n1))
    emit(4, colsum(dh))
    dr1 = norm_rows_back(dh, n1, s1, vrow(3))
    da = dr1.astype(BF)
    right_ref[6] = da
    emit(2, colsum(da))
    dobig = by_head(dot_nt(da, tile(15)).astype(BF))
    dp = dot_nt(dobig, kv[1])
    ds = (prob * (dp - jnp.sum(prob * dp, axis=1, keepdims=True)) * 0.125).astype(BF)
    dq = from_heads(dot_nn(ds, kv[0])).astype(BF)
    right_ref[7] = dq
    emit(0, colsum(dq))
    dcls_ref[...] = dot_nt(dq, tile(14)) + dr1
    dkv_ref[0] = dot_tn(ds, qbig).astype(BF)
    dv = dot_tn(plow, dobig).astype(BF)
    dkv_ref[1] = dv
    emit(1, colsum(dv))
    for d in range(1, 8):
        spread_copy(d).wait_send()

    def drain(t, _):
        for cpy in zcopies(t) + first(t) + second(t) + [core(t)]:
            cpy.wait_send()
        outc(t).wait()
        return 0

    lax.fori_loop(0, KT, drain, 0)
    for t in range(KT, T):
        for cpy in pair_z(t) + [pair_first(t), pair_last(t), core(t)]:
            cpy.wait_send()
        outc(t).wait()
    for cpy in slope_copies[2:]:
        cpy.wait()
    for cpy in flushes:
        cpy.wait()


def forward_fused(slots, master, tokens, lengths, vectors, pair_index):
    T = slots.shape[0]
    total = pair_index.shape[0]
    dma = lambda *n: pltpu.SemaphoreType.DMA(n)
    V = pl.BlockSpec(memory_space=pltpu.VMEM)
    S = pl.BlockSpec(memory_space=pltpu.SMEM)
    ANY = pl.BlockSpec(memory_space=pl.ANY)
    shapes = [
        ((T, 4, 2, 2, R, D), BF), ((3, 512, D), BF), ((6, 4, 256, 384), BF), ((512, D), BF), ((512, D), F32), ((512, D), BF),
        ((4, 512, D), BF), ((4, 512, D), BF), ((512, D), F32), ((512, 2), F32), ((512, D), BF),
        ((2, 512, D), BF), ((8, D), F32), ((16, 4, 8, 128), BF), ((8, 8, D), BF), ((13, D), F32), ((1, 1), F32),
    ]
    vm = pltpu.VMEM
    scratch = [
        vm((T, 4, 2, 2, R, D), BF), vm((4, 4, R, D), BF), vm((32, R, H), BF), vm((3, 512, D), BF), vm((2, 4, 256, 384), BF), vm((512, D), BF),
        vm((512, D), F32), vm((512, D), F32), vm((512, D), F32), vm((512, D), BF), vm((512, D), BF), vm((4, 512, D), BF), vm((2, 512, D), BF),
        vm((512, 2), F32), vm((2, 512, D), BF), vm((4, 128, 384), F32), vm((8, D), F32), vm((4, 8, D), BF), vm((4, 8, D), F32), vm((8, D), BF), vm((32, 8, D), BF),
        dma(), dma(7), dma(7), dma(T, 3), dma(T, 3), dma(T, 2), dma(T, 2), dma(T, 2), dma(T, 2), dma(T), dma(T), dma(T), dma(24), dma(32), dma(32),
    ]
    return pl.pallas_call(
        functools.partial(forward_kernel, T, total),
        out_shape=tuple(jax.ShapeDtypeStruct(*s) for s in shapes),
        in_specs=[S, S, S] + [V] * 4,
        out_specs=(ANY,) * 11 + (V,) * 6,
        scratch_shapes=scratch,
        compiler_params=pltpu.CompilerParams(collective_id=0, has_side_effects=True, vmem_limit_bytes=BIG),
    )(slots, lengths.reshape(-1), pair_index, master, tokens, vectors, pair_index[None, :])

RS_TILES = (13, 14, 8, 4, 9, 5, 10, 6, 11, 7, 3, 0, 1, 2)
PIECE_ORDER = RS_TILES + (12,) + tuple(range(15, 25))
LATE = 5
FACTOR_MODES = ("xzyk", "yzxk")
FACTOR_TICKS = ((3, 8, 18), (3, 8, 18))
EARLY_LAGS = ((1, 3, 6, 11), (1, 4, 7, 11), (2, 4, 8, 11))
RS_LAGS = (2, 5, 8, 11)
W_SEQ = (12, 13, 8, 4, 9, 5, 10, 6, 11, 7, 3, 0, 1, 2)


def backward_kernel(
    len_ref, src_ref, fill_ref, fac_ref, dcls_ref, packed_ref, right_ref, vg_ref, vec_ref,
    w_ref, a1_ref, tok_ref, qkv_ref, p_ref, o_ref, n1_ref, h1_ref, act_ref, slope_ref, n2_ref, dkv_ref,
    own_ref, vout_ref, dtok_ref,
    g, rc, r1, r2, r3, every, lefts, piece, spread, vecs, vin, vsum,
    wbuf, xbuf, h1b, qkv, prob, dqkv, norm, acc, dy, df, dk_acc, dv_acc,
    cs, cr, as_, ar, bs, br, zs, zr, xs, xr, vs, vr, ws, wr, fs, fr, fz, fzr, ls, lr, wsem, xsem, psem, lsem,
):
    z, c, y, x, k = place()
    cx = c + 2 - 4 * x
    cy = c + 4 - 8 * y
    ck = c + 1 - 2 * k
    me = z * 8 + c
    half = half_of(k)
    other = half_of(1 - k)
    T = len(RS_TILES)
    starts = [0]
    for i in range(7):
        starts.append(starts[i] + len_ref[i])

    def wload(i):
        return pltpu.make_async_copy(w_ref.at[W_SEQ[i]], wbuf.at[i % 3], wsem.at[i % 3])

    x_seq = [a1_ref]
    for j in range(4):
        x_seq += [act_ref.at[j], slope_ref.at[j]]
    x_seq += [o_ref, tok_ref]

    def xload(i):
        return pltpu.make_async_copy(x_seq[i], xbuf.at[i % 4], xsem.at[i % 4])

    def pload(p):
        return pltpu.make_async_copy(p_ref.at[p], prob.at[p % 2], psem.at[p % 2])

    load_dkv = pltpu.make_async_copy(dkv_ref, dqkv.at[pl.ds(0, 2)], lsem.at[0])
    load_n2 = pltpu.make_async_copy(n2_ref, norm, lsem.at[1])
    load_n1 = pltpu.make_async_copy(n1_ref, norm, lsem.at[1])
    load_h1 = pltpu.make_async_copy(h1_ref, h1b, lsem.at[2])
    load_qkv = pltpu.make_async_copy(qkv_ref, qkv, lsem.at[3])
    load_dkv.start()
    xload(0).start()
    wload(0).start()
    wload(1).start()
    load_n2.start()
    for i in (1, 2, 3):
        xload(i).start()
    wload(2).start()
    load_h1.start()
    load_qkv.start()
    pload(0).start()
    pload(1).start()

    bar = pltpu.get_barrier_semaphore()

    def peer(d):
        p = lax.rem(me + d, 32)
        return p, (p // 8, lax.rem(p, 8))

    def greet(d, _):
        pl.semaphore_signal(bar, inc=1, device_id=peer(d)[1], device_id_type=MESH)
        return 0

    lax.fori_loop(1, 32, greet, 0)

    def region(n, have):
        zi = slice(None) if "z" in have else z
        yi = slice(None) if "y" in have else y
        xi = slice(None) if "x" in have else x
        ki = slice(None) if "k" in have else k
        return every.at[zi, yi, xi, ki, 4 * n : 4 * n + 4]

    def factor_copies(n, number):
        mode = FACTOR_MODES[n]
        v = region(n, mode[:number])
        axis = mode[number]
        if axis == "z":
            return [remote(v, v, fz.at[n, d - 1], fzr.at[n, d - 1], (row_peer(z, d), c)) for d in (1, 2, 3)]
        return [remote(v, v, fs.at[n, number], fr.at[n, number], (z, {"x": cx, "y": cy, "k": ck}[axis]))]

    def factor_step(n, number):
        if number:
            for cpy in factor_copies(n, number - 1):
                cpy.wait_recv()
        if number < 4:
            for cpy in factor_copies(n, number):
                cpy.start()

    def factor_stage(number):
        for n in range(2):
            factor_step(n, number)

    every[z, y, x, k] = right_ref[...]
    lefts[me] = packed_ref[me // 2]

    def lcopy(d, row):
        p, dev = peer(d)
        return remote(packed_ref.at[p // 2], lefts.at[row], ls.at[d], lr.at[d], dev)

    def lstart(d, _):
        lcopy(d, me).start()
        return 0

    pl.semaphore_wait(bar, 31)
    factor_stage(0)
    lax.fori_loop(1, 32, lstart, 0)

    def core(t):
        return remote(g.at[t, :, :, :, :, other], rc.at[t], cs.at[t], cr.at[t], (z, ck))

    def first(t):
        return [
            remote(g.at[t, 0:2, 1 - y, :, :, half], r1.at[t, 0:2], as_.at[t, 0], ar.at[t, 0], (z, cy)),
            remote(g.at[t, 2:4, :, 1 - x, :, half], r1.at[t, 2:4], as_.at[t, 1], ar.at[t, 1], (z, cx)),
        ]

    def second(t):
        return [
            remote(g.at[t, 0:2, y, 1 - x, :, half], r2.at[t, 0:2], bs.at[t, 0], br.at[t, 0], (z, cx)),
            remote(g.at[t, 2:4, 1 - y, x, :, half], r2.at[t, 2:4], bs.at[t, 1], br.at[t, 1], (z, cy)),
        ]

    def zcopies(t):
        return [
            remote(g.at[t, row_peer(z, d), y, x, :, half], r3.at[t, d - 1], zs.at[t, d - 1], zr.at[t, d - 1], (row_peer(z, d), c))
            for d in (1, 2, 3)
        ]

    def plus(a, b):
        return (a.astype(F32) + b.astype(F32)).astype(BF)

    def f1(t):
        core(t).wait_recv()
        for part in range(2):
            for zz in (2 * part, 2 * part + 1):
                g[t, zz, :, :, :, half] = plus(g[t, zz, :, :, :, half], rc[t, zz])
            first(t)[part].start()

    def f2(t):
        for part in range(2):
            first(t)[part].wait_recv()
            for zz in (2 * part, 2 * part + 1):
                if part == 0:
                    g[t, zz, y, :, :, half] = plus(g[t, zz, y, :, :, half], r1[t, zz])
                else:
                    g[t, zz, :, x, :, half] = plus(g[t, zz, :, x, :, half], r1[t, zz])
            second(t)[part].start()

    def f3(t):
        for part in range(2):
            second(t)[part].wait_recv()
        for zz in range(4):
            g[t, zz, y, x, :, half] = plus(g[t, zz, y, x, :, half], r2[t, zz])
        for cpy in zcopies(t):
            cpy.start()

    def f4(t):
        for cpy in zcopies(t):
            cpy.wait_recv()
        piece[t] = (
            g[t, z, y, x, :, half].astype(F32) + r3[t, 0].astype(F32) + r3[t, 1].astype(F32) + r3[t, 2].astype(F32)
        ).astype(BF)

    stages = tuple(zip(RS_LAGS, (f1, f2, f3, f4)))
    due = {}
    for n in range(2):
        for number in range(3):
            due.setdefault(FACTOR_TICKS[n][number], []).append(functools.partial(factor_step, n, number + 1))

    state = [0, 0]

    def enter():
        t, now = state[1], state[0]
        core(t).start()
        for lag, f in zip(EARLY_LAGS[t] if t < 3 else RS_LAGS, (f1, f2, f3, f4)):
            due.setdefault(now + lag, []).insert(0, functools.partial(f, t))
        state[1] = t + 1

    def tick():
        for f in due.pop(state[0], []):
            f()
        state[0] += 1

    def wide(b):
        return pl.ds(pl.multiple_of(b * 384, 384), 384)

    def cols(n):
        return pl.ds(pl.multiple_of(n * 256, 256), 256)

    def grad_tile(left, right):
        t = state[1]

        def rows(b, _):
            r = dot_tn(left(wide(b)), right()).astype(BF)
            g[t, pl.ds(2 * b, 2)] = r.reshape(2, 2, 2, R, D)
            return 0

        lax.fori_loop(0, 2, rows, 0)
        enter()
        tick()

    def through(grad, slot, fresh):
        def part(b, _):
            r = dot_nt(grad(), wbuf[slot, cols(b), :])
            if fresh:
                acc[:, cols(b)] = r
            else:
                acc[:, cols(b)] += r
            return 0

        lax.fori_loop(0, 3, part, 0)

    def sums(row, value):
        vecs[row] = jnp.sum(value.astype(F32), axis=0, keepdims=True)

    def fold(v):
        return jnp.sum(v.reshape(8, 8, D), axis=0)

    def norm_back(number, gain, rows_out, place_cls):
        def rows(m, carry):
            rs = pl.ds(pl.multiple_of(m * 64, 64), 64)
            dh = acc[rs, :]
            if place_cls:
                rid = lax.broadcasted_iota(jnp.int32, (64, 1), 0) + m * 64
                for s in range(8):
                    dh = dh + jnp.where(rid == starts[s], dcls_ref[s : s + 1, :], 0.0)
            nv = norm[rs, :]
            e = dh * gain
            dr = fac_ref[rs, number : number + 1] * (
                e - jnp.mean(e, axis=1, keepdims=True) - nv * jnp.mean(e * nv, axis=1, keepdims=True)
            )
            acc[rs, :] = dr
            low = dr.astype(BF)
            dy[rs, :] = low
            a, b, d = carry
            return a + fold(dh * nv), b + fold(dh), d + fold(low.astype(F32))

        zero = jnp.zeros((8, D), F32)
        out = lax.fori_loop(0, 8, rows, (zero, zero, zero))
        for row, v in zip(rows_out, out):
            vecs[row] = jnp.sum(v, axis=0, keepdims=True)

    for i in range(13):
        vecs[12 + i] = vg_ref[i : i + 1, :]
    for i in range(25, 32):
        vecs[i] = jnp.zeros((1, D), F32)

    load_dkv.wait()
    xload(0).wait()
    for part in range(2):
        grad_tile(lambda part_: xbuf[0, :, part_], lambda: dqkv[part])
    xload(4).start()
    for part in range(2):
        wload(part).wait()
        through(lambda: dqkv[part], part, part == 0)
        wload(part + 3).start()
    load_n2.wait()
    norm_back(1, vec_ref[10:11, :], (10, 11, 9), True)
    load_n1.start()
    load_h1.wait()
    for j in range(4):
        xload(1 + 2 * j).wait()
        grad_tile(lambda part_: xbuf[(1 + 2 * j) % 4, :, part_], lambda: dy[...])
        if 5 + 2 * j < 11:
            xload(5 + 2 * j).start()
        wload(2 + 2 * j).wait()
        xload(2 + 2 * j).wait()

        def pre(b, _):
            r = dot_nt(dy[...], wbuf[(2 + 2 * j) % 3, cols(b), :])
            df[:, cols(b)] = (r * xbuf[(2 + 2 * j) % 4, :, cols(b)].astype(F32)).astype(BF)
            return 0

        lax.fori_loop(0, 3, pre, 0)
        if 6 + 2 * j < 11:
            xload(6 + 2 * j).start()
        wload(5 + 2 * j).start()
        grad_tile(lambda part_: h1b[:, part_], lambda: df[...])
        sums(5 + j, df[...])
        wload(3 + 2 * j).wait()
        through(lambda: df[...], (3 + 2 * j) % 3, False)
        if 6 + 2 * j < 14:
            wload(6 + 2 * j).start()
    load_n1.wait()
    norm_back(0, vec_ref[3:4, :], (3, 4, 2), False)
    xload(9).wait()
    grad_tile(lambda part_: xbuf[1, :, part_], lambda: dy[...])
    wload(10).wait()

    def mixed_grad(b, _):
        df[:, cols(b)] = dot_nt(dy[...], wbuf[10 % 3, cols(b), :]).astype(BF)
        return 0

    lax.fori_loop(0, 3, mixed_grad, 0)
    wload(13).start()
    load_qkv.wait()
    left = lax.broadcasted_iota(jnp.int32, (1, 128), 1) < 64
    keep_left = jnp.where(left, 1.0, 0.0).astype(BF)
    keep_right = jnp.where(left, 0.0, 1.0).astype(BF)

    def both(v):
        return jnp.concatenate([v * keep_left, v * keep_right], axis=0)

    entered = state[1]
    base = state[0]

    def pairs(m, _):
        for side in range(2):
            p = 2 * m + side
            lanes = pl.ds(pl.multiple_of(p * 128, 128), 128)
            pltpu.make_async_copy(p_ref.at[p], prob.at[side], psem.at[side]).wait()
            for b in range(4):
                lo, hi = window(b)
                rows = pl.ds(128 * b, 128)
                go = both(df[rows, lanes])
                pr = prob[side, b, :, 0 : hi - lo]
                pf = pr.astype(F32)
                dp = dot_nt(go, qkv[2, lo:hi, lanes])
                ds = (pf * (dp - jnp.sum(pf * dp, axis=1, keepdims=True)) * 0.125).astype(BF)
                dq = dot_nn(ds, qkv[1, lo:hi, lanes])
                dqkv[0, rows, lanes] = jnp.where(left, dq[0:128, :], dq[128:256, :]).astype(BF)
                dkp = dot_tn(ds, both(qkv[0, rows, lanes]))
                dvp = dot_tn(pr, go)
                seen = 0 if b == 0 else min(4, b + 1) * 128
                if seen > lo:
                    dk_acc[lo:seen, :] += dkp[0 : seen - lo, :]
                    dv_acc[lo:seen, :] += dvp[0 : seen - lo, :]
                if hi > seen:
                    dk_acc[seen:hi, :] = dkp[seen - lo :, :]
                    dv_acc[seen:hi, :] = dvp[seen - lo :, :]
            dqkv[1, :, lanes] = dk_acc[...].astype(BF)
            dqkv[2, :, lanes] = dv_acc[...].astype(BF)

            @pl.when(m < 2)
            def _():
                pltpu.make_async_copy(p_ref.at[p + 2], prob.at[side], psem.at[side]).start()

            for lag, f in stages:
                t = base + p - lag
                pl.when(t < entered)(functools.partial(f, t))
        return 0

    lax.fori_loop(0, 3, pairs, 0)
    for i in range(6):
        due.pop(state[0], None)
        state[0] += 1
    xload(10).wait()
    for part in range(3):
        grad_tile(lambda part_: xbuf[2, :, part_], lambda: dqkv[part])
        if part != 1:
            sums(part // 2, dqkv[part])
    def vcopy(d):
        p, dev = peer(d)
        return remote(vecs.at[p], vin.at[d], vs.at[d], vr.at[d], dev)

    def vstart(d, _):
        vcopy(d).start()
        return 0

    lax.fori_loop(1, 32, vstart, 0)
    vin[0] = vecs[me]

    for part in range(3):
        wload(11 + part).wait()
        through(lambda: dqkv[part], (11 + part) % 3, False)
        tick()
    out = pltpu.make_async_copy(acc, dtok_ref, lsem.at[0])
    out.start()

    tick()
    factor_stage(4)

    def lwait(d, _):
        lcopy(d, lax.rem(me + 32 - d, 32)).wait()
        return 0

    lax.fori_loop(1, 32, lwait, 0)

    def product(a, b):
        lv = lefts[:, a].astype(F32).reshape(256, 128).astype(BF)
        rv = every[:, :, :, :, b, :, half].astype(F32).reshape(256, 384).astype(BF)
        return dot_tn(lv, rv).astype(BF)

    for a in range(2):
        r = product(a, 1)
        piece[20 + 2 * a] = r[0:R, :]
        piece[21 + 2 * a] = r[64 : 64 + R, :]
    tick()

    def up_tiles(j, _):
        piece[16 + j] = product(2, 2 + j)[0:R, :]
        return 0

    lax.fori_loop(0, 4, up_tiles, 0)
    tick()
    piece[15] = product(2, 6)[64 : 64 + R, :]
    piece[14] = product(3, 7)[0:R, :]
    piece[24] = product(3, 0)[64 : 64 + R, :]
    while due and max(due) - state[0] >= LATE:
        tick()
    def vwait(d, _):
        vcopy(d).wait()
        return 0

    lax.fori_loop(1, 32, vwait, 0)
    vsum[...] = jnp.sum(vin[...], axis=0)
    vout_ref[me] = vsum[...]

    def wcopy(d, row):
        return remote(vsum, vout_ref.at[row], ws.at[d], wr.at[d], peer(d)[1])

    def wstart(d, _):
        wcopy(d, me).start()
        return 0

    lax.fori_loop(1, 32, wstart, 0)
    while due:
        tick()

    def back(d):
        p = col_peer(c, d)
        return remote(spread.at[pl.ds(4 * p, 4)], own_ref.at[:, c // 2, :, half], xs.at[d - 1], xr.at[d - 1], (z, p))

    own = pltpu.make_async_copy(spread.at[pl.ds(4 * c, 4)], own_ref.at[:, c // 2, :, half], lsem.at[1])
    for d in (1, 2, 3, 4, 5, 6, 7, 0):
        for i in range(4):
            s = 4 * col_peer(c, d) + i
            v = piece[src_ref[s]]
            spread[s] = jnp.where(fill_ref[s] > 0, v, jnp.zeros_like(v))
        if d:
            back(d).start()
        else:
            own.start()

    def wwait(d, _):
        wcopy(d, me).wait_send()
        wcopy(d, lax.rem(me + 32 - d, 32)).wait_recv()
        return 0

    lax.fori_loop(1, 32, wwait, 0)
    for n in range(2):
        for number in range(4):
            for cpy in factor_copies(n, number):
                cpy.wait_send()
    def drain(t, _):
        for cpy in [core(t)] + first(t) + second(t) + zcopies(t):
            cpy.wait_send()
        return 0

    lax.fori_loop(0, T, drain, 0)
    out.wait()
    own.wait()
    for d in range(1, 8):
        back(d).wait()


def backward_fused(lengths, source, filled, fac, dcls, packed, right, vg, vectors, w, a1, tokens, qkv, prob, o, n1, h1, act, slope, n2, dkv):
    T = len(RS_TILES)
    dma = lambda *n: pltpu.SemaphoreType.DMA(n)
    V = pl.BlockSpec(memory_space=pltpu.VMEM)
    S = pl.BlockSpec(memory_space=pltpu.SMEM)
    ANY = pl.BlockSpec(memory_space=pl.ANY)
    vm = pltpu.VMEM
    scratch = [
        vm((T, 4, 2, 2, R, D), BF), vm((T, 4, 2, 2, R, H), BF), vm((T, 4, 2, R, H), BF), vm((T, 4, R, H), BF), vm((T, 3, R, H), BF),
        vm((4, 2, 2, 2, 8, 8, D), BF), vm((32, 4, 8, 128), BF), vm((25, R, H), BF), vm((32, R, H), BF),
        vm((32, 1, D), F32), vm((32, 1, D), F32), vm((1, D), F32),
        vm((3, D, D), BF), vm((4, 512, D), BF), vm((512, D), BF), vm((3, 512, D), BF), vm((2, 4, 256, 384), BF), vm((3, 512, D), BF),
        vm((512, D), F32), vm((512, D), F32), vm((512, D), BF), vm((512, D), BF), vm((512, 128), F32), vm((512, 128), F32),
    ]
    scratch += [dma(T), dma(T), dma(T, 2), dma(T, 2), dma(T, 2), dma(T, 2), dma(T, 3), dma(T, 3), dma(7), dma(7)] + [dma(32) for _ in range(4)]
    scratch += [dma(2, 4), dma(2, 4), dma(2, 3), dma(2, 3), dma(32), dma(32), dma(3), dma(4), dma(2), dma(4)]
    return pl.pallas_call(
        functools.partial(backward_kernel),
        out_shape=(jax.ShapeDtypeStruct((4, 4, R, D), BF), jax.ShapeDtypeStruct((32, 1, D), F32), jax.ShapeDtypeStruct((512, D), F32)),
        in_specs=[S, S, S] + [V] * 6 + [ANY] * 12,
        out_specs=(V, V, ANY),
        scratch_shapes=scratch,
        compiler_params=pltpu.CompilerParams(collective_id=1, has_side_effects=True, vmem_limit_bytes=BIG),
    )(lengths.reshape(-1), source, filled, fac, dcls, packed, right, vg, vectors, w.reshape(-1, D, D), a1, tokens, qkv, prob, o, n1, h1, act, slope, n2, dkv)

def adam_fast(weights, first_moment, second_moment, grad_values, step_rate):
    first_new = first_decay * first_moment + (1.0 - first_decay) * grad_values
    second_new = second_decay * second_moment + (1.0 - second_decay) * grad_values * grad_values
    root = jnp.sqrt(second_new * (1.0 / (1.0 - second_decay**STEP))) + adam_eps
    step = (first_new * (1.0 / (1.0 - first_decay**STEP))) / root + weight_decay * weights
    return (weights - step_rate * step, first_new, second_new)


def adam_kernel(
    rate, own_ref, w_ref, m_ref, v_ref, sums_ref, vec_ref, vm_ref, vv_ref,
    g_out, w_out, m_out, v_out, vg_out, vec_out, vm_out, vv_out, bias_out,
):
    grad = own_ref[...].astype(F32)
    g_out[...] = grad
    w_out[...], m_out[...], v_out[...] = adam_fast(w_ref[...], m_ref[...], v_ref[...], grad, rate)

    @pl.when(pl.program_id(0) == 0)
    def _():
        count = vec_ref.shape[0]

        def row(r, _):
            vg_out[pl.ds(r, 1), :] = sums_ref[r]
            return 0

        lax.fori_loop(0, count, row, 0)
        bias_out[...] = sums_ref[12 * (LAYERS - 1) + 2, 0]
        vec_out[...], vm_out[...], vv_out[...] = adam_fast(vec_ref[...], vm_ref[...], vv_ref[...], vg_out[...], vector_rate)


def adam_all(own, store, first, second, sums, vectors, vector_first, vector_second, steps=2):
    rows = D // steps
    rate = store_rate_factor / math.sqrt(vectors.shape[1])
    flat = lambda v: v.reshape(D, D)
    tall = pl.BlockSpec((rows, D), lambda i: (i, 0))
    count = vectors.shape[0]
    whole = pl.BlockSpec((count, D), lambda i: (0, 0))
    f = lambda *s: jax.ShapeDtypeStruct(s, F32)
    out = pl.pallas_call(
        functools.partial(adam_kernel, rate),
        grid=(steps,),
        out_shape=(f(D, D),) * 4 + (f(count, D),) * 4 + (f(D),),
        in_specs=[tall] * 4 + [pl.BlockSpec(sums.shape, lambda i: (0, 0, 0))] + [whole] * 3,
        out_specs=(tall,) * 4 + (whole,) * 4 + (pl.BlockSpec((D,), lambda i: (0,)),),
    )(flat(own), flat(store), flat(first), flat(second), sums, vectors, vector_first, vector_second)
    return tuple(v.reshape(store.shape) for v in out[:4]) + out[4:8] + (out[8],)


def linear_map_apply(left_side, right_side):
    return jnp.dot(left_side, right_side, preferred_element_type=jnp.float32)


def layer_norm(values, gain_values, shift_values):
    center = values - jnp.mean(values, axis=-1, keepdims=True)
    spread = jnp.mean(center * center, axis=-1, keepdims=True)
    factor = lax.rsqrt(spread + norm_eps)
    normed = center * factor
    return (normed * gain_values + shift_values, normed, factor)


def norm_back(grad_in, normed, factor, gain_values):
    scaled = grad_in * gain_values
    input_grad = factor * (
        scaled
        - jnp.mean(scaled, axis=-1, keepdims=True)
        - normed * jnp.mean(scaled * normed, axis=-1, keepdims=True)
    )
    return (input_grad, jnp.sum(grad_in * normed, axis=0), jnp.sum(grad_in, axis=0))


def gelu_exact(values):
    return 0.5 * values * (1.0 + lax.erf(values * root_half))


def gelu_slope(values):
    return (
        0.5 * (1.0 + lax.erf(values * root_half))
        + values * jnp.exp(-0.5 * values * values) * slope_norm
    )


def layer_weights(weight_tiles, base):
    joint_weight = jnp.concatenate(
        [weight_tiles[base], weight_tiles[base + 1], weight_tiles[base + 2]], axis=1
    )
    up_weight = jnp.concatenate([weight_tiles[base + 4 + number] for number in range(4)], axis=1)
    down_weight = jnp.concatenate([weight_tiles[base + 8 + number] for number in range(4)], axis=0)
    return (joint_weight, weight_tiles[base + 3], up_weight, down_weight)


def split_heads(joint_row, head_count):
    seq_len = joint_row.shape[0]
    model_width = joint_row.shape[1] // 3
    shaped = joint_row.reshape(seq_len, 3, head_count, model_width // head_count)
    return (shaped[:, 0], shaped[:, 1], shaped[:, 2])


def masked_scores(queries, keys_here, seg_row):
    score_scale = 1.0 / math.sqrt(queries.shape[-1])
    raw_scores = jnp.einsum("qhd,khd->hqk", queries, keys_here, preferred_element_type=jnp.float32)
    same_segment = seg_row[:, None] == seg_row[None, :]
    return (jnp.where(same_segment[None], raw_scores * score_scale, -1e30), score_scale)


def attend_forward(joint_row, seg_row, head_count):
    queries, keys_here, values_here = split_heads(joint_row, head_count)
    scores, score_scale = masked_scores(queries, keys_here, seg_row)
    row_peak = jnp.max(scores, axis=-1, keepdims=True)
    weights = jnp.exp(scores - row_peak)
    exp_total = jnp.sum(weights, axis=-1, keepdims=True)
    row_probabilities = (weights / exp_total).astype(jnp.bfloat16)
    mixed_heads = jnp.einsum(
        "hqk,khd->qhd", row_probabilities, values_here, preferred_element_type=jnp.float32
    )
    return (
        mixed_heads.reshape(mixed_heads.shape[0], -1),
        row_peak[..., 0] + jnp.log(exp_total[..., 0]),
    )


def attend_backward(joint_row, seg_row, lse_row, grad_row, head_count):
    queries, keys_here, values_here = split_heads(joint_row, head_count)
    seq_len = joint_row.shape[0]
    grad_heads = grad_row.reshape(seq_len, head_count, -1)
    scores, score_scale = masked_scores(queries, keys_here, seg_row)
    row_probabilities = jnp.exp(scores - lse_row[..., None])
    prob_grads = jnp.einsum(
        "qhd,khd->hqk", grad_heads, values_here, preferred_element_type=jnp.float32
    )
    inner_sum = jnp.sum(row_probabilities * prob_grads, axis=-1, keepdims=True)
    score_grads = (row_probabilities * (prob_grads - inner_sum) * score_scale).astype(jnp.bfloat16)
    query_grad = jnp.einsum(
        "hqk,khd->qhd", score_grads, keys_here, preferred_element_type=jnp.float32
    )
    key_grad = jnp.einsum("hqk,qhd->khd", score_grads, queries, preferred_element_type=jnp.float32)
    value_grad = jnp.einsum(
        "hqk,qhd->khd",
        row_probabilities.astype(jnp.bfloat16),
        grad_heads,
        preferred_element_type=jnp.float32,
    )
    return jnp.concatenate(
        [
            query_grad.reshape(seq_len, -1),
            key_grad.reshape(seq_len, -1),
            value_grad.reshape(seq_len, -1),
        ],
        axis=1,
    )


def layer_forward(inputs, segment, weight_tiles, vectors, base, head_count):
    joint_weight, out_weight, up_weight, down_weight = layer_weights(weight_tiles, base)
    model_width = inputs.shape[1]
    rows_here = segment.shape[0]
    inputs_low = inputs.astype(jnp.bfloat16)
    joint_bias = jnp.concatenate(
        [vectors[base], jnp.zeros((model_width,), jnp.float32), vectors[base + 1]]
    )
    joint_out = (linear_map_apply(inputs_low, joint_weight) + joint_bias).astype(jnp.bfloat16)
    joint_rows = joint_out.reshape(rows_here, -1, 3 * model_width)

    def forward_row(row_items):
        return attend_forward(row_items[0], row_items[1], head_count)

    mixed, log_total = lax.map(forward_row, (joint_rows, segment))
    mixed_low = mixed.reshape(-1, model_width).astype(jnp.bfloat16)
    branch = linear_map_apply(mixed_low, out_weight) + vectors[base + 2]
    hidden, normed_one, factor_one = layer_norm(
        inputs + branch, vectors[base + 3], vectors[base + 4]
    )
    hidden_low = hidden.astype(jnp.bfloat16)
    pre_gelu = linear_map_apply(hidden_low, up_weight) + vectors[base + 5 : base + 9].reshape(-1)
    active = gelu_exact(pre_gelu).astype(jnp.bfloat16)
    output = linear_map_apply(active, down_weight) + vectors[base + 9]
    result, normed_two, factor_two = layer_norm(
        hidden + output, vectors[base + 10], vectors[base + 11]
    )
    kept_values = (
        inputs_low,
        joint_rows,
        log_total,
        mixed_low,
        normed_one,
        factor_one,
        hidden_low,
        pre_gelu,
        active,
        normed_two,
        factor_two,
    )
    return (result, kept_values)


def layer_backward(grad_out, kept_values, segment, weight_tiles, vectors, base, head_count):
    joint_weight, out_weight, up_weight, down_weight = layer_weights(weight_tiles, base)
    (
        inputs_low,
        joint_rows,
        log_total,
        mixed_low,
        normed_one,
        factor_one,
        hidden_low,
        pre_gelu,
        active,
        normed_two,
        factor_two,
    ) = kept_values
    model_width = inputs_low.shape[1]
    grad_res2, gain_two, shift_two = norm_back(grad_out, normed_two, factor_two, vectors[base + 10])
    grad_output = grad_res2.astype(jnp.bfloat16)
    down_grad = jnp.einsum("tf,td->fd", active, grad_output, preferred_element_type=jnp.float32)
    down_bias = jnp.sum(grad_output.astype(jnp.float32), axis=0)
    grad_active = jnp.einsum(
        "td,fd->tf", grad_output, down_weight, preferred_element_type=jnp.float32
    )
    grad_pre = (grad_active * gelu_slope(pre_gelu)).astype(jnp.bfloat16)
    up_grad = jnp.einsum("td,tf->df", hidden_low, grad_pre, preferred_element_type=jnp.float32)
    up_bias = jnp.sum(grad_pre.astype(jnp.float32), axis=0)
    grad_hidden = (
        jnp.einsum("tf,df->td", grad_pre, up_weight, preferred_element_type=jnp.float32) + grad_res2
    )
    grad_res1, gain_one, shift_one = norm_back(
        grad_hidden, normed_one, factor_one, vectors[base + 3]
    )
    grad_branch = grad_res1.astype(jnp.bfloat16)
    out_grad = jnp.einsum("tc,td->cd", mixed_low, grad_branch, preferred_element_type=jnp.float32)
    out_bias = jnp.sum(grad_branch.astype(jnp.float32), axis=0)
    grad_mixed = jnp.einsum(
        "td,cd->tc", grad_branch, out_weight, preferred_element_type=jnp.float32
    ).astype(jnp.bfloat16)

    def backward_row(row_items):
        return attend_backward(row_items[0], row_items[1], row_items[2], row_items[3], head_count)

    grad_joint = lax.map(
        backward_row,
        (joint_rows, segment, log_total, grad_mixed.reshape(joint_rows.shape[0], -1, model_width)),
    )
    grad_joint = grad_joint.reshape(-1, 3 * model_width).astype(jnp.bfloat16)
    joint_grad = jnp.einsum("tc,te->ce", inputs_low, grad_joint, preferred_element_type=jnp.float32)
    joint_sums = jnp.sum(grad_joint.astype(jnp.float32), axis=0)
    grad_inputs = (
        jnp.einsum("te,ce->tc", grad_joint, joint_weight, preferred_element_type=jnp.float32)
        + grad_res1
    )
    tile_list = [
        joint_grad[:, :model_width],
        joint_grad[:, model_width : 2 * model_width],
        joint_grad[:, 2 * model_width :],
        out_grad,
    ]
    tile_list = tile_list + [
        up_grad[:, number * model_width : (number + 1) * model_width] for number in range(4)
    ]
    tile_list = tile_list + [
        down_grad[number * model_width : (number + 1) * model_width] for number in range(4)
    ]
    vector_list = [
        joint_sums[:model_width],
        joint_sums[2 * model_width :],
        out_bias,
        gain_one,
        shift_one,
    ]
    vector_list = vector_list + [
        up_bias[number * model_width : (number + 1) * model_width] for number in range(4)
    ]
    vector_list = vector_list + [down_bias, gain_two, shift_two]
    return (grad_inputs, tile_list, vector_list)


def adam_step(weights, first_moment, second_moment, grad_values, step_rate):
    first_new = first_decay * first_moment + (1.0 - first_decay) * grad_values
    second_new = second_decay * second_moment + (1.0 - second_decay) * grad_values * grad_values
    first_hat = first_new / (1.0 - first_decay**STEP)
    second_hat = second_new / (1.0 - second_decay**STEP)
    new_weights = weights - step_rate * (
        first_hat / (jnp.sqrt(second_hat) + adam_eps) + weight_decay * weights
    )
    return (new_weights, first_new, second_new)


def pick_rows(row_values, row_starts):
    return row_values[row_starts]


def local_any(
    tokens,
    lengths,
    pair_index,
    tile_slot,
    master_store,
    first_moment_store,
    second_moment_store,
    vectors,
    vector_first,
    vector_second,
):
    model_width = tokens.shape[1]
    rows_here = lengths.shape[0]
    sent_count = lengths.shape[1]
    seq_len = tokens.shape[0] // rows_here
    head_count = HEADS
    tile_count = tile_slot.shape[0]
    row_count = lax.axis_size("row")
    col_count = lax.axis_size("col")
    slot_count = master_store.shape[0] * col_count
    gathered_rows = lax.all_gather(master_store.astype(jnp.bfloat16), "row", axis=1, tiled=True)
    gathered = lax.all_gather(gathered_rows, "col", axis=0, tiled=True)
    weight_tiles = jnp.take(gathered, tile_slot, axis=0)
    starts = jnp.cumsum(lengths, axis=1) - lengths
    places = jnp.arange(seq_len, dtype=jnp.int32)
    segment = jnp.sum((places[None, :, None] >= starts[:, None, :]).astype(jnp.int32), axis=2) - 1
    hidden_state = tokens.astype(jnp.float32)
    kept_layers = []
    for layer_number in range(LAYERS):
        hidden_state, kept_values = layer_forward(
            hidden_state, segment, weight_tiles, vectors, 12 * layer_number, head_count
        )
        kept_layers.append(kept_values)
    encoded = hidden_state.reshape(rows_here, seq_len, model_width)
    cls_rows = jax.vmap(pick_rows)(encoded, starts).reshape(-1, model_width)
    cls_low = cls_rows.astype(jnp.bfloat16)
    pool_weight = weight_tiles[tile_count - 1]
    pooled = jnp.tanh(linear_map_apply(cls_low, pool_weight) + vectors[tile_count - 1])
    inverse = lax.rsqrt(jnp.sum(pooled * pooled, axis=1, keepdims=True) + unit_eps)
    unit_low = (pooled * inverse).astype(jnp.bfloat16)
    row_emb = lax.all_gather(unit_low, "col", axis=0, tiled=True)
    col_emb = lax.all_gather(unit_low, "row", axis=0, tiled=True)
    sent_dev = unit_low.shape[0]
    row_pos = lax.axis_index("row")
    col_pos = lax.axis_index("col")
    row_indices = row_pos * (col_count * sent_dev) + jnp.arange(
        col_count * sent_dev, dtype=jnp.int32
    )
    column_indices = (
        (jnp.arange(row_count, dtype=jnp.int32)[:, None] * col_count + col_pos) * sent_dev
        + jnp.arange(sent_dev, dtype=jnp.int32)[None, :]
    ).reshape(-1)
    plain_closeness = jnp.einsum("rd,cd->rc", row_emb, col_emb, preferred_element_type=jnp.float32)
    angular_closeness = jnp.where(
        row_indices[:, None] == column_indices[None, :],
        -1e30,
        plain_closeness / logit_sharpness_divisor,
    )
    target = jnp.take(pair_index, row_indices)
    positive_pair_matches = column_indices[None, :] == target[:, None]
    positive_local = jnp.sum(jnp.where(positive_pair_matches, angular_closeness, 0.0), axis=1)
    peak_local = jnp.max(angular_closeness, axis=1)
    row_peak = lax.pmax(peak_local, "col")
    mass_total, positive = lax.psum(
        (jnp.sum(jnp.exp(angular_closeness - row_peak[:, None]), axis=1), positive_local), "col"
    )
    log_mass = row_peak + jnp.log(mass_total)
    sentence_total = row_count * col_count * sent_dev
    row_probabilities = jnp.exp(angular_closeness - log_mass[:, None])
    similarity_gradient = (
        (row_probabilities - positive_pair_matches.astype(jnp.float32))
        / sentence_total
        / logit_sharpness_divisor
    ).astype(jnp.bfloat16)
    rows_part = jnp.einsum(
        "rc,cd->rd", similarity_gradient, col_emb, preferred_element_type=jnp.float32
    )
    cols_part = jnp.einsum(
        "rc,rd->cd", similarity_gradient, row_emb, preferred_element_type=jnp.float32
    )
    unit_sensitivity = lax.psum_scatter(
        rows_part.astype(jnp.bfloat16), "col", scatter_dimension=0, tiled=True
    ).astype(jnp.float32) + lax.psum_scatter(
        cols_part.astype(jnp.bfloat16), "row", scatter_dimension=0, tiled=True
    ).astype(
        jnp.float32
    )
    own_loss = jnp.sum(lax.dynamic_slice_in_dim(log_mass - positive, col_pos * sent_dev, sent_dev))
    dot_unit = jnp.sum(pooled * unit_sensitivity, axis=1, keepdims=True)
    grad_pooled = inverse * unit_sensitivity - pooled * inverse * inverse * inverse * dot_unit
    grad_pre = (grad_pooled * (1.0 - pooled * pooled)).astype(jnp.bfloat16)
    pool_grad = jnp.einsum("sd,se->de", cls_low, grad_pre, preferred_element_type=jnp.float32)
    pool_bias = jnp.sum(grad_pre.astype(jnp.float32), axis=0)
    grad_cls = jnp.einsum("se,de->sd", grad_pre, pool_weight, preferred_element_type=jnp.float32)
    one_hot = (places[None, None, :] == starts[:, :, None]).astype(jnp.float32)
    grad_state = jnp.einsum(
        "pek,pex->pkx",
        one_hot,
        grad_cls.reshape(rows_here, sent_count, model_width),
        precision=lax.Precision.HIGHEST,
    ).reshape(-1, model_width)
    tile_grads = []
    vector_grads = []
    for layer_number in reversed(range(LAYERS)):
        grad_state, tile_list, vector_list = layer_backward(
            grad_state,
            kept_layers[layer_number],
            segment,
            weight_tiles,
            vectors,
            12 * layer_number,
            head_count,
        )
        tile_grads = tile_list + tile_grads
        vector_grads = vector_list + vector_grads
    grad_stack = jnp.stack(tile_grads + [pool_grad])
    vector_stack = jnp.stack(vector_grads + [pool_bias])
    slot_indices = jnp.arange(slot_count, dtype=jnp.int32)
    matches = tile_slot[None, :] == slot_indices[:, None]
    filled = jnp.any(matches, axis=1)
    source_tile = jnp.sum(
        jnp.where(matches, jnp.arange(tile_count, dtype=jnp.int32)[None, :], 0), axis=1
    )
    whole_slots = lax.psum_scatter(
        jnp.where(filled[:, None, None], jnp.take(grad_stack, source_tile, axis=0), 0.0).astype(
            jnp.bfloat16
        ),
        "col",
        scatter_dimension=0,
        tiled=True,
    )
    owned_grad = lax.psum_scatter(whole_slots, "row", scatter_dimension=1, tiled=True).astype(
        jnp.float32
    )
    vector_total, loss_total = lax.psum((vector_stack, own_loss), ("row", "col"))
    mean_loss = loss_total / sentence_total
    new_store, new_store_first, new_store_second = adam_step(
        master_store,
        first_moment_store,
        second_moment_store,
        owned_grad,
        store_rate_factor / math.sqrt(model_width),
    )
    new_vectors, new_vector_first, new_vector_second = adam_step(
        vectors, vector_first, vector_second, vector_total, vector_rate
    )
    out_bias_grad = vector_total[12 * (LAYERS - 1) + 2]
    return (
        grad_state,
        mean_loss,
        owned_grad,
        new_store,
        new_store_first,
        new_store_second,
        vector_total,
        new_vectors,
        new_vector_first,
        new_vector_second,
        out_bias_grad,
    )


def local_here(
    tokens,
    lengths,
    pair_index,
    tile_slot,
    master_store,
    first_moment_store,
    second_moment_store,
    vectors,
    vector_first,
    vector_second,
):
    tile_count = tile_slot.shape[0]
    slot_count = master_store.shape[0] * lax.axis_size("col")
    slot_indices = jnp.arange(slot_count, dtype=jnp.int32)
    place_of = [PIECE_ORDER.index(number) for number in range(tile_count)]
    matches = tile_slot[None, :] == slot_indices[:, None]
    filled = jnp.sum(matches.astype(jnp.int32), axis=1)
    source_tile = jnp.sum(jnp.where(matches, jnp.array(place_of, jnp.int32)[None, :], 0), axis=1)
    (
        weights, joint, prob, mixed, normed_one, hidden_low, active, slope, normed_two, factors, state_low,
        keys_grad, cls_grad, packed_left, row_right, head_vectors, loss,
    ) = forward_fused(tile_slot, master_store, tokens, lengths, vectors, pair_index)
    owned_low, vector_sums, grad_state = backward_fused(
        lengths, source_tile, filled, factors, cls_grad, packed_left, row_right, head_vectors, vectors, weights, state_low, tokens,
        joint, prob, mixed, normed_one, hidden_low, active, slope, normed_two, keys_grad,
    )
    (
        owned_grad, new_store, new_store_first, new_store_second,
        vector_total, new_vectors, new_vector_first, new_vector_second, out_bias_grad,
    ) = adam_all(
        owned_low, master_store, first_moment_store, second_moment_store, vector_sums, vectors, vector_first, vector_second
    )
    return (
        grad_state,
        loss[0, 0],
        owned_grad,
        new_store,
        new_store_first,
        new_store_second,
        vector_total,
        new_vectors,
        new_vector_first,
        new_vector_second,
        out_bias_grad,
    )


def solution(mesh):
    placed = (
        P(("row", "col"), None),
        P(("row", "col"), None),
        P(),
        P(),
        P("col", "row", None),
        P("col", "row", None),
        P("col", "row", None),
        P(),
        P(),
        P(),
    )
    fits = (mesh.shape["row"], mesh.shape["col"]) == (4, 8)
    return jax.shard_map(
        local_here if fits else local_any,
        mesh=mesh,
        in_specs=placed,
        out_specs=(
            P(("row", "col"), None),
            P(),
            P("col", "row", None),
            P("col", "row", None),
            P("col", "row", None),
            P("col", "row", None),
            P(),
            P(),
            P(),
            P(),
            P(),
        ),
        check_vma=False,
    )
```

```python
import functools
import math

import jax
import jax.numpy as jnp
from jax import lax
from jax.experimental import pallas as pl
from jax.experimental.pallas import tpu as pltpu
from jax.sharding import PartitionSpec as P

HEADS = 12
LAYERS = 2
STEP = 10


norm_eps = 1e-12
unit_eps = 1e-06
logit_sharpness_divisor = 0.05
first_decay = 0.9
second_decay = 0.999
adam_eps = 1e-08
weight_decay = 0.01
vector_rate = 0.5
store_rate_factor = 1.5
root_half = 1.0 / math.sqrt(2.0)
slope_norm = 1.0 / math.sqrt(2.0 * math.pi)


MESH = pl.DeviceIdType.MESH
D = 768
H = 384
R = 48
BIG = 67043328 - 256 * 1024


def remote(src, dst, s, r, dev):
    return pltpu.make_async_remote_copy(
        src_ref=src, dst_ref=dst, send_sem=s, recv_sem=r, device_id=dev, device_id_type=MESH
    )


def place():
    z = lax.axis_index("row")
    c = lax.axis_index("col")
    return z, c, c // 4, (c // 2) % 2, c % 2


def col_peer(c, d):
    return lax.rem(c + d, 8)


def row_peer(z, d):
    return lax.rem(z + d, 4)


def half_of(k):
    return pl.ds(pl.multiple_of(k * H, H), H)


BF = jnp.bfloat16
F32 = jnp.float32
KT = 14
ORDER = tuple(range(12)) + (13, 14, 12, 15) + tuple(range(16, 25))


def dot_nn(left, right):
    return jnp.dot(left, right, preferred_element_type=F32)


def dot_nt(left, right):
    return lax.dot_general(left, right, (((1,), (1,)), ((), ())), preferred_element_type=F32)


def dot_tn(left, right):
    return lax.dot_general(left, right, (((0,), (0,)), ((), ())), preferred_element_type=F32)


def colsum(v):
    return jnp.sum(v.astype(F32), axis=0, keepdims=True)


def norm_rows(v):
    center = v - jnp.mean(v, axis=1, keepdims=True)
    factor = lax.rsqrt(jnp.mean(center * center, axis=1, keepdims=True) + norm_eps)
    return center * factor, factor


def norm_rows_back(grad, normed, factor, gain):
    e = grad * gain
    return factor * (e - jnp.mean(e, axis=1, keepdims=True) - normed * jnp.mean(e * normed, axis=1, keepdims=True))


def window(block):
    return max(0, block - 1) * 128, min(4, block + 2) * 128


def forward_kernel(
    T, total, slot_ref, len_ref, pair_ref, master_ref, tok_ref, vec_ref, pairr_ref,
    w_out, qkv_out, p_out, o_out, n1_out, h1_out, act_out, slope_out, n2_out, s_out, low_out,
    src_ref, fill_ref, dkv_ref, dcls_ref, packed_ref, right_ref, vg_ref, loss_ref,
    w, stage, spread, qkv, prob, mixed, acc, normed, h1, h1b, u1b, act, slope, fac, kv, bias, uc, acts, slopes, unit, everyone,
    lsem, xs, xr, zs, zr, as_, ar, bs, br, cs, cr, osem, fsem, ss, sr,
):
    z, c, y, x, k = place()
    cx = c + 2 - 4 * x
    cy = c + 4 - 8 * y
    ck = c + 1 - 2 * k
    half = half_of(k)
    me = z * 8 + c
    bar = pltpu.get_barrier_semaphore()

    def peer(d):
        p = lax.rem(me + d, 32)
        return p, (p // 8, lax.rem(p, 8))

    def greet(d, _):
        pl.semaphore_signal(bar, inc=1, device_id=peer(d)[1], device_id_type=MESH)
        return 0

    lax.fori_loop(1, 32, greet, 0)

    def cast(s, _):
        stage[s] = master_ref[s].reshape(4, R, D).astype(BF)
        return 0

    lax.fori_loop(0, 4, cast, 0)
    pl.semaphore_wait(bar, 31)

    def spread_copy(d):
        p = col_peer(c, d)
        return remote(stage.at[:, p // 2, :, half_of(p % 2)], spread.at[pl.ds(4 * c, 4)], xs.at[d - 1], xr.at[d - 1], (z, p))

    for d in range(1, 8):
        spread_copy(d).start()
    own = pltpu.make_async_copy(stage.at[:, c // 2, :, half], spread.at[pl.ds(4 * c, 4)], lsem)
    own.start()
    starts = [0]
    for i in range(7):
        starts.append(starts[i] + len_ref[i])
    row_places = lax.broadcasted_iota(jnp.int32, (1, 512), 1)
    segr = jnp.zeros((1, 512), jnp.int32)
    for i in range(1, 8):
        segr = segr + (row_places >= starts[i]).astype(jnp.int32)
    for b in range(4):
        lo, hi = window(b)
        places = lax.broadcasted_iota(jnp.int32, (128, 1), 0) + 128 * b
        segc = jnp.zeros((128, 1), jnp.int32)
        for i in range(1, 8):
            segc = segc + (places >= starts[i]).astype(jnp.int32)
        bias[b, :, 0 : hi - lo] = jnp.where(segc == segr[:, lo:hi], 0.0, -1e30)

    def slot_source(s, _):
        found, hits = 0, 0
        for t in range(T):
            hit = slot_ref[t] == s
            found = found + jnp.where(hit, PIECE_ORDER.index(t), 0)
            hits = hits + jnp.where(hit, 1, 0)
        src_ref[s] = found
        fill_ref[s] = hits
        return 0

    lax.fori_loop(0, 32, slot_source, 0)
    own.wait()
    for d in range(1, 8):
        spread_copy(d).wait_recv()

    def zcopies(t):
        v = w.at[t, z, y, x, :, half]
        return [remote(v, v, zs.at[t, d - 1], zr.at[t, d - 1], (row_peer(z, d), c)) for d in (1, 2, 3)]

    def first(t):
        va, vb = w.at[t, 0:2, y, x, :, half], w.at[t, 2:4, y, x, :, half]
        return [remote(va, va, as_.at[t, 0], ar.at[t, 0], (z, cx)), remote(vb, vb, as_.at[t, 1], ar.at[t, 1], (z, cy))]

    def second(t):
        va, vb = w.at[t, 0:2, y, :, :, half], w.at[t, 2:4, :, x, :, half]
        return [remote(va, va, bs.at[t, 0], br.at[t, 0], (z, cy)), remote(vb, vb, bs.at[t, 1], br.at[t, 1], (z, cx))]

    def core(t):
        v = w.at[t, :, :, :, :, half]
        return remote(v, v, cs.at[t], cr.at[t], (z, ck))

    def outc(t):
        return pltpu.make_async_copy(w.at[t], w_out.at[t], osem.at[t])

    for t in range(T):
        w[t, z, y, x, :, half] = spread[slot_ref[ORDER[t]]]

    def issue(t, _):
        for cpy in zcopies(t):
            cpy.start()
        return 0

    lax.fori_loop(0, KT, issue, 0)

    def pair_first(t):
        v = w.at[t, z, y, x, :, half]
        return remote(v, v, as_.at[t, 0], ar.at[t, 0], (z, cx if t % 2 == 0 else cy))

    def pair_z(t):
        v = w.at[t, z, y, :, :, half] if t % 2 == 0 else w.at[t, z, :, x, :, half]
        return [remote(v, v, zs.at[t, d - 1], zr.at[t, d - 1], (row_peer(z, d), c)) for d in (1, 2, 3)]

    def pair_last(t):
        v = w.at[t, :, y, :, :, half] if t % 2 == 0 else w.at[t, :, :, x, :, half]
        return remote(v, v, bs.at[t, 0], br.at[t, 0], (z, cy if t % 2 == 0 else cx))

    for t in range(KT, T):
        pair_first(t).start()
    LAGS = (0, 1, 3, 4)

    def f0(t):
        if isinstance(t, int) and t >= KT:
            for cpy in pair_z(t):
                cpy.wait_recv()
            pair_last(t).start()
            return
        for cpy in zcopies(t):
            cpy.wait_recv()
        for cpy in first(t):
            cpy.start()

    def f1(t):
        if isinstance(t, int) and t >= KT:
            return
        for there, on in zip(first(t), second(t)):
            there.wait_recv()
            on.start()

    def f2(t):
        for cpy in [pair_last(t)] if isinstance(t, int) and t >= KT else second(t):
            cpy.wait_recv()
        core(t).start()

    def f3(t):
        core(t).wait_recv()
        outc(t).start()

    state = [0]

    def pump():
        i = state[0]
        if i < T + LAGS[3]:
            for f, lag in zip((f0, f1, f2, f3), LAGS):
                if 0 <= i - lag < T:
                    f(i - lag)
            state[0] = i + 1

    def pump_at(i):
        for f, lag in zip((f0, f1, f2, f3), LAGS):
            f(i - lag)

    def need(t):
        if isinstance(t, int):
            while state[0] <= t + LAGS[3]:
                pump()

    flushes = []
    counter = [0]

    def flush(src, dst):
        cpy = pltpu.make_async_copy(src, dst, fsem.at[counter[0]])
        counter[0] += 1
        cpy.start()
        flushes.append(cpy)

    def wcols(t, n):
        return w[t, :, :, :, :, pl.ds(pl.multiple_of(n * 256, 256), 256)].reshape(D, 256)

    def cols(n):
        return pl.ds(pl.multiple_of(n * 256, 256), 256)

    def norm(gain, shift, normed, out, low, number):
        def rows(m, _):
            rs = pl.ds(pl.multiple_of(m * 64, 64), 64)
            v = acc[rs, :]
            center = v - jnp.mean(v, axis=1, keepdims=True)
            factor = lax.rsqrt(jnp.mean(center * center, axis=1, keepdims=True) + norm_eps)
            nv = center * factor
            normed[rs, :] = nv
            fac[rs, number : number + 1] = factor
            o = nv * gain + shift
            out[rs, :] = o
            if low is not None:
                low[rs, :] = o.astype(BF)
            return 0

        lax.fori_loop(0, 8, rows, 0)

    for part in range(3):
        need(part)
        if part == 1:
            for t in range(KT, T):
                pair_first(t).wait_recv()
                for cpy in pair_z(t):
                    cpy.start()

        def project(n, _):
            r = dot_nn(tok_ref[...], wcols(part, n))
            if part != 1:
                r = r + vec_ref[part // 2 : part // 2 + 1, cols(n)]
            qkv[part, :, cols(n)] = r.astype(BF)
            return 0

        lax.fori_loop(0, 3, project, 0)
    flush(qkv, qkv_out)
    left = lax.broadcasted_iota(jnp.int32, (1, 128), 1) < 64

    keep_left = jnp.where(left, 0.125, 0.0).astype(BF)
    keep_right = jnp.where(left, 0.0, 0.125).astype(BF)

    def pair(p, side):
        lanes = pl.ds(pl.multiple_of(p * 128, 128), 128)
        for b in range(4):
            lo, hi = window(b)
            q = qkv[0, 128 * b : 128 * (b + 1), lanes]
            kk = qkv[1, lo:hi, lanes]
            vv = qkv[2, lo:hi, lanes]
            s = dot_nt(jnp.concatenate([q * keep_left, q * keep_right], axis=0), kk)
            mask = bias[b, :, 0 : hi - lo]
            s = s + jnp.concatenate([mask, mask], axis=0)
            ex = jnp.exp(s - jnp.max(s, axis=1, keepdims=True))
            pr = (ex * (1.0 / jnp.sum(ex, axis=1, keepdims=True))).astype(BF)
            prob[side, b, :, 0 : hi - lo] = pr
            big = dot_nn(pr, vv)
            mixed[128 * b : 128 * (b + 1), lanes] = jnp.where(left, big[0:128, :], big[128:256, :]).astype(BF)

    def pairs(p, _):
        side = lax.rem(p, 2)
        out = pltpu.make_async_copy(prob.at[side], p_out.at[p], fsem.at[20 + side])

        @pl.when(p > 1)
        def _():
            out.wait()

        pair(p, side)
        out.start()
        pump_at(base + p)
        return 0

    base = state[0]
    lax.fori_loop(0, 6, pairs, 0)
    state[0] = base + 6
    for side in range(2):
        pltpu.make_async_copy(prob.at[side], p_out.at[4 + side], fsem.at[20 + side]).wait()
    flush(mixed, o_out)
    need(3)

    def attend_out(n, _):
        acc[:, cols(n)] = (
            dot_nn(mixed[...], wcols(3, n)) + vec_ref[2:3, cols(n)] + tok_ref[:, cols(n)].astype(F32)
        )
        return 0

    lax.fori_loop(0, 3, attend_out, 0)
    norm(vec_ref[3:4, :], vec_ref[4:5, :], normed, h1, h1b, 0)
    flush(normed, n1_out)
    first_norm = flushes.pop()
    flush(h1b, h1_out)
    slope_copies = []
    for j in range(4):
        need(4 + j)

        def up(n, _):
            acc[:, cols(n)] = dot_nn(h1b[...], wcols(4 + j, n)) + vec_ref[5 + j : 6 + j, cols(n)]
            return 0

        lax.fori_loop(0, 3, up, 0)

        def gelu(m, _):
            rs = pl.ds(pl.multiple_of(m * 32, 32), 32)
            f = acc[rs, :]
            cdf = 0.5 * (1.0 + lax.erf(f * root_half))
            act[j, rs, :] = (f * cdf).astype(BF)
            slope[j % 2, rs, :] = (cdf + f * jnp.exp(-0.5 * f * f) * slope_norm).astype(BF)
            return 0

        if j >= 2:
            slope_copies[j - 2].wait()
        lax.fori_loop(0, 16, gelu, 0)
        flush(act.at[j], act_out.at[j])
        slope_copies.append(pltpu.make_async_copy(slope.at[j % 2], slope_out.at[j], fsem.at[22 + j % 2]))
        slope_copies[j].start()
    for j in range(4):
        need(8 + j)

        def down(n, _):
            r = dot_nn(act[j], wcols(8 + j, n))
            if j == 0:
                acc[:, cols(n)] = r + vec_ref[9:10, cols(n)] + h1[:, cols(n)]
            else:
                acc[:, cols(n)] += r
            return 0

        lax.fori_loop(0, 3, down, 0)
    first_norm.wait()
    norm(vec_ref[10:11, :], vec_ref[11:12, :], normed, h1, u1b, 1)
    flush(normed, n2_out)
    flush(fac, s_out)
    flush(u1b, low_out)
    for part in range(2):
        need(12 + part)

        def project_next(n, _):
            r = dot_nn(u1b[...], wcols(12 + part, n))
            if part == 1:
                r = r + vec_ref[13:14, cols(n)]
            kv[part, :, cols(n)] = r.astype(BF)
            return 0

        lax.fori_loop(0, 3, project_next, 0)
    def tile(t):
        return w[t].reshape(D, D)

    def vrow(r):
        return vec_ref[12 + r : 13 + r, :]

    def emit(r, v):
        vg_ref[r : r + 1, :] = v

    head_of = lax.broadcasted_iota(jnp.int32, (1, D), 1) // 64

    def by_head(v):
        v = v.astype(F32)
        return jnp.concatenate([jnp.where(head_of == h, v, 0.0) for h in range(12)], axis=0).astype(BF)

    def from_heads(big):
        out = jnp.where(head_of == 0, big[0:8, :], 0.0)
        for h in range(1, 12):
            out = out + jnp.where(head_of == h, big[8 * h : 8 * h + 8, :], 0.0)
        return out

    for s in range(8):
        uc[s : s + 1, :] = h1[pl.ds(starts[s], 1), :]
    low = uc[...].astype(BF)
    need(14)
    q = (dot_nn(low, tile(14)) + vrow(0)).astype(BF)
    qbig = by_head(q)
    same = segr == lax.broadcasted_iota(jnp.int32, (8, 512), 0)
    bias = jnp.where(same, 0.0, -1e30)
    sc = dot_nt(qbig, kv[0]) * 0.125 + jnp.concatenate([bias] * 12, axis=0)
    ex = jnp.exp(sc - jnp.max(sc, axis=1, keepdims=True))
    prob = ex * (1.0 / jnp.sum(ex, axis=1, keepdims=True))
    plow = prob.astype(BF)
    o = from_heads(dot_nn(plow, kv[1])).astype(BF)
    need(15)
    n1, s1 = norm_rows(uc[...] + dot_nn(o, tile(15)) + vrow(2))
    h1 = n1 * vrow(3) + vrow(4)
    h1b_cls = h1.astype(BF)
    need(19)

    def up_cls(j, _):
        f = dot_nn(h1b_cls, tile(16 + j)) + vec_ref[pl.ds(17 + j, 1), :]
        cdf = 0.5 * (1.0 + lax.erf(f * root_half))
        acts[j] = (f * cdf).astype(BF)
        slopes[j] = cdf + f * jnp.exp(-0.5 * f * f) * slope_norm
        return 0

    lax.fori_loop(0, 4, up_cls, 0)
    need(23)
    out = lax.fori_loop(0, 4, lambda j, total_: total_ + dot_nn(acts[j], tile(20 + j)), h1 + vrow(9))
    n2, s2 = norm_rows(out)
    zb = (n2 * vrow(10) + vrow(11)).astype(BF)
    need(24)
    pooled = jnp.tanh(dot_nn(zb, tile(24)) + vrow(12))
    inv = lax.rsqrt(jnp.sum(pooled * pooled, axis=1, keepdims=True) + unit_eps)
    unit[...] = (pooled * inv).astype(BF)
    everyone[me] = unit[...]

    def send(d, _):
        p, dev = peer(d)
        remote(unit, everyone.at[me], ss.at[d], sr.at[d], dev).start()
        return 0

    lax.fori_loop(1, 32, send, 0)
    packed_ref[...] = jnp.zeros((16, 4, 8, 128), BF)
    wholes = (acts[0], acts[1], acts[2], acts[3], h1b_cls, o, low, zb)
    for n, v in enumerate(wholes):
        v = v.astype(F32)
        off = 64 * (n % 2)
        for i in range(16):
            packed_ref[i, n // 2, :, off : off + R] = v[:, R * i : R * i + R].astype(BF)

    def arrive(d, _):
        q_ = lax.rem(me + 32 - d, 32)
        remote(unit, everyone.at[q_], ss.at[d], sr.at[d], peer(d)[1]).wait()
        return 0

    lax.fori_loop(1, 32, arrive, 0)
    everybody = everyone[...].astype(F32).reshape(256, D).astype(BF)
    sim = dot_nt(everybody, everybody) / logit_sharpness_divisor
    ri = lax.broadcasted_iota(jnp.int32, (256, 256), 0)
    ci = lax.broadcasted_iota(jnp.int32, (256, 256), 1)
    sim = jnp.where(ri == ci, -1e30, sim)
    peak = jnp.max(sim, axis=0, keepdims=True)
    lse = peak + jnp.log(jnp.sum(jnp.exp(sim - peak), axis=0, keepdims=True))
    pos = jnp.sum(jnp.where(ri == pairr_ref[...], sim, 0.0), axis=0, keepdims=True)
    loss_ref[...] = jnp.sum(lse - pos, axis=1, keepdims=True) / total
    own = dot_nt(unit[...], everybody) / logit_sharpness_divisor
    oi = lax.broadcasted_iota(jnp.int32, (8, 256), 0) + me * 8
    oj = lax.broadcasted_iota(jnp.int32, (8, 256), 1)
    own = jnp.where(oi == oj, -1e30, own)
    opeak = jnp.max(own, axis=1, keepdims=True)
    olse = opeak + jnp.log(jnp.sum(jnp.exp(own - opeak), axis=1, keepdims=True))
    sub = lax.broadcasted_iota(jnp.int32, (8, 1), 0)
    opair = jnp.zeros((8, 1), jnp.int32)
    for s in range(8):
        opair = jnp.where(sub == s, pair_ref[me * 8 + s], opair)
    g_rows = ((jnp.exp(own - olse) - (oj == opair).astype(F32)) / total / logit_sharpness_divisor).astype(BF)
    g_cols = ((jnp.exp(own - lse) - (pairr_ref[...] == oi).astype(F32)) / total / logit_sharpness_divisor).astype(BF)
    dunit = dot_nn(g_rows, everybody) + dot_nn(g_cols, everybody)
    dpooled = inv * dunit - pooled * (inv * inv * inv * jnp.sum(pooled * dunit, axis=1, keepdims=True))
    dpre = (dpooled * (1.0 - pooled * pooled)).astype(BF)
    right_ref[0] = dpre
    emit(12, colsum(dpre))
    dz = dot_nt(dpre, tile(24))
    emit(10, colsum(dz * n2))
    emit(11, colsum(dz))
    dr2 = norm_rows_back(dz, n2, s2, vrow(10))
    dy = dr2.astype(BF)
    right_ref[1] = dy
    emit(9, colsum(dy))

    def down_cls(j, dh):
        df = (dot_nt(dy, tile(20 + j)) * slopes[j]).astype(BF)
        right_ref[2 + j] = df
        vg_ref[pl.ds(5 + j, 1), :] = colsum(df)
        return dh + dot_nt(df, tile(16 + j))

    dh = lax.fori_loop(0, 4, down_cls, dr2)
    emit(3, colsum(dh * n1))
    emit(4, colsum(dh))
    dr1 = norm_rows_back(dh, n1, s1, vrow(3))
    da = dr1.astype(BF)
    right_ref[6] = da
    emit(2, colsum(da))
    dobig = by_head(dot_nt(da, tile(15)).astype(BF))
    dp = dot_nt(dobig, kv[1])
    ds = (prob * (dp - jnp.sum(prob * dp, axis=1, keepdims=True)) * 0.125).astype(BF)
    dq = from_heads(dot_nn(ds, kv[0])).astype(BF)
    right_ref[7] = dq
    emit(0, colsum(dq))
    dcls_ref[...] = dot_nt(dq, tile(14)) + dr1
    dkv_ref[0] = dot_tn(ds, qbig).astype(BF)
    dv = dot_tn(plow, dobig).astype(BF)
    dkv_ref[1] = dv
    emit(1, colsum(dv))
    for d in range(1, 8):
        spread_copy(d).wait_send()

    def drain(t, _):
        for cpy in zcopies(t) + first(t) + second(t) + [core(t)]:
            cpy.wait_send()
        outc(t).wait()
        return 0

    lax.fori_loop(0, KT, drain, 0)
    for t in range(KT, T):
        for cpy in pair_z(t) + [pair_first(t), pair_last(t), core(t)]:
            cpy.wait_send()
        outc(t).wait()
    for cpy in slope_copies[2:]:
        cpy.wait()
    for cpy in flushes:
        cpy.wait()


def forward_fused(slots, master, tokens, lengths, vectors, pair_index):
    T = slots.shape[0]
    total = pair_index.shape[0]
    dma = lambda *n: pltpu.SemaphoreType.DMA(n)
    V = pl.BlockSpec(memory_space=pltpu.VMEM)
    S = pl.BlockSpec(memory_space=pltpu.SMEM)
    ANY = pl.BlockSpec(memory_space=pl.ANY)
    shapes = [
        ((T, 4, 2, 2, R, D), BF), ((3, 512, D), BF), ((6, 4, 256, 384), BF), ((512, D), BF), ((512, D), F32), ((512, D), BF),
        ((4, 512, D), BF), ((4, 512, D), BF), ((512, D), F32), ((512, 2), F32), ((512, D), BF),
        ((32,), jnp.int32), ((32,), jnp.int32), ((2, 512, D), BF), ((8, D), F32), ((16, 4, 8, 128), BF), ((8, 8, D), BF), ((13, D), F32), ((1, 1), F32),
    ]
    vm = pltpu.VMEM
    scratch = [
        vm((T, 4, 2, 2, R, D), BF), vm((4, 4, R, D), BF), vm((32, R, H), BF), vm((3, 512, D), BF), vm((2, 4, 256, 384), BF), vm((512, D), BF),
        vm((512, D), F32), vm((512, D), F32), vm((512, D), F32), vm((512, D), BF), vm((512, D), BF), vm((4, 512, D), BF), vm((2, 512, D), BF),
        vm((512, 2), F32), vm((2, 512, D), BF), vm((4, 128, 384), F32), vm((8, D), F32), vm((4, 8, D), BF), vm((4, 8, D), F32), vm((8, D), BF), vm((32, 8, D), BF),
        dma(), dma(7), dma(7), dma(T, 3), dma(T, 3), dma(T, 2), dma(T, 2), dma(T, 2), dma(T, 2), dma(T), dma(T), dma(T), dma(24), dma(32), dma(32),
    ]
    return pl.pallas_call(
        functools.partial(forward_kernel, T, total),
        out_shape=tuple(jax.ShapeDtypeStruct(*s) for s in shapes),
        in_specs=[S, S, S] + [V] * 4,
        out_specs=(ANY,) * 11 + (S, S) + (V,) * 6,
        scratch_shapes=scratch,
        compiler_params=pltpu.CompilerParams(collective_id=0, has_side_effects=True, vmem_limit_bytes=BIG),
    )(slots, lengths.reshape(-1), pair_index, master, tokens, vectors, pair_index[None, :])

RS_TILES = (13, 14, 8, 4, 9, 5, 10, 6, 11, 7, 3, 0, 1, 2)
PIECE_ORDER = RS_TILES + (12,) + tuple(range(15, 25))
LATE = 5
FACTOR_MODES = ("xzyk", "yzxk")
FACTOR_TICKS = ((3, 8, 18), (3, 8, 18))
EARLY_LAGS = ((1, 3, 6, 11), (1, 4, 7, 11), (2, 4, 8, 11))
RS_LAGS = (2, 5, 8, 11)
W_SEQ = (12, 13, 8, 4, 9, 5, 10, 6, 11, 7, 3, 0, 1, 2)


def backward_kernel(
    len_ref, src_ref, fill_ref, fac_ref, dcls_ref, packed_ref, right_ref, vg_ref, vec_ref,
    w_ref, a1_ref, tok_ref, qkv_ref, p_ref, o_ref, n1_ref, h1_ref, act_ref, slope_ref, n2_ref, dkv_ref,
    own_ref, vout_ref, dtok_ref,
    g, rc, r1, r2, r3, every, lefts, piece, spread, vecs, vin, vsum,
    wbuf, xbuf, h1b, qkv, prob, dqkv, norm, acc, dy, df, dk_acc, dv_acc,
    cs, cr, as_, ar, bs, br, zs, zr, xs, xr, vs, vr, ws, wr, fs, fr, fz, fzr, ls, lr, wsem, xsem, psem, lsem,
):
    z, c, y, x, k = place()
    cx = c + 2 - 4 * x
    cy = c + 4 - 8 * y
    ck = c + 1 - 2 * k
    me = z * 8 + c
    half = half_of(k)
    other = half_of(1 - k)
    T = len(RS_TILES)
    starts = [0]
    for i in range(7):
        starts.append(starts[i] + len_ref[i])

    def wload(i):
        return pltpu.make_async_copy(w_ref.at[W_SEQ[i]], wbuf.at[i % 3], wsem.at[i % 3])

    x_seq = [a1_ref]
    for j in range(4):
        x_seq += [act_ref.at[j], slope_ref.at[j]]
    x_seq += [o_ref, tok_ref]

    def xload(i):
        return pltpu.make_async_copy(x_seq[i], xbuf.at[i % 4], xsem.at[i % 4])

    def pload(p):
        return pltpu.make_async_copy(p_ref.at[p], prob.at[p % 2], psem.at[p % 2])

    load_dkv = pltpu.make_async_copy(dkv_ref, dqkv.at[pl.ds(0, 2)], lsem.at[0])
    load_n2 = pltpu.make_async_copy(n2_ref, norm, lsem.at[1])
    load_n1 = pltpu.make_async_copy(n1_ref, norm, lsem.at[1])
    load_h1 = pltpu.make_async_copy(h1_ref, h1b, lsem.at[2])
    load_qkv = pltpu.make_async_copy(qkv_ref, qkv, lsem.at[3])
    load_dkv.start()
    xload(0).start()
    wload(0).start()
    wload(1).start()
    load_n2.start()
    for i in (1, 2, 3):
        xload(i).start()
    wload(2).start()
    load_h1.start()
    load_qkv.start()
    pload(0).start()
    pload(1).start()

    bar = pltpu.get_barrier_semaphore()

    def peer(d):
        p = lax.rem(me + d, 32)
        return p, (p // 8, lax.rem(p, 8))

    def greet(d, _):
        pl.semaphore_signal(bar, inc=1, device_id=peer(d)[1], device_id_type=MESH)
        return 0

    lax.fori_loop(1, 32, greet, 0)

    def region(n, have):
        zi = slice(None) if "z" in have else z
        yi = slice(None) if "y" in have else y
        xi = slice(None) if "x" in have else x
        ki = slice(None) if "k" in have else k
        return every.at[zi, yi, xi, ki, 4 * n : 4 * n + 4]

    def factor_copies(n, number):
        mode = FACTOR_MODES[n]
        v = region(n, mode[:number])
        axis = mode[number]
        if axis == "z":
            return [remote(v, v, fz.at[n, d - 1], fzr.at[n, d - 1], (row_peer(z, d), c)) for d in (1, 2, 3)]
        return [remote(v, v, fs.at[n, number], fr.at[n, number], (z, {"x": cx, "y": cy, "k": ck}[axis]))]

    def factor_step(n, number):
        if number:
            for cpy in factor_copies(n, number - 1):
                cpy.wait_recv()
        if number < 4:
            for cpy in factor_copies(n, number):
                cpy.start()

    def factor_stage(number):
        for n in range(2):
            factor_step(n, number)

    every[z, y, x, k] = right_ref[...]
    lefts[me] = packed_ref[me // 2]

    def lcopy(d, row):
        p, dev = peer(d)
        return remote(packed_ref.at[p // 2], lefts.at[row], ls.at[d], lr.at[d], dev)

    def lstart(d, _):
        lcopy(d, me).start()
        return 0

    pl.semaphore_wait(bar, 31)
    factor_stage(0)
    lax.fori_loop(1, 32, lstart, 0)

    def core(t):
        return remote(g.at[t, :, :, :, :, other], rc.at[t], cs.at[t], cr.at[t], (z, ck))

    def first(t):
        return [
            remote(g.at[t, 0:2, 1 - y, :, :, half], r1.at[t, 0:2], as_.at[t, 0], ar.at[t, 0], (z, cy)),
            remote(g.at[t, 2:4, :, 1 - x, :, half], r1.at[t, 2:4], as_.at[t, 1], ar.at[t, 1], (z, cx)),
        ]

    def second(t):
        return [
            remote(g.at[t, 0:2, y, 1 - x, :, half], r2.at[t, 0:2], bs.at[t, 0], br.at[t, 0], (z, cx)),
            remote(g.at[t, 2:4, 1 - y, x, :, half], r2.at[t, 2:4], bs.at[t, 1], br.at[t, 1], (z, cy)),
        ]

    def zcopies(t):
        return [
            remote(g.at[t, row_peer(z, d), y, x, :, half], r3.at[t, d - 1], zs.at[t, d - 1], zr.at[t, d - 1], (row_peer(z, d), c))
            for d in (1, 2, 3)
        ]

    def plus(a, b):
        return (a.astype(F32) + b.astype(F32)).astype(BF)

    def f1(t):
        core(t).wait_recv()
        for part in range(2):
            for zz in (2 * part, 2 * part + 1):
                g[t, zz, :, :, :, half] = plus(g[t, zz, :, :, :, half], rc[t, zz])
            first(t)[part].start()

    def f2(t):
        for part in range(2):
            first(t)[part].wait_recv()
            for zz in (2 * part, 2 * part + 1):
                if part == 0:
                    g[t, zz, y, :, :, half] = plus(g[t, zz, y, :, :, half], r1[t, zz])
                else:
                    g[t, zz, :, x, :, half] = plus(g[t, zz, :, x, :, half], r1[t, zz])
            second(t)[part].start()

    def f3(t):
        for part in range(2):
            second(t)[part].wait_recv()
        for zz in range(4):
            g[t, zz, y, x, :, half] = plus(g[t, zz, y, x, :, half], r2[t, zz])
        for cpy in zcopies(t):
            cpy.start()

    def f4(t):
        for cpy in zcopies(t):
            cpy.wait_recv()
        piece[t] = (
            g[t, z, y, x, :, half].astype(F32) + r3[t, 0].astype(F32) + r3[t, 1].astype(F32) + r3[t, 2].astype(F32)
        ).astype(BF)

    stages = tuple(zip(RS_LAGS, (f1, f2, f3, f4)))
    due = {}
    for n in range(2):
        for number in range(3):
            due.setdefault(FACTOR_TICKS[n][number], []).append(functools.partial(factor_step, n, number + 1))

    state = [0, 0]

    def enter():
        t, now = state[1], state[0]
        core(t).start()
        for lag, f in zip(EARLY_LAGS[t] if t < 3 else RS_LAGS, (f1, f2, f3, f4)):
            due.setdefault(now + lag, []).insert(0, functools.partial(f, t))
        state[1] = t + 1

    def tick():
        for f in due.pop(state[0], []):
            f()
        state[0] += 1

    def wide(b):
        return pl.ds(pl.multiple_of(b * 384, 384), 384)

    def cols(n):
        return pl.ds(pl.multiple_of(n * 256, 256), 256)

    def grad_tile(left, right):
        t = state[1]

        def rows(b, _):
            r = dot_tn(left(wide(b)), right()).astype(BF)
            g[t, pl.ds(2 * b, 2)] = r.reshape(2, 2, 2, R, D)
            return 0

        lax.fori_loop(0, 2, rows, 0)
        enter()
        tick()

    def through(grad, slot, fresh):
        def part(b, _):
            r = dot_nt(grad(), wbuf[slot, cols(b), :])
            if fresh:
                acc[:, cols(b)] = r
            else:
                acc[:, cols(b)] += r
            return 0

        lax.fori_loop(0, 3, part, 0)

    def sums(row, value):
        vecs[row] = jnp.sum(value.astype(F32), axis=0, keepdims=True)

    def fold(v):
        return jnp.sum(v.reshape(8, 8, D), axis=0)

    def norm_back(number, gain, rows_out, place_cls):
        def rows(m, carry):
            rs = pl.ds(pl.multiple_of(m * 64, 64), 64)
            dh = acc[rs, :]
            if place_cls:
                rid = lax.broadcasted_iota(jnp.int32, (64, 1), 0) + m * 64
                for s in range(8):
                    dh = dh + jnp.where(rid == starts[s], dcls_ref[s : s + 1, :], 0.0)
            nv = norm[rs, :]
            e = dh * gain
            dr = fac_ref[rs, number : number + 1] * (
                e - jnp.mean(e, axis=1, keepdims=True) - nv * jnp.mean(e * nv, axis=1, keepdims=True)
            )
            acc[rs, :] = dr
            low = dr.astype(BF)
            dy[rs, :] = low
            a, b, d = carry
            return a + fold(dh * nv), b + fold(dh), d + fold(low.astype(F32))

        zero = jnp.zeros((8, D), F32)
        out = lax.fori_loop(0, 8, rows, (zero, zero, zero))
        for row, v in zip(rows_out, out):
            vecs[row] = jnp.sum(v, axis=0, keepdims=True)

    for i in range(13):
        vecs[12 + i] = vg_ref[i : i + 1, :]
    for i in range(25, 32):
        vecs[i] = jnp.zeros((1, D), F32)

    load_dkv.wait()
    xload(0).wait()
    for part in range(2):
        grad_tile(lambda part_: xbuf[0, :, part_], lambda: dqkv[part])
    xload(4).start()
    for part in range(2):
        wload(part).wait()
        through(lambda: dqkv[part], part, part == 0)
        wload(part + 3).start()
    load_n2.wait()
    norm_back(1, vec_ref[10:11, :], (10, 11, 9), True)
    load_n1.start()
    load_h1.wait()
    for j in range(4):
        xload(1 + 2 * j).wait()
        grad_tile(lambda part_: xbuf[(1 + 2 * j) % 4, :, part_], lambda: dy[...])
        if 5 + 2 * j < 11:
            xload(5 + 2 * j).start()
        wload(2 + 2 * j).wait()
        xload(2 + 2 * j).wait()

        def pre(b, _):
            r = dot_nt(dy[...], wbuf[(2 + 2 * j) % 3, cols(b), :])
            df[:, cols(b)] = (r * xbuf[(2 + 2 * j) % 4, :, cols(b)].astype(F32)).astype(BF)
            return 0

        lax.fori_loop(0, 3, pre, 0)
        if 6 + 2 * j < 11:
            xload(6 + 2 * j).start()
        wload(5 + 2 * j).start()
        grad_tile(lambda part_: h1b[:, part_], lambda: df[...])
        sums(5 + j, df[...])
        wload(3 + 2 * j).wait()
        through(lambda: df[...], (3 + 2 * j) % 3, False)
        if 6 + 2 * j < 14:
            wload(6 + 2 * j).start()
    load_n1.wait()
    norm_back(0, vec_ref[3:4, :], (3, 4, 2), False)
    xload(9).wait()
    grad_tile(lambda part_: xbuf[1, :, part_], lambda: dy[...])
    wload(10).wait()

    def mixed_grad(b, _):
        df[:, cols(b)] = dot_nt(dy[...], wbuf[10 % 3, cols(b), :]).astype(BF)
        return 0

    lax.fori_loop(0, 3, mixed_grad, 0)
    wload(13).start()
    load_qkv.wait()
    left = lax.broadcasted_iota(jnp.int32, (1, 128), 1) < 64
    keep_left = jnp.where(left, 1.0, 0.0).astype(BF)
    keep_right = jnp.where(left, 0.0, 1.0).astype(BF)

    def both(v):
        return jnp.concatenate([v * keep_left, v * keep_right], axis=0)

    entered = state[1]
    base = state[0]

    def pairs(p, _):
        if True:
            side = lax.rem(p, 2)
            lanes = pl.ds(pl.multiple_of(p * 128, 128), 128)
            pltpu.make_async_copy(p_ref.at[p], prob.at[side], psem.at[side]).wait()
            for b in range(4):
                lo, hi = window(b)
                rows = pl.ds(128 * b, 128)
                go = both(df[rows, lanes])
                pr = prob[side, b, :, 0 : hi - lo]
                pf = pr.astype(F32)
                dp = dot_nt(go, qkv[2, lo:hi, lanes])
                ds = (pf * (dp - jnp.sum(pf * dp, axis=1, keepdims=True)) * 0.125).astype(BF)
                dq = dot_nn(ds, qkv[1, lo:hi, lanes])
                dqkv[0, rows, lanes] = jnp.where(left, dq[0:128, :], dq[128:256, :]).astype(BF)
                dkp = dot_tn(ds, both(qkv[0, rows, lanes]))
                dvp = dot_tn(pr, go)
                seen = 0 if b == 0 else min(4, b + 1) * 128
                if seen > lo:
                    dk_acc[lo:seen, :] += dkp[0 : seen - lo, :]
                    dv_acc[lo:seen, :] += dvp[0 : seen - lo, :]
                if hi > seen:
                    dk_acc[seen:hi, :] = dkp[seen - lo :, :]
                    dv_acc[seen:hi, :] = dvp[seen - lo :, :]
            dqkv[1, :, lanes] = dk_acc[...].astype(BF)
            dqkv[2, :, lanes] = dv_acc[...].astype(BF)

            @pl.when(p < 4)
            def _():
                pltpu.make_async_copy(p_ref.at[p + 2], prob.at[side], psem.at[side]).start()

            for lag, f in stages:
                t = base + p - lag
                pl.when(t < entered)(functools.partial(f, t))
        return 0

    lax.fori_loop(0, 6, pairs, 0)
    for i in range(6):
        due.pop(state[0], None)
        state[0] += 1
    xload(10).wait()
    for part in range(3):
        grad_tile(lambda part_: xbuf[2, :, part_], lambda: dqkv[part])
        if part != 1:
            sums(part // 2, dqkv[part])
    def vcopy(d):
        p, dev = peer(d)
        return remote(vecs.at[p], vin.at[d], vs.at[d], vr.at[d], dev)

    def vstart(d, _):
        vcopy(d).start()
        return 0

    lax.fori_loop(1, 32, vstart, 0)
    vin[0] = vecs[me]

    for part in range(3):
        wload(11 + part).wait()
        through(lambda: dqkv[part], (11 + part) % 3, False)
        tick()
    out = pltpu.make_async_copy(acc, dtok_ref, lsem.at[0])
    out.start()

    tick()
    factor_stage(4)

    def lwait(d, _):
        lcopy(d, lax.rem(me + 32 - d, 32)).wait()
        return 0

    lax.fori_loop(1, 32, lwait, 0)

    def product(a, b):
        lv = lefts[:, a].astype(F32).reshape(256, 128).astype(BF)
        rv = every[:, :, :, :, b, :, half].astype(F32).reshape(256, 384).astype(BF)
        return dot_tn(lv, rv).astype(BF)

    for a in range(2):
        r = product(a, 1)
        piece[20 + 2 * a] = r[0:R, :]
        piece[21 + 2 * a] = r[64 : 64 + R, :]
    tick()

    def up_tiles(j, _):
        piece[16 + j] = product(2, 2 + j)[0:R, :]
        return 0

    lax.fori_loop(0, 4, up_tiles, 0)
    tick()
    piece[15] = product(2, 6)[64 : 64 + R, :]
    piece[14] = product(3, 7)[0:R, :]
    piece[24] = product(3, 0)[64 : 64 + R, :]
    while due and max(due) - state[0] >= LATE:
        tick()
    def vwait(d, _):
        vcopy(d).wait()
        return 0

    lax.fori_loop(1, 32, vwait, 0)
    vsum[...] = jnp.sum(vin[...], axis=0)
    vout_ref[me] = vsum[...]

    def wcopy(d, row):
        return remote(vsum, vout_ref.at[row], ws.at[d], wr.at[d], peer(d)[1])

    def wstart(d, _):
        wcopy(d, me).start()
        return 0

    lax.fori_loop(1, 32, wstart, 0)
    while due:
        tick()

    def back(d):
        p = col_peer(c, d)
        return remote(spread.at[pl.ds(4 * p, 4)], own_ref.at[:, c // 2, :, half], xs.at[d - 1], xr.at[d - 1], (z, p))

    own = pltpu.make_async_copy(spread.at[pl.ds(4 * c, 4)], own_ref.at[:, c // 2, :, half], lsem.at[1])
    for d in (1, 2, 3, 4, 5, 6, 7, 0):
        for i in range(4):
            s = 4 * col_peer(c, d) + i
            v = piece[src_ref[s]]
            spread[s] = jnp.where(fill_ref[s] > 0, v, jnp.zeros_like(v))
        if d:
            back(d).start()
        else:
            own.start()

    def wwait(d, _):
        wcopy(d, me).wait_send()
        wcopy(d, lax.rem(me + 32 - d, 32)).wait_recv()
        return 0

    lax.fori_loop(1, 32, wwait, 0)
    for n in range(2):
        for number in range(4):
            for cpy in factor_copies(n, number):
                cpy.wait_send()
    def drain(t, _):
        for cpy in [core(t)] + first(t) + second(t) + zcopies(t):
            cpy.wait_send()
        return 0

    lax.fori_loop(0, T, drain, 0)
    out.wait()
    own.wait()
    for d in range(1, 8):
        back(d).wait()


def backward_fused(lengths, source, filled, fac, dcls, packed, right, vg, vectors, w, a1, tokens, qkv, prob, o, n1, h1, act, slope, n2, dkv):
    T = len(RS_TILES)
    dma = lambda *n: pltpu.SemaphoreType.DMA(n)
    V = pl.BlockSpec(memory_space=pltpu.VMEM)
    S = pl.BlockSpec(memory_space=pltpu.SMEM)
    ANY = pl.BlockSpec(memory_space=pl.ANY)
    vm = pltpu.VMEM
    scratch = [
        vm((T, 4, 2, 2, R, D), BF), vm((T, 4, 2, 2, R, H), BF), vm((T, 4, 2, R, H), BF), vm((T, 4, R, H), BF), vm((T, 3, R, H), BF),
        vm((4, 2, 2, 2, 8, 8, D), BF), vm((32, 4, 8, 128), BF), vm((25, R, H), BF), vm((32, R, H), BF),
        vm((32, 1, D), F32), vm((32, 1, D), F32), vm((1, D), F32),
        vm((3, D, D), BF), vm((4, 512, D), BF), vm((512, D), BF), vm((3, 512, D), BF), vm((2, 4, 256, 384), BF), vm((3, 512, D), BF),
        vm((512, D), F32), vm((512, D), F32), vm((512, D), BF), vm((512, D), BF), vm((512, 128), F32), vm((512, 128), F32),
    ]
    scratch += [dma(T), dma(T), dma(T, 2), dma(T, 2), dma(T, 2), dma(T, 2), dma(T, 3), dma(T, 3), dma(7), dma(7)] + [dma(32) for _ in range(4)]
    scratch += [dma(2, 4), dma(2, 4), dma(2, 3), dma(2, 3), dma(32), dma(32), dma(3), dma(4), dma(2), dma(4)]
    return pl.pallas_call(
        functools.partial(backward_kernel),
        out_shape=(jax.ShapeDtypeStruct((4, 4, R, D), BF), jax.ShapeDtypeStruct((32, 1, D), F32), jax.ShapeDtypeStruct((512, D), F32)),
        in_specs=[S, S, S] + [V] * 6 + [ANY] * 12,
        out_specs=(V, V, ANY),
        scratch_shapes=scratch,
        compiler_params=pltpu.CompilerParams(collective_id=1, has_side_effects=True, vmem_limit_bytes=BIG),
    )(lengths.reshape(-1), source, filled, fac, dcls, packed, right, vg, vectors, w.reshape(-1, D, D), a1, tokens, qkv, prob, o, n1, h1, act, slope, n2, dkv)

def adam_fast(weights, first_moment, second_moment, grad_values, step_rate):
    first_new = first_decay * first_moment + (1.0 - first_decay) * grad_values
    second_new = second_decay * second_moment + (1.0 - second_decay) * grad_values * grad_values
    root = jnp.sqrt(second_new * (1.0 / (1.0 - second_decay**STEP))) + adam_eps
    step = (first_new * (1.0 / (1.0 - first_decay**STEP))) / root + weight_decay * weights
    return (weights - step_rate * step, first_new, second_new)


def adam_kernel(
    rate, own_ref, w_ref, m_ref, v_ref, sums_ref, vec_ref, vm_ref, vv_ref,
    g_out, w_out, m_out, v_out, vg_out, vec_out, vm_out, vv_out, bias_out,
):
    grad = own_ref[...].astype(F32)
    g_out[...] = grad
    w_out[...], m_out[...], v_out[...] = adam_fast(w_ref[...], m_ref[...], v_ref[...], grad, rate)

    @pl.when(pl.program_id(0) == 0)
    def _():
        count = vec_ref.shape[0]

        def row(r, _):
            vg_out[pl.ds(r, 1), :] = sums_ref[r]
            return 0

        lax.fori_loop(0, count, row, 0)
        bias_out[...] = sums_ref[12 * (LAYERS - 1) + 2, 0]
        vec_out[...], vm_out[...], vv_out[...] = adam_fast(vec_ref[...], vm_ref[...], vv_ref[...], vg_out[...], vector_rate)


def adam_all(own, store, first, second, sums, vectors, vector_first, vector_second, steps=2):
    rows = D // steps
    rate = store_rate_factor / math.sqrt(vectors.shape[1])
    flat = lambda v: v.reshape(D, D)
    tall = pl.BlockSpec((rows, D), lambda i: (i, 0))
    count = vectors.shape[0]
    whole = pl.BlockSpec((count, D), lambda i: (0, 0))
    f = lambda *s: jax.ShapeDtypeStruct(s, F32)
    out = pl.pallas_call(
        functools.partial(adam_kernel, rate),
        grid=(steps,),
        out_shape=(f(D, D),) * 4 + (f(count, D),) * 4 + (f(D),),
        in_specs=[tall] * 4 + [pl.BlockSpec(sums.shape, lambda i: (0, 0, 0))] + [whole] * 3,
        out_specs=(tall,) * 4 + (whole,) * 4 + (pl.BlockSpec((D,), lambda i: (0,)),),
    )(flat(own), flat(store), flat(first), flat(second), sums, vectors, vector_first, vector_second)
    return tuple(v.reshape(store.shape) for v in out[:4]) + out[4:8] + (out[8],)


def linear_map_apply(left_side, right_side):
    return jnp.dot(left_side, right_side, preferred_element_type=jnp.float32)


def layer_norm(values, gain_values, shift_values):
    center = values - jnp.mean(values, axis=-1, keepdims=True)
    spread = jnp.mean(center * center, axis=-1, keepdims=True)
    factor = lax.rsqrt(spread + norm_eps)
    normed = center * factor
    return (normed * gain_values + shift_values, normed, factor)


def norm_back(grad_in, normed, factor, gain_values):
    scaled = grad_in * gain_values
    input_grad = factor * (
        scaled
        - jnp.mean(scaled, axis=-1, keepdims=True)
        - normed * jnp.mean(scaled * normed, axis=-1, keepdims=True)
    )
    return (input_grad, jnp.sum(grad_in * normed, axis=0), jnp.sum(grad_in, axis=0))


def gelu_exact(values):
    return 0.5 * values * (1.0 + lax.erf(values * root_half))


def gelu_slope(values):
    return (
        0.5 * (1.0 + lax.erf(values * root_half))
        + values * jnp.exp(-0.5 * values * values) * slope_norm
    )


def layer_weights(weight_tiles, base):
    joint_weight = jnp.concatenate(
        [weight_tiles[base], weight_tiles[base + 1], weight_tiles[base + 2]], axis=1
    )
    up_weight = jnp.concatenate([weight_tiles[base + 4 + number] for number in range(4)], axis=1)
    down_weight = jnp.concatenate([weight_tiles[base + 8 + number] for number in range(4)], axis=0)
    return (joint_weight, weight_tiles[base + 3], up_weight, down_weight)


def split_heads(joint_row, head_count):
    seq_len = joint_row.shape[0]
    model_width = joint_row.shape[1] // 3
    shaped = joint_row.reshape(seq_len, 3, head_count, model_width // head_count)
    return (shaped[:, 0], shaped[:, 1], shaped[:, 2])


def masked_scores(queries, keys_here, seg_row):
    score_scale = 1.0 / math.sqrt(queries.shape[-1])
    raw_scores = jnp.einsum("qhd,khd->hqk", queries, keys_here, preferred_element_type=jnp.float32)
    same_segment = seg_row[:, None] == seg_row[None, :]
    return (jnp.where(same_segment[None], raw_scores * score_scale, -1e30), score_scale)


def attend_forward(joint_row, seg_row, head_count):
    queries, keys_here, values_here = split_heads(joint_row, head_count)
    scores, score_scale = masked_scores(queries, keys_here, seg_row)
    row_peak = jnp.max(scores, axis=-1, keepdims=True)
    weights = jnp.exp(scores - row_peak)
    exp_total = jnp.sum(weights, axis=-1, keepdims=True)
    row_probabilities = (weights / exp_total).astype(jnp.bfloat16)
    mixed_heads = jnp.einsum(
        "hqk,khd->qhd", row_probabilities, values_here, preferred_element_type=jnp.float32
    )
    return (
        mixed_heads.reshape(mixed_heads.shape[0], -1),
        row_peak[..., 0] + jnp.log(exp_total[..., 0]),
    )


def attend_backward(joint_row, seg_row, lse_row, grad_row, head_count):
    queries, keys_here, values_here = split_heads(joint_row, head_count)
    seq_len = joint_row.shape[0]
    grad_heads = grad_row.reshape(seq_len, head_count, -1)
    scores, score_scale = masked_scores(queries, keys_here, seg_row)
    row_probabilities = jnp.exp(scores - lse_row[..., None])
    prob_grads = jnp.einsum(
        "qhd,khd->hqk", grad_heads, values_here, preferred_element_type=jnp.float32
    )
    inner_sum = jnp.sum(row_probabilities * prob_grads, axis=-1, keepdims=True)
    score_grads = (row_probabilities * (prob_grads - inner_sum) * score_scale).astype(jnp.bfloat16)
    query_grad = jnp.einsum(
        "hqk,khd->qhd", score_grads, keys_here, preferred_element_type=jnp.float32
    )
    key_grad = jnp.einsum("hqk,qhd->khd", score_grads, queries, preferred_element_type=jnp.float32)
    value_grad = jnp.einsum(
        "hqk,qhd->khd",
        row_probabilities.astype(jnp.bfloat16),
        grad_heads,
        preferred_element_type=jnp.float32,
    )
    return jnp.concatenate(
        [
            query_grad.reshape(seq_len, -1),
            key_grad.reshape(seq_len, -1),
            value_grad.reshape(seq_len, -1),
        ],
        axis=1,
    )


def layer_forward(inputs, segment, weight_tiles, vectors, base, head_count):
    joint_weight, out_weight, up_weight, down_weight = layer_weights(weight_tiles, base)
    model_width = inputs.shape[1]
    rows_here = segment.shape[0]
    inputs_low = inputs.astype(jnp.bfloat16)
    joint_bias = jnp.concatenate(
        [vectors[base], jnp.zeros((model_width,), jnp.float32), vectors[base + 1]]
    )
    joint_out = (linear_map_apply(inputs_low, joint_weight) + joint_bias).astype(jnp.bfloat16)
    joint_rows = joint_out.reshape(rows_here, -1, 3 * model_width)

    def forward_row(row_items):
        return attend_forward(row_items[0], row_items[1], head_count)

    mixed, log_total = lax.map(forward_row, (joint_rows, segment))
    mixed_low = mixed.reshape(-1, model_width).astype(jnp.bfloat16)
    branch = linear_map_apply(mixed_low, out_weight) + vectors[base + 2]
    hidden, normed_one, factor_one = layer_norm(
        inputs + branch, vectors[base + 3], vectors[base + 4]
    )
    hidden_low = hidden.astype(jnp.bfloat16)
    pre_gelu = linear_map_apply(hidden_low, up_weight) + vectors[base + 5 : base + 9].reshape(-1)
    active = gelu_exact(pre_gelu).astype(jnp.bfloat16)
    output = linear_map_apply(active, down_weight) + vectors[base + 9]
    result, normed_two, factor_two = layer_norm(
        hidden + output, vectors[base + 10], vectors[base + 11]
    )
    kept_values = (
        inputs_low,
        joint_rows,
        log_total,
        mixed_low,
        normed_one,
        factor_one,
        hidden_low,
        pre_gelu,
        active,
        normed_two,
        factor_two,
    )
    return (result, kept_values)


def layer_backward(grad_out, kept_values, segment, weight_tiles, vectors, base, head_count):
    joint_weight, out_weight, up_weight, down_weight = layer_weights(weight_tiles, base)
    (
        inputs_low,
        joint_rows,
        log_total,
        mixed_low,
        normed_one,
        factor_one,
        hidden_low,
        pre_gelu,
        active,
        normed_two,
        factor_two,
    ) = kept_values
    model_width = inputs_low.shape[1]
    grad_res2, gain_two, shift_two = norm_back(grad_out, normed_two, factor_two, vectors[base + 10])
    grad_output = grad_res2.astype(jnp.bfloat16)
    down_grad = jnp.einsum("tf,td->fd", active, grad_output, preferred_element_type=jnp.float32)
    down_bias = jnp.sum(grad_output.astype(jnp.float32), axis=0)
    grad_active = jnp.einsum(
        "td,fd->tf", grad_output, down_weight, preferred_element_type=jnp.float32
    )
    grad_pre = (grad_active * gelu_slope(pre_gelu)).astype(jnp.bfloat16)
    up_grad = jnp.einsum("td,tf->df", hidden_low, grad_pre, preferred_element_type=jnp.float32)
    up_bias = jnp.sum(grad_pre.astype(jnp.float32), axis=0)
    grad_hidden = (
        jnp.einsum("tf,df->td", grad_pre, up_weight, preferred_element_type=jnp.float32) + grad_res2
    )
    grad_res1, gain_one, shift_one = norm_back(
        grad_hidden, normed_one, factor_one, vectors[base + 3]
    )
    grad_branch = grad_res1.astype(jnp.bfloat16)
    out_grad = jnp.einsum("tc,td->cd", mixed_low, grad_branch, preferred_element_type=jnp.float32)
    out_bias = jnp.sum(grad_branch.astype(jnp.float32), axis=0)
    grad_mixed = jnp.einsum(
        "td,cd->tc", grad_branch, out_weight, preferred_element_type=jnp.float32
    ).astype(jnp.bfloat16)

    def backward_row(row_items):
        return attend_backward(row_items[0], row_items[1], row_items[2], row_items[3], head_count)

    grad_joint = lax.map(
        backward_row,
        (joint_rows, segment, log_total, grad_mixed.reshape(joint_rows.shape[0], -1, model_width)),
    )
    grad_joint = grad_joint.reshape(-1, 3 * model_width).astype(jnp.bfloat16)
    joint_grad = jnp.einsum("tc,te->ce", inputs_low, grad_joint, preferred_element_type=jnp.float32)
    joint_sums = jnp.sum(grad_joint.astype(jnp.float32), axis=0)
    grad_inputs = (
        jnp.einsum("te,ce->tc", grad_joint, joint_weight, preferred_element_type=jnp.float32)
        + grad_res1
    )
    tile_list = [
        joint_grad[:, :model_width],
        joint_grad[:, model_width : 2 * model_width],
        joint_grad[:, 2 * model_width :],
        out_grad,
    ]
    tile_list = tile_list + [
        up_grad[:, number * model_width : (number + 1) * model_width] for number in range(4)
    ]
    tile_list = tile_list + [
        down_grad[number * model_width : (number + 1) * model_width] for number in range(4)
    ]
    vector_list = [
        joint_sums[:model_width],
        joint_sums[2 * model_width :],
        out_bias,
        gain_one,
        shift_one,
    ]
    vector_list = vector_list + [
        up_bias[number * model_width : (number + 1) * model_width] for number in range(4)
    ]
    vector_list = vector_list + [down_bias, gain_two, shift_two]
    return (grad_inputs, tile_list, vector_list)


def adam_step(weights, first_moment, second_moment, grad_values, step_rate):
    first_new = first_decay * first_moment + (1.0 - first_decay) * grad_values
    second_new = second_decay * second_moment + (1.0 - second_decay) * grad_values * grad_values
    first_hat = first_new / (1.0 - first_decay**STEP)
    second_hat = second_new / (1.0 - second_decay**STEP)
    new_weights = weights - step_rate * (
        first_hat / (jnp.sqrt(second_hat) + adam_eps) + weight_decay * weights
    )
    return (new_weights, first_new, second_new)


def pick_rows(row_values, row_starts):
    return row_values[row_starts]


def local_any(
    tokens,
    lengths,
    pair_index,
    tile_slot,
    master_store,
    first_moment_store,
    second_moment_store,
    vectors,
    vector_first,
    vector_second,
):
    model_width = tokens.shape[1]
    rows_here = lengths.shape[0]
    sent_count = lengths.shape[1]
    seq_len = tokens.shape[0] // rows_here
    head_count = HEADS
    tile_count = tile_slot.shape[0]
    row_count = lax.axis_size("row")
    col_count = lax.axis_size("col")
    slot_count = master_store.shape[0] * col_count
    gathered_rows = lax.all_gather(master_store.astype(jnp.bfloat16), "row", axis=1, tiled=True)
    gathered = lax.all_gather(gathered_rows, "col", axis=0, tiled=True)
    weight_tiles = jnp.take(gathered, tile_slot, axis=0)
    starts = jnp.cumsum(lengths, axis=1) - lengths
    places = jnp.arange(seq_len, dtype=jnp.int32)
    segment = jnp.sum((places[None, :, None] >= starts[:, None, :]).astype(jnp.int32), axis=2) - 1
    hidden_state = tokens.astype(jnp.float32)
    kept_layers = []
    for layer_number in range(LAYERS):
        hidden_state, kept_values = layer_forward(
            hidden_state, segment, weight_tiles, vectors, 12 * layer_number, head_count
        )
        kept_layers.append(kept_values)
    encoded = hidden_state.reshape(rows_here, seq_len, model_width)
    cls_rows = jax.vmap(pick_rows)(encoded, starts).reshape(-1, model_width)
    cls_low = cls_rows.astype(jnp.bfloat16)
    pool_weight = weight_tiles[tile_count - 1]
    pooled = jnp.tanh(linear_map_apply(cls_low, pool_weight) + vectors[tile_count - 1])
    inverse = lax.rsqrt(jnp.sum(pooled * pooled, axis=1, keepdims=True) + unit_eps)
    unit_low = (pooled * inverse).astype(jnp.bfloat16)
    row_emb = lax.all_gather(unit_low, "col", axis=0, tiled=True)
    col_emb = lax.all_gather(unit_low, "row", axis=0, tiled=True)
    sent_dev = unit_low.shape[0]
    row_pos = lax.axis_index("row")
    col_pos = lax.axis_index("col")
    row_indices = row_pos * (col_count * sent_dev) + jnp.arange(
        col_count * sent_dev, dtype=jnp.int32
    )
    column_indices = (
        (jnp.arange(row_count, dtype=jnp.int32)[:, None] * col_count + col_pos) * sent_dev
        + jnp.arange(sent_dev, dtype=jnp.int32)[None, :]
    ).reshape(-1)
    plain_closeness = jnp.einsum("rd,cd->rc", row_emb, col_emb, preferred_element_type=jnp.float32)
    angular_closeness = jnp.where(
        row_indices[:, None] == column_indices[None, :],
        -1e30,
        plain_closeness / logit_sharpness_divisor,
    )
    target = jnp.take(pair_index, row_indices)
    positive_pair_matches = column_indices[None, :] == target[:, None]
    positive_local = jnp.sum(jnp.where(positive_pair_matches, angular_closeness, 0.0), axis=1)
    peak_local = jnp.max(angular_closeness, axis=1)
    row_peak = lax.pmax(peak_local, "col")
    mass_total, positive = lax.psum(
        (jnp.sum(jnp.exp(angular_closeness - row_peak[:, None]), axis=1), positive_local), "col"
    )
    log_mass = row_peak + jnp.log(mass_total)
    sentence_total = row_count * col_count * sent_dev
    row_probabilities = jnp.exp(angular_closeness - log_mass[:, None])
    similarity_gradient = (
        (row_probabilities - positive_pair_matches.astype(jnp.float32))
        / sentence_total
        / logit_sharpness_divisor
    ).astype(jnp.bfloat16)
    rows_part = jnp.einsum(
        "rc,cd->rd", similarity_gradient, col_emb, preferred_element_type=jnp.float32
    )
    cols_part = jnp.einsum(
        "rc,rd->cd", similarity_gradient, row_emb, preferred_element_type=jnp.float32
    )
    unit_sensitivity = lax.psum_scatter(
        rows_part.astype(jnp.bfloat16), "col", scatter_dimension=0, tiled=True
    ).astype(jnp.float32) + lax.psum_scatter(
        cols_part.astype(jnp.bfloat16), "row", scatter_dimension=0, tiled=True
    ).astype(
        jnp.float32
    )
    own_loss = jnp.sum(lax.dynamic_slice_in_dim(log_mass - positive, col_pos * sent_dev, sent_dev))
    dot_unit = jnp.sum(pooled * unit_sensitivity, axis=1, keepdims=True)
    grad_pooled = inverse * unit_sensitivity - pooled * inverse * inverse * inverse * dot_unit
    grad_pre = (grad_pooled * (1.0 - pooled * pooled)).astype(jnp.bfloat16)
    pool_grad = jnp.einsum("sd,se->de", cls_low, grad_pre, preferred_element_type=jnp.float32)
    pool_bias = jnp.sum(grad_pre.astype(jnp.float32), axis=0)
    grad_cls = jnp.einsum("se,de->sd", grad_pre, pool_weight, preferred_element_type=jnp.float32)
    one_hot = (places[None, None, :] == starts[:, :, None]).astype(jnp.float32)
    grad_state = jnp.einsum(
        "pek,pex->pkx",
        one_hot,
        grad_cls.reshape(rows_here, sent_count, model_width),
        precision=lax.Precision.HIGHEST,
    ).reshape(-1, model_width)
    tile_grads = []
    vector_grads = []
    for layer_number in reversed(range(LAYERS)):
        grad_state, tile_list, vector_list = layer_backward(
            grad_state,
            kept_layers[layer_number],
            segment,
            weight_tiles,
            vectors,
            12 * layer_number,
            head_count,
        )
        tile_grads = tile_list + tile_grads
        vector_grads = vector_list + vector_grads
    grad_stack = jnp.stack(tile_grads + [pool_grad])
    vector_stack = jnp.stack(vector_grads + [pool_bias])
    slot_indices = jnp.arange(slot_count, dtype=jnp.int32)
    matches = tile_slot[None, :] == slot_indices[:, None]
    filled = jnp.any(matches, axis=1)
    source_tile = jnp.sum(
        jnp.where(matches, jnp.arange(tile_count, dtype=jnp.int32)[None, :], 0), axis=1
    )
    whole_slots = lax.psum_scatter(
        jnp.where(filled[:, None, None], jnp.take(grad_stack, source_tile, axis=0), 0.0).astype(
            jnp.bfloat16
        ),
        "col",
        scatter_dimension=0,
        tiled=True,
    )
    owned_grad = lax.psum_scatter(whole_slots, "row", scatter_dimension=1, tiled=True).astype(
        jnp.float32
    )
    vector_total, loss_total = lax.psum((vector_stack, own_loss), ("row", "col"))
    mean_loss = loss_total / sentence_total
    new_store, new_store_first, new_store_second = adam_step(
        master_store,
        first_moment_store,
        second_moment_store,
        owned_grad,
        store_rate_factor / math.sqrt(model_width),
    )
    new_vectors, new_vector_first, new_vector_second = adam_step(
        vectors, vector_first, vector_second, vector_total, vector_rate
    )
    out_bias_grad = vector_total[12 * (LAYERS - 1) + 2]
    return (
        grad_state,
        mean_loss,
        owned_grad,
        new_store,
        new_store_first,
        new_store_second,
        vector_total,
        new_vectors,
        new_vector_first,
        new_vector_second,
        out_bias_grad,
    )


def local_here(
    tokens,
    lengths,
    pair_index,
    tile_slot,
    master_store,
    first_moment_store,
    second_moment_store,
    vectors,
    vector_first,
    vector_second,
):
    (
        weights, joint, prob, mixed, normed_one, hidden_low, active, slope, normed_two, factors, state_low,
        source_tile, filled, keys_grad, cls_grad, packed_left, row_right, head_vectors, loss,
    ) = forward_fused(tile_slot, master_store, tokens, lengths, vectors, pair_index)
    owned_low, vector_sums, grad_state = backward_fused(
        lengths, source_tile, filled, factors, cls_grad, packed_left, row_right, head_vectors, vectors, weights, state_low, tokens,
        joint, prob, mixed, normed_one, hidden_low, active, slope, normed_two, keys_grad,
    )
    (
        owned_grad, new_store, new_store_first, new_store_second,
        vector_total, new_vectors, new_vector_first, new_vector_second, out_bias_grad,
    ) = adam_all(
        owned_low, master_store, first_moment_store, second_moment_store, vector_sums, vectors, vector_first, vector_second
    )
    return (
        grad_state,
        loss[0, 0],
        owned_grad,
        new_store,
        new_store_first,
        new_store_second,
        vector_total,
        new_vectors,
        new_vector_first,
        new_vector_second,
        out_bias_grad,
    )


def solution(mesh):
    placed = (
        P(("row", "col"), None),
        P(("row", "col"), None),
        P(),
        P(),
        P("col", "row", None),
        P("col", "row", None),
        P("col", "row", None),
        P(),
        P(),
        P(),
    )
    fits = (mesh.shape["row"], mesh.shape["col"]) == (4, 8)
    return jax.shard_map(
        local_here if fits else local_any,
        mesh=mesh,
        in_specs=placed,
        out_specs=(
            P(("row", "col"), None),
            P(),
            P("col", "row", None),
            P("col", "row", None),
            P("col", "row", None),
            P("col", "row", None),
            P(),
            P(),
            P(),
            P(),
            P(),
        ),
        check_vma=False,
    )
```

```python
import functools
import math

import jax
import jax.numpy as jnp
from jax import lax
from jax.experimental import pallas as pl
from jax.experimental.pallas import tpu as pltpu
from jax.sharding import PartitionSpec as P

HEADS = 12
LAYERS = 2
STEP = 10


norm_eps = 1e-12
unit_eps = 1e-06
logit_sharpness_divisor = 0.05
first_decay = 0.9
second_decay = 0.999
adam_eps = 1e-08
weight_decay = 0.01
vector_rate = 0.5
store_rate_factor = 1.5
root_half = 1.0 / math.sqrt(2.0)
slope_norm = 1.0 / math.sqrt(2.0 * math.pi)


MESH = pl.DeviceIdType.MESH
D = 768
H = 384
R = 48
BIG = 67043328 - 256 * 1024


def remote(src, dst, s, r, dev):
    return pltpu.make_async_remote_copy(
        src_ref=src, dst_ref=dst, send_sem=s, recv_sem=r, device_id=dev, device_id_type=MESH
    )


def place():
    z = lax.axis_index("row")
    c = lax.axis_index("col")
    return z, c, c // 4, (c // 2) % 2, c % 2


def col_peer(c, d):
    return lax.rem(c + d, 8)


def row_peer(z, d):
    return lax.rem(z + d, 4)


def half_of(k):
    return pl.ds(pl.multiple_of(k * H, H), H)


BF = jnp.bfloat16
F32 = jnp.float32
KT = 14
ORDER = tuple(range(12)) + (13, 14, 12, 15) + tuple(range(16, 25))


def dot_nn(left, right):
    return jnp.dot(left, right, preferred_element_type=F32)


def dot_nt(left, right):
    return lax.dot_general(left, right, (((1,), (1,)), ((), ())), preferred_element_type=F32)


def dot_tn(left, right):
    return lax.dot_general(left, right, (((0,), (0,)), ((), ())), preferred_element_type=F32)


def colsum(v):
    return jnp.sum(v.astype(F32), axis=0, keepdims=True)


def norm_rows(v):
    center = v - jnp.mean(v, axis=1, keepdims=True)
    factor = lax.rsqrt(jnp.mean(center * center, axis=1, keepdims=True) + norm_eps)
    return center * factor, factor


def norm_rows_back(grad, normed, factor, gain):
    e = grad * gain
    return factor * (e - jnp.mean(e, axis=1, keepdims=True) - normed * jnp.mean(e * normed, axis=1, keepdims=True))


def window(block):
    return max(0, block - 1) * 128, min(4, block + 2) * 128


def forward_kernel(
    T, total, slot_ref, len_ref, pair_ref, master_ref, tok_ref, vec_ref, pairr_ref,
    w_out, qkv_out, p_out, o_out, n1_out, h1_out, act_out, slope_out, n2_out, s_out, low_out,
    src_ref, fill_ref, dkv_ref, dcls_ref, packed_ref, right_ref, vg_ref, loss_ref,
    w, stage, spread, qkv, prob, mixed, acc, normed, h1, h1b, u1b, act, slope, fac, kv, bias, uc, acts, slopes, unit, everyone,
    lsem, xs, xr, zs, zr, as_, ar, bs, br, cs, cr, osem, fsem, ss, sr,
):
    z, c, y, x, k = place()
    cx = c + 2 - 4 * x
    cy = c + 4 - 8 * y
    ck = c + 1 - 2 * k
    half = half_of(k)
    me = z * 8 + c
    bar = pltpu.get_barrier_semaphore()

    def peer(d):
        p = lax.rem(me + d, 32)
        return p, (p // 8, lax.rem(p, 8))

    def greet(d, _):
        pl.semaphore_signal(bar, inc=1, device_id=peer(d)[1], device_id_type=MESH)
        return 0

    lax.fori_loop(1, 32, greet, 0)

    def cast(s, _):
        stage[s] = master_ref[s].reshape(4, R, D).astype(BF)
        return 0

    lax.fori_loop(0, 4, cast, 0)
    pl.semaphore_wait(bar, 31)

    def spread_copy(d):
        p = col_peer(c, d)
        return remote(stage.at[:, p // 2, :, half_of(p % 2)], spread.at[pl.ds(4 * c, 4)], xs.at[d - 1], xr.at[d - 1], (z, p))

    for d in range(1, 8):
        spread_copy(d).start()
    own = pltpu.make_async_copy(stage.at[:, c // 2, :, half], spread.at[pl.ds(4 * c, 4)], lsem)
    own.start()
    starts = [0]
    for i in range(7):
        starts.append(starts[i] + len_ref[i])
    row_places = lax.broadcasted_iota(jnp.int32, (1, 512), 1)
    segr = jnp.zeros((1, 512), jnp.int32)
    for i in range(1, 8):
        segr = segr + (row_places >= starts[i]).astype(jnp.int32)
    for b in range(4):
        lo, hi = window(b)
        places = lax.broadcasted_iota(jnp.int32, (128, 1), 0) + 128 * b
        segc = jnp.zeros((128, 1), jnp.int32)
        for i in range(1, 8):
            segc = segc + (places >= starts[i]).astype(jnp.int32)
        bias[b, :, 0 : hi - lo] = jnp.where(segc == segr[:, lo:hi], 0.0, -1e30)

    def slot_source(s, _):
        found, hits = 0, 0
        for t in range(T):
            hit = slot_ref[t] == s
            found = found + jnp.where(hit, PIECE_ORDER.index(t), 0)
            hits = hits + jnp.where(hit, 1, 0)
        src_ref[s] = found
        fill_ref[s] = hits
        return 0

    lax.fori_loop(0, 32, slot_source, 0)
    own.wait()
    for d in range(1, 8):
        spread_copy(d).wait_recv()

    def zcopies(t):
        v = w.at[t, z, y, x, :, half]
        return [remote(v, v, zs.at[t, d - 1], zr.at[t, d - 1], (row_peer(z, d), c)) for d in (1, 2, 3)]

    def first(t):
        va, vb = w.at[t, 0:2, y, x, :, half], w.at[t, 2:4, y, x, :, half]
        return [remote(va, va, as_.at[t, 0], ar.at[t, 0], (z, cx)), remote(vb, vb, as_.at[t, 1], ar.at[t, 1], (z, cy))]

    def second(t):
        va, vb = w.at[t, 0:2, y, :, :, half], w.at[t, 2:4, :, x, :, half]
        return [remote(va, va, bs.at[t, 0], br.at[t, 0], (z, cy)), remote(vb, vb, bs.at[t, 1], br.at[t, 1], (z, cx))]

    def core(t):
        v = w.at[t, :, :, :, :, half]
        return remote(v, v, cs.at[t], cr.at[t], (z, ck))

    def outc(t):
        return pltpu.make_async_copy(w.at[t], w_out.at[t], osem.at[t])

    for t in range(T):
        w[t, z, y, x, :, half] = spread[slot_ref[ORDER[t]]]

    def issue(t, _):
        for cpy in zcopies(t):
            cpy.start()
        return 0

    lax.fori_loop(0, KT, issue, 0)

    def pair_first(t):
        v = w.at[t, z, y, x, :, half]
        return remote(v, v, as_.at[t, 0], ar.at[t, 0], (z, cx if t % 2 == 0 else cy))

    def pair_z(t):
        v = w.at[t, z, y, :, :, half] if t % 2 == 0 else w.at[t, z, :, x, :, half]
        return [remote(v, v, zs.at[t, d - 1], zr.at[t, d - 1], (row_peer(z, d), c)) for d in (1, 2, 3)]

    def pair_last(t):
        v = w.at[t, :, y, :, :, half] if t % 2 == 0 else w.at[t, :, :, x, :, half]
        return remote(v, v, bs.at[t, 0], br.at[t, 0], (z, cy if t % 2 == 0 else cx))

    for t in range(KT, T):
        pair_first(t).start()
    LAGS = (0, 1, 3, 4)

    def f0(t):
        if isinstance(t, int) and t >= KT:
            for cpy in pair_z(t):
                cpy.wait_recv()
            pair_last(t).start()
            return
        for cpy in zcopies(t):
            cpy.wait_recv()
        for cpy in first(t):
            cpy.start()

    def f1(t):
        if isinstance(t, int) and t >= KT:
            return
        for there, on in zip(first(t), second(t)):
            there.wait_recv()
            on.start()

    def f2(t):
        for cpy in [pair_last(t)] if isinstance(t, int) and t >= KT else second(t):
            cpy.wait_recv()
        core(t).start()

    def f3(t):
        core(t).wait_recv()
        outc(t).start()

    state = [0]

    def pump():
        i = state[0]
        if i < T + LAGS[3]:
            for f, lag in zip((f0, f1, f2, f3), LAGS):
                if 0 <= i - lag < T:
                    f(i - lag)
            state[0] = i + 1

    def pump_at(i):
        for f, lag in zip((f0, f1, f2, f3), LAGS):
            f(i - lag)

    def need(t):
        if isinstance(t, int):
            while state[0] <= t + LAGS[3]:
                pump()

    flushes = []
    counter = [0]

    def flush(src, dst):
        cpy = pltpu.make_async_copy(src, dst, fsem.at[counter[0]])
        counter[0] += 1
        cpy.start()
        flushes.append(cpy)

    def wcols(t, n):
        return w[t, :, :, :, :, pl.ds(pl.multiple_of(n * 256, 256), 256)].reshape(D, 256)

    def cols(n):
        return pl.ds(pl.multiple_of(n * 256, 256), 256)

    def norm(gain, shift, normed, out, low, number):
        def rows(m, _):
            rs = pl.ds(pl.multiple_of(m * 64, 64), 64)
            v = acc[rs, :]
            center = v - jnp.mean(v, axis=1, keepdims=True)
            factor = lax.rsqrt(jnp.mean(center * center, axis=1, keepdims=True) + norm_eps)
            nv = center * factor
            normed[rs, :] = nv
            fac[rs, number : number + 1] = factor
            o = nv * gain + shift
            out[rs, :] = o
            if low is not None:
                low[rs, :] = o.astype(BF)
            return 0

        lax.fori_loop(0, 8, rows, 0)

    for part in range(3):
        need(part)
        if part == 1:
            for t in range(KT, T):
                pair_first(t).wait_recv()
                for cpy in pair_z(t):
                    cpy.start()

        def project(n, _):
            r = dot_nn(tok_ref[...], wcols(part, n))
            if part != 1:
                r = r + vec_ref[part // 2 : part // 2 + 1, cols(n)]
            qkv[part, :, cols(n)] = r.astype(BF)
            return 0

        lax.fori_loop(0, 3, project, 0)
    flush(qkv, qkv_out)
    left = lax.broadcasted_iota(jnp.int32, (1, 128), 1) < 64

    keep_left = jnp.where(left, 0.125, 0.0).astype(BF)
    keep_right = jnp.where(left, 0.0, 0.125).astype(BF)

    def pair(p, side):
        lanes = pl.ds(pl.multiple_of(p * 128, 128), 128)
        for b in range(4):
            lo, hi = window(b)
            q = qkv[0, 128 * b : 128 * (b + 1), lanes]
            kk = qkv[1, lo:hi, lanes]
            vv = qkv[2, lo:hi, lanes]
            s = dot_nt(jnp.concatenate([q * keep_left, q * keep_right], axis=0), kk)
            mask = bias[b, :, 0 : hi - lo]
            s = s + jnp.concatenate([mask, mask], axis=0)
            ex = jnp.exp(s - jnp.max(s, axis=1, keepdims=True))
            pr = (ex * (1.0 / jnp.sum(ex, axis=1, keepdims=True))).astype(BF)
            prob[side, b, :, 0 : hi - lo] = pr
            big = dot_nn(pr, vv)
            mixed[128 * b : 128 * (b + 1), lanes] = jnp.where(left, big[0:128, :], big[128:256, :]).astype(BF)

    def pairs(p, _):
        side = lax.rem(p, 2)
        out = pltpu.make_async_copy(prob.at[side], p_out.at[p], fsem.at[20 + side])

        @pl.when(p > 1)
        def _():
            out.wait()

        pair(p, side)
        out.start()
        pump_at(base + p)
        return 0

    base = state[0]
    lax.fori_loop(0, 6, pairs, 0)
    state[0] = base + 6
    for side in range(2):
        pltpu.make_async_copy(prob.at[side], p_out.at[4 + side], fsem.at[20 + side]).wait()
    flush(mixed, o_out)
    need(3)

    def attend_out(n, _):
        acc[:, cols(n)] = (
            dot_nn(mixed[...], wcols(3, n)) + vec_ref[2:3, cols(n)] + tok_ref[:, cols(n)].astype(F32)
        )
        return 0

    lax.fori_loop(0, 3, attend_out, 0)
    norm(vec_ref[3:4, :], vec_ref[4:5, :], normed, h1, h1b, 0)
    flush(normed, n1_out)
    first_norm = flushes.pop()
    flush(h1b, h1_out)
    slope_copies = []
    for j in range(4):
        need(4 + j)

        def up(n, _):
            acc[:, cols(n)] = dot_nn(h1b[...], wcols(4 + j, n)) + vec_ref[5 + j : 6 + j, cols(n)]
            return 0

        lax.fori_loop(0, 3, up, 0)

        def gelu(m, _):
            rs = pl.ds(pl.multiple_of(m * 32, 32), 32)
            f = acc[rs, :]
            cdf = 0.5 * (1.0 + lax.erf(f * root_half))
            act[j, rs, :] = (f * cdf).astype(BF)
            slope[j % 2, rs, :] = (cdf + f * jnp.exp(-0.5 * f * f) * slope_norm).astype(BF)
            return 0

        if j >= 2:
            slope_copies[j - 2].wait()
        lax.fori_loop(0, 16, gelu, 0)
        flush(act.at[j], act_out.at[j])
        slope_copies.append(pltpu.make_async_copy(slope.at[j % 2], slope_out.at[j], fsem.at[22 + j % 2]))
        slope_copies[j].start()
    for j in range(4):
        need(8 + j)

        def down(n, _):
            r = dot_nn(act[j], wcols(8 + j, n))
            if j == 0:
                acc[:, cols(n)] = r + vec_ref[9:10, cols(n)] + h1[:, cols(n)]
            else:
                acc[:, cols(n)] += r
            return 0

        lax.fori_loop(0, 3, down, 0)
    first_norm.wait()
    norm(vec_ref[10:11, :], vec_ref[11:12, :], normed, h1, u1b, 1)
    flush(normed, n2_out)
    flush(fac, s_out)
    flush(u1b, low_out)
    for part in range(2):
        need(12 + part)

        def project_next(n, _):
            r = dot_nn(u1b[...], wcols(12 + part, n))
            if part == 1:
                r = r + vec_ref[13:14, cols(n)]
            kv[part, :, cols(n)] = r.astype(BF)
            return 0

        lax.fori_loop(0, 3, project_next, 0)
    def tile(t):
        return w[t].reshape(D, D)

    def vrow(r):
        return vec_ref[12 + r : 13 + r, :]

    def emit(r, v):
        vg_ref[r : r + 1, :] = v

    head_of = lax.broadcasted_iota(jnp.int32, (1, D), 1) // 64

    def by_head(v):
        v = v.astype(F32)
        return jnp.concatenate([jnp.where(head_of == h, v, 0.0) for h in range(12)], axis=0).astype(BF)

    def from_heads(big):
        out = jnp.where(head_of == 0, big[0:8, :], 0.0)
        for h in range(1, 12):
            out = out + jnp.where(head_of == h, big[8 * h : 8 * h + 8, :], 0.0)
        return out

    for s in range(8):
        uc[s : s + 1, :] = h1[pl.ds(starts[s], 1), :]
    low = uc[...].astype(BF)
    need(14)
    q = (dot_nn(low, tile(14)) + vrow(0)).astype(BF)
    qbig = by_head(q)
    same = segr == lax.broadcasted_iota(jnp.int32, (8, 512), 0)
    bias = jnp.where(same, 0.0, -1e30)
    sc = dot_nt(qbig, kv[0]) * 0.125 + jnp.concatenate([bias] * 12, axis=0)
    ex = jnp.exp(sc - jnp.max(sc, axis=1, keepdims=True))
    prob = ex * (1.0 / jnp.sum(ex, axis=1, keepdims=True))
    plow = prob.astype(BF)
    o = from_heads(dot_nn(plow, kv[1])).astype(BF)
    need(15)
    n1, s1 = norm_rows(uc[...] + dot_nn(o, tile(15)) + vrow(2))
    h1 = n1 * vrow(3) + vrow(4)
    h1b_cls = h1.astype(BF)
    need(19)

    def up_cls(j, _):
        f = dot_nn(h1b_cls, tile(16 + j)) + vec_ref[pl.ds(17 + j, 1), :]
        cdf = 0.5 * (1.0 + lax.erf(f * root_half))
        acts[j] = (f * cdf).astype(BF)
        slopes[j] = cdf + f * jnp.exp(-0.5 * f * f) * slope_norm
        return 0

    lax.fori_loop(0, 4, up_cls, 0)
    need(23)
    out = lax.fori_loop(0, 4, lambda j, total_: total_ + dot_nn(acts[j], tile(20 + j)), h1 + vrow(9))
    n2, s2 = norm_rows(out)
    zb = (n2 * vrow(10) + vrow(11)).astype(BF)
    need(24)
    pooled = jnp.tanh(dot_nn(zb, tile(24)) + vrow(12))
    inv = lax.rsqrt(jnp.sum(pooled * pooled, axis=1, keepdims=True) + unit_eps)
    unit[...] = (pooled * inv).astype(BF)
    everyone[me] = unit[...]

    def send(d, _):
        p, dev = peer(d)
        remote(unit, everyone.at[me], ss.at[d], sr.at[d], dev).start()
        return 0

    lax.fori_loop(1, 32, send, 0)
    packed_ref[...] = jnp.zeros((16, 4, 8, 128), BF)
    wholes = (acts[0], acts[1], acts[2], acts[3], h1b_cls, o, low, zb)
    for n, v in enumerate(wholes):
        v = v.astype(F32)
        off = 64 * (n % 2)
        for i in range(16):
            packed_ref[i, n // 2, :, off : off + R] = v[:, R * i : R * i + R].astype(BF)

    def arrive(d, _):
        q_ = lax.rem(me + 32 - d, 32)
        remote(unit, everyone.at[q_], ss.at[d], sr.at[d], peer(d)[1]).wait()
        return 0

    lax.fori_loop(1, 32, arrive, 0)
    everybody = everyone[...].astype(F32).reshape(256, D).astype(BF)
    sim = dot_nt(everybody, everybody) / logit_sharpness_divisor
    ri = lax.broadcasted_iota(jnp.int32, (256, 256), 0)
    ci = lax.broadcasted_iota(jnp.int32, (256, 256), 1)
    sim = jnp.where(ri == ci, -1e30, sim)
    peak = jnp.max(sim, axis=0, keepdims=True)
    lse = peak + jnp.log(jnp.sum(jnp.exp(sim - peak), axis=0, keepdims=True))
    pos = jnp.sum(jnp.where(ri == pairr_ref[...], sim, 0.0), axis=0, keepdims=True)
    loss_ref[...] = jnp.sum(lse - pos, axis=1, keepdims=True) / total
    own = dot_nt(unit[...], everybody) / logit_sharpness_divisor
    oi = lax.broadcasted_iota(jnp.int32, (8, 256), 0) + me * 8
    oj = lax.broadcasted_iota(jnp.int32, (8, 256), 1)
    own = jnp.where(oi == oj, -1e30, own)
    opeak = jnp.max(own, axis=1, keepdims=True)
    olse = opeak + jnp.log(jnp.sum(jnp.exp(own - opeak), axis=1, keepdims=True))
    sub = lax.broadcasted_iota(jnp.int32, (8, 1), 0)
    opair = jnp.zeros((8, 1), jnp.int32)
    for s in range(8):
        opair = jnp.where(sub == s, pair_ref[me * 8 + s], opair)
    g_rows = ((jnp.exp(own - olse) - (oj == opair).astype(F32)) / total / logit_sharpness_divisor).astype(BF)
    g_cols = ((jnp.exp(own - lse) - (pairr_ref[...] == oi).astype(F32)) / total / logit_sharpness_divisor).astype(BF)
    dunit = dot_nn(g_rows, everybody) + dot_nn(g_cols, everybody)
    dpooled = inv * dunit - pooled * (inv * inv * inv * jnp.sum(pooled * dunit, axis=1, keepdims=True))
    dpre = (dpooled * (1.0 - pooled * pooled)).astype(BF)
    right_ref[0] = dpre
    emit(12, colsum(dpre))
    dz = dot_nt(dpre, tile(24))
    emit(10, colsum(dz * n2))
    emit(11, colsum(dz))
    dr2 = norm_rows_back(dz, n2, s2, vrow(10))
    dy = dr2.astype(BF)
    right_ref[1] = dy
    emit(9, colsum(dy))

    def down_cls(j, dh):
        df = (dot_nt(dy, tile(20 + j)) * slopes[j]).astype(BF)
        right_ref[2 + j] = df
        vg_ref[pl.ds(5 + j, 1), :] = colsum(df)
        return dh + dot_nt(df, tile(16 + j))

    dh = lax.fori_loop(0, 4, down_cls, dr2)
    emit(3, colsum(dh * n1))
    emit(4, colsum(dh))
    dr1 = norm_rows_back(dh, n1, s1, vrow(3))
    da = dr1.astype(BF)
    right_ref[6] = da
    emit(2, colsum(da))
    dobig = by_head(dot_nt(da, tile(15)).astype(BF))
    dp = dot_nt(dobig, kv[1])
    ds = (prob * (dp - jnp.sum(prob * dp, axis=1, keepdims=True)) * 0.125).astype(BF)
    dq = from_heads(dot_nn(ds, kv[0])).astype(BF)
    right_ref[7] = dq
    emit(0, colsum(dq))
    dcls_ref[...] = dot_nt(dq, tile(14)) + dr1
    dkv_ref[0] = dot_tn(ds, qbig).astype(BF)
    dv = dot_tn(plow, dobig).astype(BF)
    dkv_ref[1] = dv
    emit(1, colsum(dv))
    for d in range(1, 8):
        spread_copy(d).wait_send()

    def drain(t, _):
        for cpy in zcopies(t) + first(t) + second(t) + [core(t)]:
            cpy.wait_send()
        outc(t).wait()
        return 0

    lax.fori_loop(0, KT, drain, 0)
    for t in range(KT, T):
        for cpy in pair_z(t) + [pair_first(t), pair_last(t), core(t)]:
            cpy.wait_send()
        outc(t).wait()
    for cpy in slope_copies[2:]:
        cpy.wait()
    for cpy in flushes:
        cpy.wait()


def forward_fused(slots, master, tokens, lengths, vectors, pair_index):
    T = slots.shape[0]
    total = pair_index.shape[0]
    dma = lambda *n: pltpu.SemaphoreType.DMA(n)
    V = pl.BlockSpec(memory_space=pltpu.VMEM)
    S = pl.BlockSpec(memory_space=pltpu.SMEM)
    ANY = pl.BlockSpec(memory_space=pl.ANY)
    shapes = [
        ((T, 4, 2, 2, R, D), BF), ((3, 512, D), BF), ((6, 4, 256, 384), BF), ((512, D), BF), ((512, D), F32), ((512, D), BF),
        ((4, 512, D), BF), ((4, 512, D), BF), ((512, D), F32), ((512, 2), F32), ((512, D), BF),
        ((32,), jnp.int32), ((32,), jnp.int32), ((2, 512, D), BF), ((8, D), F32), ((16, 4, 8, 128), BF), ((8, 8, D), BF), ((13, D), F32), ((1, 1), F32),
    ]
    vm = pltpu.VMEM
    scratch = [
        vm((T, 4, 2, 2, R, D), BF), vm((4, 4, R, D), BF), vm((32, R, H), BF), vm((3, 512, D), BF), vm((2, 4, 256, 384), BF), vm((512, D), BF),
        vm((512, D), F32), vm((512, D), F32), vm((512, D), F32), vm((512, D), BF), vm((512, D), BF), vm((4, 512, D), BF), vm((2, 512, D), BF),
        vm((512, 2), F32), vm((2, 512, D), BF), vm((4, 128, 384), F32), vm((8, D), F32), vm((4, 8, D), BF), vm((4, 8, D), F32), vm((8, D), BF), vm((32, 8, D), BF),
        dma(), dma(7), dma(7), dma(T, 3), dma(T, 3), dma(T, 2), dma(T, 2), dma(T, 2), dma(T, 2), dma(T), dma(T), dma(T), dma(24), dma(32), dma(32),
    ]
    return pl.pallas_call(
        functools.partial(forward_kernel, T, total),
        out_shape=tuple(jax.ShapeDtypeStruct(*s) for s in shapes),
        in_specs=[S, S, S] + [V] * 4,
        out_specs=(ANY,) * 11 + (S, S) + (V,) * 6,
        scratch_shapes=scratch,
        compiler_params=pltpu.CompilerParams(collective_id=0, has_side_effects=True, vmem_limit_bytes=BIG),
    )(slots, lengths.reshape(-1), pair_index, master, tokens, vectors, pair_index[None, :])

RS_TILES = (13, 14, 8, 4, 9, 5, 10, 6, 11, 7, 3, 0, 1, 2)
PIECE_ORDER = RS_TILES + (12,) + tuple(range(15, 25))
LATE = 5
FACTOR_MODES = ("xzyk", "yzxk")
FACTOR_TICKS = ((3, 8, 18), (3, 8, 18))
EARLY_LAGS = ((1, 3, 5, 11), (1, 3, 6, 11), (1, 4, 7, 11))
RS_LAGS = (2, 5, 8, 11)
W_SEQ = (12, 13, 8, 4, 9, 5, 10, 6, 11, 7, 3, 0, 1, 2)


def backward_kernel(
    len_ref, src_ref, fill_ref, fac_ref, dcls_ref, packed_ref, right_ref, vg_ref, vec_ref,
    w_ref, a1_ref, tok_ref, qkv_ref, p_ref, o_ref, n1_ref, h1_ref, act_ref, slope_ref, n2_ref, dkv_ref,
    own_ref, vout_ref, dtok_ref,
    g, rc, r1, r2, r3, every, lefts, piece, spread, vecs, vin, vsum,
    wbuf, xbuf, h1b, qkv, prob, dqkv, norm, acc, dy, df, dk_acc, dv_acc,
    cs, cr, as_, ar, bs, br, zs, zr, xs, xr, vs, vr, ws, wr, fs, fr, fz, fzr, ls, lr, wsem, xsem, psem, lsem,
):
    z, c, y, x, k = place()
    cx = c + 2 - 4 * x
    cy = c + 4 - 8 * y
    ck = c + 1 - 2 * k
    me = z * 8 + c
    half = half_of(k)
    other = half_of(1 - k)
    T = len(RS_TILES)
    starts = [0]
    for i in range(7):
        starts.append(starts[i] + len_ref[i])

    def wload(i):
        return pltpu.make_async_copy(w_ref.at[W_SEQ[i]], wbuf.at[i % 3], wsem.at[i % 3])

    x_seq = [a1_ref]
    for j in range(4):
        x_seq += [act_ref.at[j], slope_ref.at[j]]
    x_seq += [o_ref, tok_ref]

    def xload(i):
        return pltpu.make_async_copy(x_seq[i], xbuf.at[i % 4], xsem.at[i % 4])

    def pload(p):
        return pltpu.make_async_copy(p_ref.at[p], prob.at[p % 2], psem.at[p % 2])

    load_dkv = pltpu.make_async_copy(dkv_ref, dqkv.at[pl.ds(0, 2)], lsem.at[0])
    load_n2 = pltpu.make_async_copy(n2_ref, norm, lsem.at[1])
    load_n1 = pltpu.make_async_copy(n1_ref, norm, lsem.at[1])
    load_h1 = pltpu.make_async_copy(h1_ref, h1b, lsem.at[2])
    load_qkv = pltpu.make_async_copy(qkv_ref, qkv, lsem.at[3])
    load_dkv.start()
    xload(0).start()
    wload(0).start()
    wload(1).start()
    load_n2.start()
    for i in (1, 2, 3):
        xload(i).start()
    wload(2).start()
    load_h1.start()
    load_qkv.start()
    pload(0).start()
    pload(1).start()

    bar = pltpu.get_barrier_semaphore()

    def peer(d):
        p = lax.rem(me + d, 32)
        return p, (p // 8, lax.rem(p, 8))

    def greet(d, _):
        pl.semaphore_signal(bar, inc=1, device_id=peer(d)[1], device_id_type=MESH)
        return 0

    lax.fori_loop(1, 32, greet, 0)

    def region(n, have):
        zi = slice(None) if "z" in have else z
        yi = slice(None) if "y" in have else y
        xi = slice(None) if "x" in have else x
        ki = slice(None) if "k" in have else k
        return every.at[zi, yi, xi, ki, 4 * n : 4 * n + 4]

    def factor_copies(n, number):
        mode = FACTOR_MODES[n]
        v = region(n, mode[:number])
        axis = mode[number]
        if axis == "z":
            return [remote(v, v, fz.at[n, d - 1], fzr.at[n, d - 1], (row_peer(z, d), c)) for d in (1, 2, 3)]
        return [remote(v, v, fs.at[n, number], fr.at[n, number], (z, {"x": cx, "y": cy, "k": ck}[axis]))]

    def factor_step(n, number):
        if number:
            for cpy in factor_copies(n, number - 1):
                cpy.wait_recv()
        if number < 4:
            for cpy in factor_copies(n, number):
                cpy.start()

    def factor_stage(number):
        for n in range(2):
            factor_step(n, number)

    every[z, y, x, k] = right_ref[...]
    lefts[me] = packed_ref[me // 2]

    def lcopy(d, row):
        p, dev = peer(d)
        return remote(packed_ref.at[p // 2], lefts.at[row], ls.at[d], lr.at[d], dev)

    def lstart(d, _):
        lcopy(d, me).start()
        return 0

    pl.semaphore_wait(bar, 31)
    factor_stage(0)
    lax.fori_loop(1, 32, lstart, 0)

    def core(t):
        return remote(g.at[t, :, :, :, :, other], rc.at[t], cs.at[t], cr.at[t], (z, ck))

    def first(t):
        return [
            remote(g.at[t, 0:2, 1 - y, :, :, half], r1.at[t, 0:2], as_.at[t, 0], ar.at[t, 0], (z, cy)),
            remote(g.at[t, 2:4, :, 1 - x, :, half], r1.at[t, 2:4], as_.at[t, 1], ar.at[t, 1], (z, cx)),
        ]

    def second(t):
        return [
            remote(g.at[t, 0:2, y, 1 - x, :, half], r2.at[t, 0:2], bs.at[t, 0], br.at[t, 0], (z, cx)),
            remote(g.at[t, 2:4, 1 - y, x, :, half], r2.at[t, 2:4], bs.at[t, 1], br.at[t, 1], (z, cy)),
        ]

    def zcopies(t):
        return [
            remote(g.at[t, row_peer(z, d), y, x, :, half], r3.at[t, d - 1], zs.at[t, d - 1], zr.at[t, d - 1], (row_peer(z, d), c))
            for d in (1, 2, 3)
        ]

    def plus(a, b):
        return (a.astype(F32) + b.astype(F32)).astype(BF)

    def f1(t):
        core(t).wait_recv()
        for part in range(2):
            for zz in (2 * part, 2 * part + 1):
                g[t, zz, :, :, :, half] = plus(g[t, zz, :, :, :, half], rc[t, zz])
            first(t)[part].start()

    def f2(t):
        for part in range(2):
            first(t)[part].wait_recv()
            for zz in (2 * part, 2 * part + 1):
                if part == 0:
                    g[t, zz, y, :, :, half] = plus(g[t, zz, y, :, :, half], r1[t, zz])
                else:
                    g[t, zz, :, x, :, half] = plus(g[t, zz, :, x, :, half], r1[t, zz])
            second(t)[part].start()

    def f3(t):
        for part in range(2):
            second(t)[part].wait_recv()
        for zz in range(4):
            g[t, zz, y, x, :, half] = plus(g[t, zz, y, x, :, half], r2[t, zz])
        for cpy in zcopies(t):
            cpy.start()

    def f4(t):
        for cpy in zcopies(t):
            cpy.wait_recv()
        piece[t] = (
            g[t, z, y, x, :, half].astype(F32) + r3[t, 0].astype(F32) + r3[t, 1].astype(F32) + r3[t, 2].astype(F32)
        ).astype(BF)

    stages = tuple(zip(RS_LAGS, (f1, f2, f3, f4)))
    due = {}
    for n in range(2):
        for number in range(3):
            due.setdefault(FACTOR_TICKS[n][number], []).append(functools.partial(factor_step, n, number + 1))

    state = [0, 0]

    def enter():
        t, now = state[1], state[0]
        core(t).start()
        for lag, f in zip(EARLY_LAGS[t] if t < 3 else RS_LAGS, (f1, f2, f3, f4)):
            due.setdefault(now + lag, []).insert(0, functools.partial(f, t))
        state[1] = t + 1

    def tick():
        for f in due.pop(state[0], []):
            f()
        state[0] += 1

    def wide(b):
        return pl.ds(pl.multiple_of(b * 384, 384), 384)

    def cols(n):
        return pl.ds(pl.multiple_of(n * 256, 256), 256)

    def grad_tile(left, right):
        t = state[1]

        def rows(b, _):
            r = dot_tn(left(wide(b)), right()).astype(BF)
            g[t, pl.ds(2 * b, 2)] = r.reshape(2, 2, 2, R, D)
            return 0

        lax.fori_loop(0, 2, rows, 0)
        enter()
        tick()

    def through(grad, slot, fresh):
        def part(b, _):
            r = dot_nt(grad(), wbuf[slot, cols(b), :])
            if fresh:
                acc[:, cols(b)] = r
            else:
                acc[:, cols(b)] += r
            return 0

        lax.fori_loop(0, 3, part, 0)

    def sums(row, value):
        vecs[row] = jnp.sum(value.astype(F32), axis=0, keepdims=True)

    def fold(v):
        return jnp.sum(v.reshape(8, 8, D), axis=0)

    def norm_back(number, gain, rows_out, place_cls):
        def rows(m, carry):
            rs = pl.ds(pl.multiple_of(m * 64, 64), 64)
            dh = acc[rs, :]
            if place_cls:
                rid = lax.broadcasted_iota(jnp.int32, (64, 1), 0) + m * 64
                for s in range(8):
                    dh = dh + jnp.where(rid == starts[s], dcls_ref[s : s + 1, :], 0.0)
            nv = norm[rs, :]
            e = dh * gain
            dr = fac_ref[rs, number : number + 1] * (
                e - jnp.mean(e, axis=1, keepdims=True) - nv * jnp.mean(e * nv, axis=1, keepdims=True)
            )
            acc[rs, :] = dr
            low = dr.astype(BF)
            dy[rs, :] = low
            a, b, d = carry
            return a + fold(dh * nv), b + fold(dh), d + fold(low.astype(F32))

        zero = jnp.zeros((8, D), F32)
        out = lax.fori_loop(0, 8, rows, (zero, zero, zero))
        for row, v in zip(rows_out, out):
            vecs[row] = jnp.sum(v, axis=0, keepdims=True)

    for i in range(13):
        vecs[12 + i] = vg_ref[i : i + 1, :]
    for i in range(25, 32):
        vecs[i] = jnp.zeros((1, D), F32)

    load_dkv.wait()
    xload(0).wait()
    for part in range(2):
        grad_tile(lambda part_: xbuf[0, :, part_], lambda: dqkv[part])
    xload(4).start()
    for part in range(2):
        wload(part).wait()
        through(lambda: dqkv[part], part, part == 0)
        wload(part + 3).start()
    load_n2.wait()
    norm_back(1, vec_ref[10:11, :], (10, 11, 9), True)
    load_n1.start()
    load_h1.wait()
    for j in range(4):
        xload(1 + 2 * j).wait()
        grad_tile(lambda part_: xbuf[(1 + 2 * j) % 4, :, part_], lambda: dy[...])
        if 5 + 2 * j < 11:
            xload(5 + 2 * j).start()
        wload(2 + 2 * j).wait()
        xload(2 + 2 * j).wait()

        def pre(b, _):
            r = dot_nt(dy[...], wbuf[(2 + 2 * j) % 3, cols(b), :])
            df[:, cols(b)] = (r * xbuf[(2 + 2 * j) % 4, :, cols(b)].astype(F32)).astype(BF)
            return 0

        lax.fori_loop(0, 3, pre, 0)
        if 6 + 2 * j < 11:
            xload(6 + 2 * j).start()
        wload(5 + 2 * j).start()
        grad_tile(lambda part_: h1b[:, part_], lambda: df[...])
        sums(5 + j, df[...])
        wload(3 + 2 * j).wait()
        through(lambda: df[...], (3 + 2 * j) % 3, False)
        if 6 + 2 * j < 14:
            wload(6 + 2 * j).start()
    load_n1.wait()
    norm_back(0, vec_ref[3:4, :], (3, 4, 2), False)
    xload(9).wait()
    grad_tile(lambda part_: xbuf[1, :, part_], lambda: dy[...])
    wload(10).wait()

    def mixed_grad(b, _):
        df[:, cols(b)] = dot_nt(dy[...], wbuf[10 % 3, cols(b), :]).astype(BF)
        return 0

    lax.fori_loop(0, 3, mixed_grad, 0)
    wload(13).start()
    load_qkv.wait()
    left = lax.broadcasted_iota(jnp.int32, (1, 128), 1) < 64
    keep_left = jnp.where(left, 1.0, 0.0).astype(BF)
    keep_right = jnp.where(left, 0.0, 1.0).astype(BF)

    def both(v):
        return jnp.concatenate([v * keep_left, v * keep_right], axis=0)

    entered = state[1]
    base = state[0]

    def pairs(p, _):
        if True:
            side = lax.rem(p, 2)
            lanes = pl.ds(pl.multiple_of(p * 128, 128), 128)
            pltpu.make_async_copy(p_ref.at[p], prob.at[side], psem.at[side]).wait()
            for b in range(4):
                lo, hi = window(b)
                rows = pl.ds(128 * b, 128)
                go = both(df[rows, lanes])
                pr = prob[side, b, :, 0 : hi - lo]
                pf = pr.astype(F32)
                dp = dot_nt(go, qkv[2, lo:hi, lanes])
                ds = (pf * (dp - jnp.sum(pf * dp, axis=1, keepdims=True)) * 0.125).astype(BF)
                dq = dot_nn(ds, qkv[1, lo:hi, lanes])
                dqkv[0, rows, lanes] = jnp.where(left, dq[0:128, :], dq[128:256, :]).astype(BF)
                dkp = dot_tn(ds, both(qkv[0, rows, lanes]))
                dvp = dot_tn(pr, go)
                seen = 0 if b == 0 else min(4, b + 1) * 128
                if seen > lo:
                    dk_acc[lo:seen, :] += dkp[0 : seen - lo, :]
                    dv_acc[lo:seen, :] += dvp[0 : seen - lo, :]
                if hi > seen:
                    dk_acc[seen:hi, :] = dkp[seen - lo :, :]
                    dv_acc[seen:hi, :] = dvp[seen - lo :, :]
            dqkv[1, :, lanes] = dk_acc[...].astype(BF)
            dqkv[2, :, lanes] = dv_acc[...].astype(BF)

            @pl.when(p < 4)
            def _():
                pltpu.make_async_copy(p_ref.at[p + 2], prob.at[side], psem.at[side]).start()

            for lag, f in stages:
                t = base + p - lag
                pl.when(t < entered)(functools.partial(f, t))
        return 0

    lax.fori_loop(0, 6, pairs, 0)
    for i in range(6):
        due.pop(state[0], None)
        state[0] += 1
    xload(10).wait()
    for part in range(3):
        grad_tile(lambda part_: xbuf[2, :, part_], lambda: dqkv[part])
        if part != 1:
            sums(part // 2, dqkv[part])
    def vcopy(d):
        p, dev = peer(d)
        return remote(vecs.at[p], vin.at[d], vs.at[d], vr.at[d], dev)

    def vstart(d, _):
        vcopy(d).start()
        return 0

    lax.fori_loop(1, 32, vstart, 0)
    vin[0] = vecs[me]

    for part in range(3):
        wload(11 + part).wait()
        through(lambda: dqkv[part], (11 + part) % 3, False)
        tick()
    out = pltpu.make_async_copy(acc, dtok_ref, lsem.at[0])
    out.start()

    tick()
    factor_stage(4)

    def lwait(d, _):
        lcopy(d, lax.rem(me + 32 - d, 32)).wait()
        return 0

    lax.fori_loop(1, 32, lwait, 0)

    def product(a, b):
        lv = lefts[:, a].astype(F32).reshape(256, 128).astype(BF)
        rv = every[:, :, :, :, b, :, half].astype(F32).reshape(256, 384).astype(BF)
        return dot_tn(lv, rv).astype(BF)

    for a in range(2):
        r = product(a, 1)
        piece[20 + 2 * a] = r[0:R, :]
        piece[21 + 2 * a] = r[64 : 64 + R, :]
    tick()

    def up_tiles(j, _):
        piece[16 + j] = product(2, 2 + j)[0:R, :]
        return 0

    lax.fori_loop(0, 4, up_tiles, 0)
    tick()
    piece[15] = product(2, 6)[64 : 64 + R, :]
    piece[14] = product(3, 7)[0:R, :]
    piece[24] = product(3, 0)[64 : 64 + R, :]
    while due and max(due) - state[0] >= LATE:
        tick()
    def vwait(d, _):
        vcopy(d).wait()
        return 0

    lax.fori_loop(1, 32, vwait, 0)
    vsum[...] = jnp.sum(vin[...], axis=0)
    vout_ref[me] = vsum[...]

    def wcopy(d, row):
        return remote(vsum, vout_ref.at[row], ws.at[d], wr.at[d], peer(d)[1])

    def wstart(d, _):
        wcopy(d, me).start()
        return 0

    lax.fori_loop(1, 32, wstart, 0)
    while due:
        tick()

    def back(d):
        p = col_peer(c, d)
        return remote(spread.at[pl.ds(4 * p, 4)], own_ref.at[:, c // 2, :, half], xs.at[d - 1], xr.at[d - 1], (z, p))

    own = pltpu.make_async_copy(spread.at[pl.ds(4 * c, 4)], own_ref.at[:, c // 2, :, half], lsem.at[1])
    for d in (1, 2, 3, 4, 5, 6, 7, 0):
        for i in range(4):
            s = 4 * col_peer(c, d) + i
            v = piece[src_ref[s]]
            spread[s] = jnp.where(fill_ref[s] > 0, v, jnp.zeros_like(v))
        if d:
            back(d).start()
        else:
            own.start()

    def wwait(d, _):
        wcopy(d, me).wait_send()
        wcopy(d, lax.rem(me + 32 - d, 32)).wait_recv()
        return 0

    lax.fori_loop(1, 32, wwait, 0)
    for n in range(2):
        for number in range(4):
            for cpy in factor_copies(n, number):
                cpy.wait_send()
    def drain(t, _):
        for cpy in [core(t)] + first(t) + second(t) + zcopies(t):
            cpy.wait_send()
        return 0

    lax.fori_loop(0, T, drain, 0)
    out.wait()
    own.wait()
    for d in range(1, 8):
        back(d).wait()


def backward_fused(lengths, source, filled, fac, dcls, packed, right, vg, vectors, w, a1, tokens, qkv, prob, o, n1, h1, act, slope, n2, dkv):
    T = len(RS_TILES)
    dma = lambda *n: pltpu.SemaphoreType.DMA(n)
    V = pl.BlockSpec(memory_space=pltpu.VMEM)
    S = pl.BlockSpec(memory_space=pltpu.SMEM)
    ANY = pl.BlockSpec(memory_space=pl.ANY)
    vm = pltpu.VMEM
    scratch = [
        vm((T, 4, 2, 2, R, D), BF), vm((T, 4, 2, 2, R, H), BF), vm((T, 4, 2, R, H), BF), vm((T, 4, R, H), BF), vm((T, 3, R, H), BF),
        vm((4, 2, 2, 2, 8, 8, D), BF), vm((32, 4, 8, 128), BF), vm((25, R, H), BF), vm((32, R, H), BF),
        vm((32, 1, D), F32), vm((32, 1, D), F32), vm((1, D), F32),
        vm((3, D, D), BF), vm((4, 512, D), BF), vm((512, D), BF), vm((3, 512, D), BF), vm((2, 4, 256, 384), BF), vm((3, 512, D), BF),
        vm((512, D), F32), vm((512, D), F32), vm((512, D), BF), vm((512, D), BF), vm((512, 128), F32), vm((512, 128), F32),
    ]
    scratch += [dma(T), dma(T), dma(T, 2), dma(T, 2), dma(T, 2), dma(T, 2), dma(T, 3), dma(T, 3), dma(7), dma(7)] + [dma(32) for _ in range(4)]
    scratch += [dma(2, 4), dma(2, 4), dma(2, 3), dma(2, 3), dma(32), dma(32), dma(3), dma(4), dma(2), dma(4)]
    return pl.pallas_call(
        functools.partial(backward_kernel),
        out_shape=(jax.ShapeDtypeStruct((4, 4, R, D), BF), jax.ShapeDtypeStruct((32, 1, D), F32), jax.ShapeDtypeStruct((512, D), F32)),
        in_specs=[S, S, S] + [V] * 6 + [ANY] * 12,
        out_specs=(V, V, ANY),
        scratch_shapes=scratch,
        compiler_params=pltpu.CompilerParams(collective_id=1, has_side_effects=True, vmem_limit_bytes=BIG),
    )(lengths.reshape(-1), source, filled, fac, dcls, packed, right, vg, vectors, w.reshape(-1, D, D), a1, tokens, qkv, prob, o, n1, h1, act, slope, n2, dkv)

def adam_fast(weights, first_moment, second_moment, grad_values, step_rate):
    first_new = first_decay * first_moment + (1.0 - first_decay) * grad_values
    second_new = second_decay * second_moment + (1.0 - second_decay) * grad_values * grad_values
    root = jnp.sqrt(second_new * (1.0 / (1.0 - second_decay**STEP))) + adam_eps
    step = (first_new * (1.0 / (1.0 - first_decay**STEP))) / root + weight_decay * weights
    return (weights - step_rate * step, first_new, second_new)


def adam_kernel(
    rate, own_ref, w_ref, m_ref, v_ref, sums_ref, vec_ref, vm_ref, vv_ref,
    g_out, w_out, m_out, v_out, vg_out, vec_out, vm_out, vv_out, bias_out,
):
    grad = own_ref[...].astype(F32)
    g_out[...] = grad
    w_out[...], m_out[...], v_out[...] = adam_fast(w_ref[...], m_ref[...], v_ref[...], grad, rate)

    @pl.when(pl.program_id(0) == 0)
    def _():
        count = vec_ref.shape[0]

        def row(r, _):
            vg_out[pl.ds(r, 1), :] = sums_ref[r]
            return 0

        lax.fori_loop(0, count, row, 0)
        bias_out[...] = sums_ref[12 * (LAYERS - 1) + 2, 0]
        vec_out[...], vm_out[...], vv_out[...] = adam_fast(vec_ref[...], vm_ref[...], vv_ref[...], vg_out[...], vector_rate)


def adam_all(own, store, first, second, sums, vectors, vector_first, vector_second, steps=2):
    rows = D // steps
    rate = store_rate_factor / math.sqrt(vectors.shape[1])
    flat = lambda v: v.reshape(D, D)
    tall = pl.BlockSpec((rows, D), lambda i: (i, 0))
    count = vectors.shape[0]
    whole = pl.BlockSpec((count, D), lambda i: (0, 0))
    f = lambda *s: jax.ShapeDtypeStruct(s, F32)
    out = pl.pallas_call(
        functools.partial(adam_kernel, rate),
        grid=(steps,),
        out_shape=(f(D, D),) * 4 + (f(count, D),) * 4 + (f(D),),
        in_specs=[tall] * 4 + [pl.BlockSpec(sums.shape, lambda i: (0, 0, 0))] + [whole] * 3,
        out_specs=(tall,) * 4 + (whole,) * 4 + (pl.BlockSpec((D,), lambda i: (0,)),),
    )(flat(own), flat(store), flat(first), flat(second), sums, vectors, vector_first, vector_second)
    return tuple(v.reshape(store.shape) for v in out[:4]) + out[4:8] + (out[8],)


def linear_map_apply(left_side, right_side):
    return jnp.dot(left_side, right_side, preferred_element_type=jnp.float32)


def layer_norm(values, gain_values, shift_values):
    center = values - jnp.mean(values, axis=-1, keepdims=True)
    spread = jnp.mean(center * center, axis=-1, keepdims=True)
    factor = lax.rsqrt(spread + norm_eps)
    normed = center * factor
    return (normed * gain_values + shift_values, normed, factor)


def norm_back(grad_in, normed, factor, gain_values):
    scaled = grad_in * gain_values
    input_grad = factor * (
        scaled
        - jnp.mean(scaled, axis=-1, keepdims=True)
        - normed * jnp.mean(scaled * normed, axis=-1, keepdims=True)
    )
    return (input_grad, jnp.sum(grad_in * normed, axis=0), jnp.sum(grad_in, axis=0))


def gelu_exact(values):
    return 0.5 * values * (1.0 + lax.erf(values * root_half))


def gelu_slope(values):
    return (
        0.5 * (1.0 + lax.erf(values * root_half))
        + values * jnp.exp(-0.5 * values * values) * slope_norm
    )


def layer_weights(weight_tiles, base):
    joint_weight = jnp.concatenate(
        [weight_tiles[base], weight_tiles[base + 1], weight_tiles[base + 2]], axis=1
    )
    up_weight = jnp.concatenate([weight_tiles[base + 4 + number] for number in range(4)], axis=1)
    down_weight = jnp.concatenate([weight_tiles[base + 8 + number] for number in range(4)], axis=0)
    return (joint_weight, weight_tiles[base + 3], up_weight, down_weight)


def split_heads(joint_row, head_count):
    seq_len = joint_row.shape[0]
    model_width = joint_row.shape[1] // 3
    shaped = joint_row.reshape(seq_len, 3, head_count, model_width // head_count)
    return (shaped[:, 0], shaped[:, 1], shaped[:, 2])


def masked_scores(queries, keys_here, seg_row):
    score_scale = 1.0 / math.sqrt(queries.shape[-1])
    raw_scores = jnp.einsum("qhd,khd->hqk", queries, keys_here, preferred_element_type=jnp.float32)
    same_segment = seg_row[:, None] == seg_row[None, :]
    return (jnp.where(same_segment[None], raw_scores * score_scale, -1e30), score_scale)


def attend_forward(joint_row, seg_row, head_count):
    queries, keys_here, values_here = split_heads(joint_row, head_count)
    scores, score_scale = masked_scores(queries, keys_here, seg_row)
    row_peak = jnp.max(scores, axis=-1, keepdims=True)
    weights = jnp.exp(scores - row_peak)
    exp_total = jnp.sum(weights, axis=-1, keepdims=True)
    row_probabilities = (weights / exp_total).astype(jnp.bfloat16)
    mixed_heads = jnp.einsum(
        "hqk,khd->qhd", row_probabilities, values_here, preferred_element_type=jnp.float32
    )
    return (
        mixed_heads.reshape(mixed_heads.shape[0], -1),
        row_peak[..., 0] + jnp.log(exp_total[..., 0]),
    )


def attend_backward(joint_row, seg_row, lse_row, grad_row, head_count):
    queries, keys_here, values_here = split_heads(joint_row, head_count)
    seq_len = joint_row.shape[0]
    grad_heads = grad_row.reshape(seq_len, head_count, -1)
    scores, score_scale = masked_scores(queries, keys_here, seg_row)
    row_probabilities = jnp.exp(scores - lse_row[..., None])
    prob_grads = jnp.einsum(
        "qhd,khd->hqk", grad_heads, values_here, preferred_element_type=jnp.float32
    )
    inner_sum = jnp.sum(row_probabilities * prob_grads, axis=-1, keepdims=True)
    score_grads = (row_probabilities * (prob_grads - inner_sum) * score_scale).astype(jnp.bfloat16)
    query_grad = jnp.einsum(
        "hqk,khd->qhd", score_grads, keys_here, preferred_element_type=jnp.float32
    )
    key_grad = jnp.einsum("hqk,qhd->khd", score_grads, queries, preferred_element_type=jnp.float32)
    value_grad = jnp.einsum(
        "hqk,qhd->khd",
        row_probabilities.astype(jnp.bfloat16),
        grad_heads,
        preferred_element_type=jnp.float32,
    )
    return jnp.concatenate(
        [
            query_grad.reshape(seq_len, -1),
            key_grad.reshape(seq_len, -1),
            value_grad.reshape(seq_len, -1),
        ],
        axis=1,
    )


def layer_forward(inputs, segment, weight_tiles, vectors, base, head_count):
    joint_weight, out_weight, up_weight, down_weight = layer_weights(weight_tiles, base)
    model_width = inputs.shape[1]
    rows_here = segment.shape[0]
    inputs_low = inputs.astype(jnp.bfloat16)
    joint_bias = jnp.concatenate(
        [vectors[base], jnp.zeros((model_width,), jnp.float32), vectors[base + 1]]
    )
    joint_out = (linear_map_apply(inputs_low, joint_weight) + joint_bias).astype(jnp.bfloat16)
    joint_rows = joint_out.reshape(rows_here, -1, 3 * model_width)

    def forward_row(row_items):
        return attend_forward(row_items[0], row_items[1], head_count)

    mixed, log_total = lax.map(forward_row, (joint_rows, segment))
    mixed_low = mixed.reshape(-1, model_width).astype(jnp.bfloat16)
    branch = linear_map_apply(mixed_low, out_weight) + vectors[base + 2]
    hidden, normed_one, factor_one = layer_norm(
        inputs + branch, vectors[base + 3], vectors[base + 4]
    )
    hidden_low = hidden.astype(jnp.bfloat16)
    pre_gelu = linear_map_apply(hidden_low, up_weight) + vectors[base + 5 : base + 9].reshape(-1)
    active = gelu_exact(pre_gelu).astype(jnp.bfloat16)
    output = linear_map_apply(active, down_weight) + vectors[base + 9]
    result, normed_two, factor_two = layer_norm(
        hidden + output, vectors[base + 10], vectors[base + 11]
    )
    kept_values = (
        inputs_low,
        joint_rows,
        log_total,
        mixed_low,
        normed_one,
        factor_one,
        hidden_low,
        pre_gelu,
        active,
        normed_two,
        factor_two,
    )
    return (result, kept_values)


def layer_backward(grad_out, kept_values, segment, weight_tiles, vectors, base, head_count):
    joint_weight, out_weight, up_weight, down_weight = layer_weights(weight_tiles, base)
    (
        inputs_low,
        joint_rows,
        log_total,
        mixed_low,
        normed_one,
        factor_one,
        hidden_low,
        pre_gelu,
        active,
        normed_two,
        factor_two,
    ) = kept_values
    model_width = inputs_low.shape[1]
    grad_res2, gain_two, shift_two = norm_back(grad_out, normed_two, factor_two, vectors[base + 10])
    grad_output = grad_res2.astype(jnp.bfloat16)
    down_grad = jnp.einsum("tf,td->fd", active, grad_output, preferred_element_type=jnp.float32)
    down_bias = jnp.sum(grad_output.astype(jnp.float32), axis=0)
    grad_active = jnp.einsum(
        "td,fd->tf", grad_output, down_weight, preferred_element_type=jnp.float32
    )
    grad_pre = (grad_active * gelu_slope(pre_gelu)).astype(jnp.bfloat16)
    up_grad = jnp.einsum("td,tf->df", hidden_low, grad_pre, preferred_element_type=jnp.float32)
    up_bias = jnp.sum(grad_pre.astype(jnp.float32), axis=0)
    grad_hidden = (
        jnp.einsum("tf,df->td", grad_pre, up_weight, preferred_element_type=jnp.float32) + grad_res2
    )
    grad_res1, gain_one, shift_one = norm_back(
        grad_hidden, normed_one, factor_one, vectors[base + 3]
    )
    grad_branch = grad_res1.astype(jnp.bfloat16)
    out_grad = jnp.einsum("tc,td->cd", mixed_low, grad_branch, preferred_element_type=jnp.float32)
    out_bias = jnp.sum(grad_branch.astype(jnp.float32), axis=0)
    grad_mixed = jnp.einsum(
        "td,cd->tc", grad_branch, out_weight, preferred_element_type=jnp.float32
    ).astype(jnp.bfloat16)

    def backward_row(row_items):
        return attend_backward(row_items[0], row_items[1], row_items[2], row_items[3], head_count)

    grad_joint = lax.map(
        backward_row,
        (joint_rows, segment, log_total, grad_mixed.reshape(joint_rows.shape[0], -1, model_width)),
    )
    grad_joint = grad_joint.reshape(-1, 3 * model_width).astype(jnp.bfloat16)
    joint_grad = jnp.einsum("tc,te->ce", inputs_low, grad_joint, preferred_element_type=jnp.float32)
    joint_sums = jnp.sum(grad_joint.astype(jnp.float32), axis=0)
    grad_inputs = (
        jnp.einsum("te,ce->tc", grad_joint, joint_weight, preferred_element_type=jnp.float32)
        + grad_res1
    )
    tile_list = [
        joint_grad[:, :model_width],
        joint_grad[:, model_width : 2 * model_width],
        joint_grad[:, 2 * model_width :],
        out_grad,
    ]
    tile_list = tile_list + [
        up_grad[:, number * model_width : (number + 1) * model_width] for number in range(4)
    ]
    tile_list = tile_list + [
        down_grad[number * model_width : (number + 1) * model_width] for number in range(4)
    ]
    vector_list = [
        joint_sums[:model_width],
        joint_sums[2 * model_width :],
        out_bias,
        gain_one,
        shift_one,
    ]
    vector_list = vector_list + [
        up_bias[number * model_width : (number + 1) * model_width] for number in range(4)
    ]
    vector_list = vector_list + [down_bias, gain_two, shift_two]
    return (grad_inputs, tile_list, vector_list)


def adam_step(weights, first_moment, second_moment, grad_values, step_rate):
    first_new = first_decay * first_moment + (1.0 - first_decay) * grad_values
    second_new = second_decay * second_moment + (1.0 - second_decay) * grad_values * grad_values
    first_hat = first_new / (1.0 - first_decay**STEP)
    second_hat = second_new / (1.0 - second_decay**STEP)
    new_weights = weights - step_rate * (
        first_hat / (jnp.sqrt(second_hat) + adam_eps) + weight_decay * weights
    )
    return (new_weights, first_new, second_new)


def pick_rows(row_values, row_starts):
    return row_values[row_starts]


def local_any(
    tokens,
    lengths,
    pair_index,
    tile_slot,
    master_store,
    first_moment_store,
    second_moment_store,
    vectors,
    vector_first,
    vector_second,
):
    model_width = tokens.shape[1]
    rows_here = lengths.shape[0]
    sent_count = lengths.shape[1]
    seq_len = tokens.shape[0] // rows_here
    head_count = HEADS
    tile_count = tile_slot.shape[0]
    row_count = lax.axis_size("row")
    col_count = lax.axis_size("col")
    slot_count = master_store.shape[0] * col_count
    gathered_rows = lax.all_gather(master_store.astype(jnp.bfloat16), "row", axis=1, tiled=True)
    gathered = lax.all_gather(gathered_rows, "col", axis=0, tiled=True)
    weight_tiles = jnp.take(gathered, tile_slot, axis=0)
    starts = jnp.cumsum(lengths, axis=1) - lengths
    places = jnp.arange(seq_len, dtype=jnp.int32)
    segment = jnp.sum((places[None, :, None] >= starts[:, None, :]).astype(jnp.int32), axis=2) - 1
    hidden_state = tokens.astype(jnp.float32)
    kept_layers = []
    for layer_number in range(LAYERS):
        hidden_state, kept_values = layer_forward(
            hidden_state, segment, weight_tiles, vectors, 12 * layer_number, head_count
        )
        kept_layers.append(kept_values)
    encoded = hidden_state.reshape(rows_here, seq_len, model_width)
    cls_rows = jax.vmap(pick_rows)(encoded, starts).reshape(-1, model_width)
    cls_low = cls_rows.astype(jnp.bfloat16)
    pool_weight = weight_tiles[tile_count - 1]
    pooled = jnp.tanh(linear_map_apply(cls_low, pool_weight) + vectors[tile_count - 1])
    inverse = lax.rsqrt(jnp.sum(pooled * pooled, axis=1, keepdims=True) + unit_eps)
    unit_low = (pooled * inverse).astype(jnp.bfloat16)
    row_emb = lax.all_gather(unit_low, "col", axis=0, tiled=True)
    col_emb = lax.all_gather(unit_low, "row", axis=0, tiled=True)
    sent_dev = unit_low.shape[0]
    row_pos = lax.axis_index("row")
    col_pos = lax.axis_index("col")
    row_indices = row_pos * (col_count * sent_dev) + jnp.arange(
        col_count * sent_dev, dtype=jnp.int32
    )
    column_indices = (
        (jnp.arange(row_count, dtype=jnp.int32)[:, None] * col_count + col_pos) * sent_dev
        + jnp.arange(sent_dev, dtype=jnp.int32)[None, :]
    ).reshape(-1)
    plain_closeness = jnp.einsum("rd,cd->rc", row_emb, col_emb, preferred_element_type=jnp.float32)
    angular_closeness = jnp.where(
        row_indices[:, None] == column_indices[None, :],
        -1e30,
        plain_closeness / logit_sharpness_divisor,
    )
    target = jnp.take(pair_index, row_indices)
    positive_pair_matches = column_indices[None, :] == target[:, None]
    positive_local = jnp.sum(jnp.where(positive_pair_matches, angular_closeness, 0.0), axis=1)
    peak_local = jnp.max(angular_closeness, axis=1)
    row_peak = lax.pmax(peak_local, "col")
    mass_total, positive = lax.psum(
        (jnp.sum(jnp.exp(angular_closeness - row_peak[:, None]), axis=1), positive_local), "col"
    )
    log_mass = row_peak + jnp.log(mass_total)
    sentence_total = row_count * col_count * sent_dev
    row_probabilities = jnp.exp(angular_closeness - log_mass[:, None])
    similarity_gradient = (
        (row_probabilities - positive_pair_matches.astype(jnp.float32))
        / sentence_total
        / logit_sharpness_divisor
    ).astype(jnp.bfloat16)
    rows_part = jnp.einsum(
        "rc,cd->rd", similarity_gradient, col_emb, preferred_element_type=jnp.float32
    )
    cols_part = jnp.einsum(
        "rc,rd->cd", similarity_gradient, row_emb, preferred_element_type=jnp.float32
    )
    unit_sensitivity = lax.psum_scatter(
        rows_part.astype(jnp.bfloat16), "col", scatter_dimension=0, tiled=True
    ).astype(jnp.float32) + lax.psum_scatter(
        cols_part.astype(jnp.bfloat16), "row", scatter_dimension=0, tiled=True
    ).astype(
        jnp.float32
    )
    own_loss = jnp.sum(lax.dynamic_slice_in_dim(log_mass - positive, col_pos * sent_dev, sent_dev))
    dot_unit = jnp.sum(pooled * unit_sensitivity, axis=1, keepdims=True)
    grad_pooled = inverse * unit_sensitivity - pooled * inverse * inverse * inverse * dot_unit
    grad_pre = (grad_pooled * (1.0 - pooled * pooled)).astype(jnp.bfloat16)
    pool_grad = jnp.einsum("sd,se->de", cls_low, grad_pre, preferred_element_type=jnp.float32)
    pool_bias = jnp.sum(grad_pre.astype(jnp.float32), axis=0)
    grad_cls = jnp.einsum("se,de->sd", grad_pre, pool_weight, preferred_element_type=jnp.float32)
    one_hot = (places[None, None, :] == starts[:, :, None]).astype(jnp.float32)
    grad_state = jnp.einsum(
        "pek,pex->pkx",
        one_hot,
        grad_cls.reshape(rows_here, sent_count, model_width),
        precision=lax.Precision.HIGHEST,
    ).reshape(-1, model_width)
    tile_grads = []
    vector_grads = []
    for layer_number in reversed(range(LAYERS)):
        grad_state, tile_list, vector_list = layer_backward(
            grad_state,
            kept_layers[layer_number],
            segment,
            weight_tiles,
            vectors,
            12 * layer_number,
            head_count,
        )
        tile_grads = tile_list + tile_grads
        vector_grads = vector_list + vector_grads
    grad_stack = jnp.stack(tile_grads + [pool_grad])
    vector_stack = jnp.stack(vector_grads + [pool_bias])
    slot_indices = jnp.arange(slot_count, dtype=jnp.int32)
    matches = tile_slot[None, :] == slot_indices[:, None]
    filled = jnp.any(matches, axis=1)
    source_tile = jnp.sum(
        jnp.where(matches, jnp.arange(tile_count, dtype=jnp.int32)[None, :], 0), axis=1
    )
    whole_slots = lax.psum_scatter(
        jnp.where(filled[:, None, None], jnp.take(grad_stack, source_tile, axis=0), 0.0).astype(
            jnp.bfloat16
        ),
        "col",
        scatter_dimension=0,
        tiled=True,
    )
    owned_grad = lax.psum_scatter(whole_slots, "row", scatter_dimension=1, tiled=True).astype(
        jnp.float32
    )
    vector_total, loss_total = lax.psum((vector_stack, own_loss), ("row", "col"))
    mean_loss = loss_total / sentence_total
    new_store, new_store_first, new_store_second = adam_step(
        master_store,
        first_moment_store,
        second_moment_store,
        owned_grad,
        store_rate_factor / math.sqrt(model_width),
    )
    new_vectors, new_vector_first, new_vector_second = adam_step(
        vectors, vector_first, vector_second, vector_total, vector_rate
    )
    out_bias_grad = vector_total[12 * (LAYERS - 1) + 2]
    return (
        grad_state,
        mean_loss,
        owned_grad,
        new_store,
        new_store_first,
        new_store_second,
        vector_total,
        new_vectors,
        new_vector_first,
        new_vector_second,
        out_bias_grad,
    )


def local_here(
    tokens,
    lengths,
    pair_index,
    tile_slot,
    master_store,
    first_moment_store,
    second_moment_store,
    vectors,
    vector_first,
    vector_second,
):
    (
        weights, joint, prob, mixed, normed_one, hidden_low, active, slope, normed_two, factors, state_low,
        source_tile, filled, keys_grad, cls_grad, packed_left, row_right, head_vectors, loss,
    ) = forward_fused(tile_slot, master_store, tokens, lengths, vectors, pair_index)
    owned_low, vector_sums, grad_state = backward_fused(
        lengths, source_tile, filled, factors, cls_grad, packed_left, row_right, head_vectors, vectors, weights, state_low, tokens,
        joint, prob, mixed, normed_one, hidden_low, active, slope, normed_two, keys_grad,
    )
    (
        owned_grad, new_store, new_store_first, new_store_second,
        vector_total, new_vectors, new_vector_first, new_vector_second, out_bias_grad,
    ) = adam_all(
        owned_low, master_store, first_moment_store, second_moment_store, vector_sums, vectors, vector_first, vector_second
    )
    return (
        grad_state,
        loss[0, 0],
        owned_grad,
        new_store,
        new_store_first,
        new_store_second,
        vector_total,
        new_vectors,
        new_vector_first,
        new_vector_second,
        out_bias_grad,
    )


def solution(mesh):
    placed = (
        P(("row", "col"), None),
        P(("row", "col"), None),
        P(),
        P(),
        P("col", "row", None),
        P("col", "row", None),
        P("col", "row", None),
        P(),
        P(),
        P(),
    )
    fits = (mesh.shape["row"], mesh.shape["col"]) == (4, 8)
    return jax.shard_map(
        local_here if fits else local_any,
        mesh=mesh,
        in_specs=placed,
        out_specs=(
            P(("row", "col"), None),
            P(),
            P("col", "row", None),
            P("col", "row", None),
            P("col", "row", None),
            P("col", "row", None),
            P(),
            P(),
            P(),
            P(),
            P(),
        ),
        check_vma=False,
    )
```
